32 devices in a mesh: grp: 2 (over y), dec: 4 (over z), stg: 2 (over x), tp: 2 (over core).
Axes of the slice: x: 2, y: 2, z: 4, core: 2. Of those that a mesh axis runs over, the one named last changes fastest.
Arguments:
- hidden_x: bfloat16 [3072, 7168], P(('grp', 'dec'), ('stg', 'tp')), parts along dimension 0, may hold values from -8 to 8
- proj_weight: bfloat16 [7168, 2112], P(('stg', 'tp'), 'dec'), may hold values from -0.0625 to 0.0625
- q_gain: float32 [1536], replicated, may hold values from 0.25 to 1.75
- kv_gain: float32 [512], replicated, may hold values from 0.25 to 1.75
- old_cache: bfloat16 [256, 32, 576], P(('grp', 'dec')), parts along dimension 0, may hold values from -6 to 6
- page_plan: int32 [96, 2], P(('grp', 'dec')), parts along dimension 0, may hold values from 0 to 31, as said below
- block_table: int32 [8, 4, 8], P(('grp', 'dec')), parts along dimension 0, may hold values from 0 to 31, as said below
- split_lens: int32 [8, 4], P('grp', 'dec'), parts along dimension 0, may hold values from 2 to 256, as said below
- dec_query: bfloat16 [8, 128, 576], P('grp', ('stg', 'tp')), parts along dimension 0, may hold values from -66 to 66
- new_key: bfloat16 [8, 576], P('grp'), parts along dimension 0, may hold values from -12 to 12
Outputs:
- q_latent: bfloat16 [3072, 1536], P(('grp', 'dec'), ('stg', 'tp')), parts along dimension 0
- attn_latent: bfloat16 [8, 128, 512], P('grp', ('stg', 'tp')), parts along dimension 0
The draws below stay inside these ranges and needn't reach their ends.
There are 2 independent parts, one for each index of `grp`. The reference program is written for one: setup_inputs(seed, part) draws one part's arguments, and reference() takes and returns one part's arrays. A program takes and returns all parts, laid end to end along the dimension named above; an argument that names none is the same for every part. Nothing has to cross between parts.
Inputs may be any that keep to these rules, and one draw needn't show every extreme that they name: `page_plan`: column 0 is the owner of prefill page g, column 1 its slot among the owner's 32; no two pages share owner and slot; in each aligned block of 12 rows (one index of dec) no owner appears more than 3 times and some owner exactly 3 times; no page goes to a slot block_table[o, r, 0]. `block_table`: for each owner the 4 x 8 entries are its 32 slots, each once. `split_lens`: each request has exactly 256 tokens on at least one owner.
All inputs are finite; a program needn't handle non-finite values.
Results may differ from the reference program's by a relative error of at most 0.0054.
Values may be sent and summed in bfloat16 or wider, within the bound.
A program may use at most 64 MiB of HBM per device.

```python
import jax
import jax.numpy as jnp
from jax import lax

D = 7168
QL = 1536
KVL = 512
ROPE = 64
H = 128
PAGE = 32
REQS = 4
PPR = 8
KVW = 576
PROJ = 2112
TOKENS = 1536
PPS = 12
NPG = 48
CAPP = 3
GROUPS = 4
SLOTS = 32
N_DEC = 4


def plan_tables(key):
    shuffle = jax.random.permutation(jax.random.fold_in(key, 11), N_DEC)

    def block_owners(source):
        shuffled = jax.random.permutation(jax.random.fold_in(jax.random.fold_in(key, 12), source), PPS)
        return shuffle[(source * GROUPS + shuffled // CAPP) % N_DEC]
    owners = jax.vmap(block_owners)(jnp.arange(N_DEC, dtype=jnp.int32)).reshape(NPG)
    onehot = (owners[:, None] == jnp.arange(N_DEC, dtype=jnp.int32)[None, :]).astype(jnp.int32)
    before = jnp.cumsum(onehot, axis=0) - onehot
    arrival = jnp.sum(before * onehot, axis=1)

    def owner_slots(owner):
        return jax.random.permutation(jax.random.fold_in(jax.random.fold_in(key, 13), owner), SLOTS)
    slot_orders = jax.vmap(owner_slots)(jnp.arange(N_DEC, dtype=jnp.int32))
    plan_slots = slot_orders[owners, REQS + arrival]
    page_table = jnp.stack([owners, plan_slots], axis=1).astype(jnp.int32)
    slot_table = jnp.transpose(slot_orders.reshape(N_DEC, PPR, REQS), (0, 2, 1)).astype(jnp.int32)
    longest = PPR * PAGE
    spread = longest - 1
    draw_first = jax.random.randint(jax.random.fold_in(key, 14), (REQS, N_DEC), 0, spread)
    draw_second = jax.random.randint(jax.random.fold_in(key, 15), (REQS, N_DEC), 0, spread)
    length_table = longest - draw_first * draw_second // spread
    longest_owner = jax.random.randint(jax.random.fold_in(key, 16), (REQS,), 0, N_DEC)
    length_table = jnp.where(jnp.arange(N_DEC, dtype=jnp.int32)[None, :] == longest_owner[:, None], longest, length_table)
    return (page_table, slot_table, length_table.astype(jnp.int32))


def draw_page_plan(key, part):
    return plan_tables(key)[0]


def draw_block_table(key, part):
    return plan_tables(key)[1]


def draw_split_lens(key, part):
    return plan_tables(key)[2]


def draw_old_cache(key, part):
    extent = (N_DEC * SLOTS, PAGE, KVW)
    values_out = jnp.clip(jax.random.normal(jax.random.fold_in(key, 21), extent, jnp.float32), -6.0, 6.0)
    return values_out.astype(jnp.bfloat16)


def draw_dec_query(key, part):
    extent = (REQS, H, KVW)
    values_out = jnp.clip(1.5 * jax.random.normal(jax.random.fold_in(key, 31), extent, jnp.float32), -9.0, 9.0)
    return values_out.astype(jnp.bfloat16)


def draw_hidden_x(key, part):
    extent = (TOKENS, D)
    baseline = jnp.clip(jax.random.normal(jax.random.fold_in(key, 41), extent, jnp.float32), -4.0, 4.0)
    row_scale = jnp.exp(jax.random.uniform(jax.random.fold_in(key, 42), (TOKENS,), jnp.float32, -0.69, 0.69))
    return (baseline * row_scale[:, None]).astype(jnp.bfloat16)


def steps_of(stream_key, shape, shards, low, largest):
    level, own = 1.0, jax.random.fold_in(stream_key, 6)
    for dim, shards_of in shards:
        steps = jnp.exp(jax.random.uniform(jax.random.fold_in(own, dim), (shards_of,), jnp.float32, low / len(shards), largest / len(shards)))
        level = level * jnp.repeat(steps, shape[dim] // shards_of).reshape([-1 if axis == dim else 1 for axis in range(len(shape))])
    return level


def gaussian(key, dims, scale, most, shards=(), kind=jnp.bfloat16):
    array = jax.random.normal(key, dims, jnp.float32) * scale
    if len(shards) > 0:
        array = steps_of(key, dims, shards, -0.22, 0.18) * array
    return jnp.clip(array, min=-most, max=most).astype(kind)


def setup_inputs(seed: int = 0, part: int = 0) -> dict:
    arg_keys = jax.random.split(jax.random.key(seed), 11)
    own_keys = jax.random.split(jax.random.fold_in(arg_keys[10], part), 11)
    hidden_x = draw_hidden_x(jax.random.fold_in(jax.random.fold_in(arg_keys[10], part), 71), part)
    proj_weight = gaussian(arg_keys[1], (D, PROJ), D ** -0.5, 0.0625, ((0, 4), (1, 4)))
    q_gain = jnp.clip(1.0 + 0.15 * jax.random.normal(arg_keys[2], (QL,), jnp.float32), 0.25, 1.75)
    kv_gain = jnp.clip(1.0 + 0.15 * jax.random.normal(arg_keys[3], (KVL,), jnp.float32), 0.25, 1.75)
    old_cache = draw_old_cache(jax.random.fold_in(jax.random.fold_in(arg_keys[10], part), 71), part)
    page_plan = draw_page_plan(jax.random.fold_in(jax.random.fold_in(arg_keys[10], part), 71), part)
    block_table = draw_block_table(jax.random.fold_in(jax.random.fold_in(arg_keys[10], part), 71), part)
    split_lens = draw_split_lens(jax.random.fold_in(jax.random.fold_in(arg_keys[10], part), 71), part)
    dec_query = draw_dec_query(jax.random.fold_in(jax.random.fold_in(arg_keys[10], part), 71), part)
    new_key = gaussian(own_keys[9], (REQS, KVW), 2.0, 12.0)
    return {"hidden_x": hidden_x, "proj_weight": proj_weight, "q_gain": q_gain, "kv_gain": kv_gain, "old_cache": old_cache, "page_plan": page_plan, "block_table": block_table, "split_lens": split_lens, "dec_query": dec_query, "new_key": new_key}


softmax_scale = 192.0 ** (-0.5)
norm_eps = 1e-06

def rope_rotate(matrix, col_start, positions):
    col_count = matrix.shape[1]
    columns = col_start + jnp.arange(col_count, dtype=jnp.int32)
    is_rope = columns >= KVL
    pair_index = jnp.maximum(columns - KVL, 0) // 2
    frequency = jnp.power(jnp.float32(10000.0), -(2 * pair_index).astype(jnp.float32) / ROPE)
    angles = positions[:, None] * frequency[None, :]
    cosine = jnp.where(is_rope[None, :], jnp.cos(angles), 1.0)
    sine_part = jnp.where(is_rope[None, :], jnp.sin(angles), 0.0)
    paired = matrix.reshape(matrix.shape[0], col_count // 2, 2)
    partner = jnp.stack([-paired[:, :, 1], paired[:, :, 0]], axis=2).reshape(matrix.shape)
    return matrix * cosine + partner * sine_part

def kv_finish(matrix, col_start, latent_sq, kv_gain, positions):
    col_count = matrix.shape[1]
    columns = col_start + jnp.arange(col_count, dtype=jnp.int32)
    gain_full = jnp.concatenate([kv_gain, jnp.ones((ROPE,), jnp.float32)])
    gain_cols = lax.dynamic_slice_in_dim(gain_full, col_start, col_count)
    inverse = lax.rsqrt(latent_sq / KVL + norm_eps)
    row_scale = jnp.where(columns[None, :] < KVL, inverse[:, None] * gain_cols[None, :], 1.0)
    return rope_rotate(matrix * row_scale, col_start, positions).astype(jnp.bfloat16)

def reference(hidden_x, proj_weight, q_gain, kv_gain, old_cache, page_plan, block_table, split_lens, dec_query, new_key):
    projected = jnp.dot(hidden_x, proj_weight, preferred_element_type=jnp.float32)
    query_part = projected[:, :QL]
    query_sq = lax.optimization_barrier(jnp.sum(query_part * query_part, axis=1))
    q_latent = (query_part * lax.rsqrt(query_sq / QL + norm_eps)[:, None] * q_gain[None, :]).astype(jnp.bfloat16)
    kv_part = projected[:, QL:]
    latent_sq = lax.optimization_barrier(jnp.sum(kv_part[:, :KVL] * kv_part[:, :KVL], axis=1))
    positions = jnp.arange(TOKENS, dtype=jnp.int32).astype(jnp.float32)
    new_rows = kv_finish(kv_part, 0, latent_sq, kv_gain, positions)
    new_pages = new_rows.reshape(NPG, PAGE, KVW)
    targets = page_plan[:, 0] * SLOTS + page_plan[:, 1]
    cache = old_cache.at[targets].set(new_pages)
    query = dec_query.astype(jnp.float32)

    def owner_partial(owner):
        slot_rows = block_table[owner]
        key_rows = cache[owner * SLOTS + slot_rows].reshape(REQS, PPR * PAGE, KVW).astype(jnp.float32)
        scores = jnp.einsum('rhc,rlc->rhl', query, key_rows) * softmax_scale
        live_mask = jnp.arange(PPR * PAGE, dtype=jnp.int32)[None, :] < split_lens[:, owner][:, None]
        scores = jnp.where(live_mask[:, None, :], scores, -1e+30)
        row_peak = lax.optimization_barrier(jnp.max(scores, axis=2))
        weights = jnp.where(live_mask[:, None, :], jnp.exp(scores - row_peak[:, :, None]), 0.0)
        row_total = lax.optimization_barrier(jnp.sum(weights, axis=2))
        rounded = lax.optimization_barrier(weights.astype(jnp.bfloat16)).astype(jnp.float32)
        partial_out = jnp.einsum('rhl,rlc->rhc', rounded, key_rows[:, :, :KVL])
        return (row_peak, row_total, partial_out)
    peaks, totals, partials = lax.map(owner_partial, jnp.arange(N_DEC, dtype=jnp.int32))
    self_score = jnp.einsum('rhc,rc->rh', query, new_key.astype(jnp.float32)) * softmax_scale
    overall = jnp.maximum(lax.optimization_barrier(jnp.max(peaks, axis=0)), self_score)
    factor = jnp.exp(peaks - overall[None])
    self_weight = jnp.exp(self_score - overall)
    denom = lax.optimization_barrier(jnp.sum(totals * factor, axis=0)) + self_weight
    numer = lax.optimization_barrier(jnp.sum(partials * factor[..., None], axis=0)) + self_weight[..., None] * new_key[:, None, :KVL].astype(jnp.float32)
    attn_latent = (numer / denom[..., None]).astype(jnp.bfloat16)
    return (q_latent, attn_latent)
```

```python
import functools

import jax
import jax.numpy as jnp
import numpy as np
from jax import lax
from jax.experimental import pallas as pl
from jax.experimental.pallas import tpu as pltpu
from jax.sharding import PartitionSpec as P

QL = 1536
KVL = 512
ROPE = 64
PAGE = 32


softmax_scale = 192.0 ** (-0.5)
norm_eps = 1e-06


def combined_all(part, axis, combine):
    gathered = jax.tree.map(lambda a: lax.all_gather(a, axis), part)

    def take(source):
        return jax.tree.map(lambda a: lax.dynamic_index_in_dim(a, source, 0, False), gathered)

    return lax.fori_loop(
        1, lax.axis_size(axis), lambda source, state: combine(state, take(source)), take(0)
    )


def rope_rotate(matrix, col_start, positions):
    col_count = matrix.shape[1]
    columns = col_start + jnp.arange(col_count, dtype=jnp.int32)
    is_rope = columns >= KVL
    pair_index = jnp.maximum(columns - KVL, 0) // 2
    frequency = jnp.power(jnp.float32(10000.0), -(2 * pair_index).astype(jnp.float32) / ROPE)
    angles = positions[:, None] * frequency[None, :]
    cosine = jnp.where(is_rope[None, :], jnp.cos(angles), 1.0)
    sine_part = jnp.where(is_rope[None, :], jnp.sin(angles), 0.0)
    paired = matrix.reshape(matrix.shape[0], col_count // 2, 2)
    partner = jnp.stack([-paired[:, :, 1], paired[:, :, 0]], axis=2).reshape(matrix.shape)
    return matrix * cosine + partner * sine_part


def kv_finish(matrix, col_start, latent_sq, kv_gain, positions):
    col_count = matrix.shape[1]
    columns = col_start + jnp.arange(col_count, dtype=jnp.int32)
    gain_full = jnp.concatenate([kv_gain, jnp.ones((ROPE,), jnp.float32)])
    gain_cols = lax.dynamic_slice_in_dim(gain_full, col_start, col_count)
    inverse = lax.rsqrt(latent_sq / KVL + norm_eps)
    row_scale = jnp.where(columns[None, :] < KVL, inverse[:, None] * gain_cols[None, :], 1.0)
    return rope_rotate(matrix * row_scale, col_start, positions).astype(jnp.bfloat16)


def take_each(array, ids):
    return lax.map(lambda i: lax.dynamic_index_in_dim(array, i, 0, False), ids)


def pack_pages(kv_pages, page_table, owner_count, capacity):
    owners = page_table[:, 0]
    slot_ids = page_table[:, 1]
    page_ids = jnp.arange(kv_pages.shape[0], dtype=jnp.int32)
    earlier = (owners[:, None] == owners[None, :]) & (page_ids[None, :] < page_ids[:, None])
    ranking = jnp.sum(earlier.astype(jnp.int32), axis=1)
    targets = owners * capacity + ranking
    places = jnp.arange(owner_count * capacity, dtype=jnp.int32)
    matches = targets[None, :] == places[:, None]
    source_ids = jnp.sum(jnp.where(matches, page_ids[None, :], 0), axis=1)
    filled = jnp.any(matches, axis=1)
    chosen = jnp.where(
        filled[:, None, None], take_each(kv_pages, source_ids), jnp.zeros((), kv_pages.dtype)
    )
    labels = jnp.where(filled, jnp.take(slot_ids, source_ids), -1).astype(jnp.bfloat16)
    return (
        chosen.reshape(owner_count, capacity, kv_pages.shape[1], kv_pages.shape[2]),
        labels.reshape(owner_count, capacity),
    )


def place_pages(old_cache, got_pages, got_labels):
    flat_pages = got_pages.reshape(-1, old_cache.shape[1], old_cache.shape[2])
    label_ids = got_labels.reshape(-1).astype(jnp.int32)
    slot_ids = jnp.arange(old_cache.shape[0], dtype=jnp.int32)
    arrival_ids = jnp.arange(label_ids.shape[0], dtype=jnp.int32)
    matches = label_ids[None, :] == slot_ids[:, None]
    source_ids = jnp.sum(jnp.where(matches, arrival_ids[None, :], 0), axis=1)
    arrived = jnp.any(matches, axis=1)
    return jnp.where(arrived[:, None, None], take_each(flat_pages, source_ids), old_cache)


def combine_parts(former, latter):
    overall = jnp.maximum(former[0], latter[0])
    front_scale = jnp.exp(former[0] - overall)
    back_scale = jnp.exp(latter[0] - overall)
    return (
        overall,
        former[1] * front_scale + latter[1] * back_scale,
        former[2] * front_scale[:, :, None] + latter[2] * back_scale[:, :, None],
    )


MESH = pl.DeviceIdType.MESH


def fused_kernel(
    dims, w_ref, x_ref, qg_ref, kg_ref, rope_ref, bt_ref, lens_ref, plan_s_ref, plan_ref,
    old_ref, dq_ref, nk_ref, q_out, a_out,
    wq, wk, x2, xk, xo, pt, bq, cq, eq, yq, yr, qa, po, bo, co, eo, yo, yi, qo, ro, ri,
    ss, ssin, kvp, bk, ck, ek, kvl, sendp, got, plan_pad, plans, plans_s, rope, oldv,
    over_keys, new_keys, stat, first_out, part, pstat, parts, pstats, selfs, newk, fin,
    local_sem, zs, zr, ks, kr, xy, xz_s, xz_r,
    t_s, t_r, h_s, h_r, v_s, v_r, ot_s, ot_r, oh_s, oh_r, ov_s, ov_r, oz_s, oz_r,
    tk_s, tk_r, sk_s, sk_r, pl_s, pl_r, pg_s, pg_r, ag_s, ag_r, c_s, c_r, f_s, f_r, n_s, n_r,
):
    D, G, S, T, K, F = dims
    C, fh = w_ref.shape[0], w_ref.shape[1] // G
    rows = x_ref.shape[0]
    qw = q_out.shape[1]
    kvw = kvl.shape[2]
    cr = C // K
    N = fh - F
    NQ = QL // cr
    pages = rows // PAGE
    lane_rows = kvl.shape[1]
    cap_rows = sendp.shape[1]
    cap = capacity(pages, D)
    requests, heads = dq_ref.shape[0], dq_ref.shape[1]
    per = bt_ref.shape[2]
    spans = per * PAGE
    fold = requests * heads // D
    bf, f32 = jnp.bfloat16, jnp.float32
    me, g = lax.axis_index("dec"), lax.axis_index("grp")
    s, t = lax.axis_index("stg"), lax.axis_index("tp")
    lane = s * T + t
    mine_half = pl.ds(pl.multiple_of(g * fh, 128), fh)
    other_half = pl.ds(pl.multiple_of((1 - g) * fh, 128), fh)
    ends = []

    def remote(src, dst, send, recv, target):
        return pltpu.make_async_remote_copy(
            src_ref=src, dst_ref=dst, send_sem=send, recv_sem=recv,
            device_id=target, device_id_type=MESH,
        )

    def local(src, dst, i):
        copy = pltpu.make_async_copy(src, dst, local_sem.at[i])
        copy.start()
        return copy

    def when(condition, action):
        @pl.when(condition)
        def _():
            action()

    own_w = []
    for j in range(D):
        own_w.append(pltpu.make_async_copy(
            w_ref.at[:, mine_half], wq.at[j * C : (j + 1) * C], local_sem.at[0]
        ))
        when(me == j, own_w[j].start)
    x_mine = local(x_ref.at[:, mine_half], x2.at[g], 1)
    x_other = local(x_ref.at[:, other_half], xk, 2)
    kv_cut = 3 * C - QL
    wk_copies = {
        2: pltpu.make_async_copy(
            w_ref.at[C - kv_cut : C, other_half], wk.at[:kv_cut], local_sem.at[3]),
        3: pltpu.make_async_copy(w_ref.at[:, other_half], wk.at[kv_cut:], local_sem.at[3]),
    }
    for j, copy in wk_copies.items():
        when(me == j, copy.start)
    rope_copy = local(
        rope_ref.at[pl.ds(me * pages, pages),
                    pl.ds(pl.multiple_of(lane * lane_rows, 8), lane_rows)], rope, 4
    )
    old_copy = local(old_ref, oldv, 5)

    barrier = pltpu.get_barrier_semaphore()
    greeted = [{"dec": lax.rem(me + d, D)} for d in range(1, D)]
    greeted += [{"grp": 1 - g}, {"tp": 1 - t}, {"stg": 1 - s}, {"stg": 1 - s, "tp": 1 - t}]
    for target in greeted:
        pl.semaphore_signal(barrier, inc=1, device_id=target, device_id_type=MESH)
    pl.semaphore_wait(barrier, len(greeted))

    def w_rows(i, width):
        return wq.at[i * cr : (i + 1) * cr, :width]

    def z_width(i, m, way):
        return N if (m + way in (0, D - 1) and K <= i < NQ) else fh

    def z_copy(i, m, way):
        width = z_width(i, m, way)
        if i // K == m:
            at = (i - m * K) * cr
            src = w_ref.at[at : at + cr, pl.ds(pl.multiple_of(g * fh, 128), width)]
        else:
            src = w_rows(i, width)
        return remote(
            src, w_rows(i, width), zs.at[(way + 1) // 2, i], zr.at[i], {"dec": m + way}
        )

    def z_start(i, m, way):
        z_copy(i, m, way).start()

    def z_wait(i, m):
        way = -1 if i // K > m else 1
        z_copy_in(i, m, way).wait_recv()

    def z_copy_in(i, m, way):
        width = z_width(i, m - way, way)
        return remote(
            w_rows(i, width), w_rows(i, width), zs.at[(way + 1) // 2, i], zr.at[i],
            {"dec": m - way},
        )

    def k_rows(i):
        return (i - NQ) * cr

    def k_copy(i):
        at = k_rows(i)
        return remote(
            w_rows(i, fh), wk.at[at : at + cr], ks.at[i - NQ], kr.at[i - NQ], {"grp": 1 - g}
        )

    def sends_of(m, way):
        if not 0 <= m + way < D:
            return []
        return [
            i for i in range(D * K)
            if (i // K == m or (i // K > m if way < 0 else i // K < m))
            and not (way > 0 and i // K == D - 1) and not (way < 0 and i // K == 0)
        ]

    LM = list(range(3 * K, 4 * K)) + list(range(NQ, 3 * K)) + list(range(2 * K, NQ))
    RM = list(range(K, 2 * K)) + list(range(K))

    x_swap = remote(
        x_ref.at[:, other_half], x2.at[g], xy.at[0], xy.at[1], {"grp": 1 - g}
    )

    def x_arrived():
        return remote(
            x2.at[1 - g], x2.at[1 - g], xy.at[0], xy.at[1], {"grp": 1 - g}
        )

    def x_out_own(m):
        way = 1 if m == 0 else -1
        return remote(
            x_ref.at[:, pl.ds(pl.multiple_of(g * fh + N, 128), F)], xo.at[g],
            xz_s.at[0], xz_r.at[0], {"dec": m + way},
        )

    def x_out_other(m):
        way = 1 if m == 0 else -1
        return remote(
            x2.at[1 - g, :, N:], xo.at[1 - g], xz_s.at[1], xz_r.at[1], {"dec": m + way}
        )

    plan_pad[...] = jnp.full(plan_pad.shape, -1, jnp.int32)
    plan_pad[0:2, 0:pages] = plan_ref[...]
    plan_copies = []

    def start_first(m):
        def go():
            if m == 3:
                for i in range(3 * K, 4 * K):
                    z_start(i, 3, -1)
                if F:
                    x_out_own(3).start()
            if m == 2:
                for i in range(NQ, 3 * K):
                    z_start(i, 2, -1)
                    z_start(i, 2, 1)
                for i in range(2 * K, NQ):
                    z_start(i, 2, 1)
            if m == 1:
                for i in range(K, 2 * K):
                    z_start(i, 1, 1)
                for i in range(K, K + 2):
                    z_start(i, 1, -1)
            if m == 0:
                for i in range(K):
                    z_start(i, 0, 1)
                if F:
                    x_out_own(0).start()
        return go

    for d in range(1, D):
        copy = remote(
            plan_pad, plans.at[me], pl_s.at[d - 1], pl_r.at[d - 1], {"dec": lax.rem(me + d, D)}
        )
        copy.start()
        plan_copies.append(copy)
    plans[me] = plan_pad[...]
    for m in (3, 2, 1, 0):
        when(me == m, start_first(m))
    x_swap.start()

    def waited_at_tick(i, m):
        if i // K > m:
            return i in LM and (m > 0 or i >= NQ)
        return (i in RM and m < D - 1) or i >= NQ

    def relay(n):
        def go(m):
            def act():
                if n < len(LM):
                    i = LM[n]
                    if i // K > m and waited_at_tick(i, m):
                        z_wait(i, m)
                        if m > 0:
                            z_start(i, m, -1)
                        if i >= NQ:
                            k_copy(i).start()
                if n < len(RM):
                    i = RM[n]
                    if i // K < m and waited_at_tick(i, m):
                        z_wait(i, m)
                        z_start(i, m, 1)
                if m == D - 1 and n < 3 * K - NQ:
                    i = NQ + n
                    z_wait(i, m)
                    k_copy(i).start()
                if m == 1 and n >= K and K + 2 + (n - K) < 2 * K:
                    z_start(K + 2 + (n - K), 1, -1)
                if m == 2 and n == K - 1:
                    for i in range(2 * K, NQ):
                        z_start(i, 2, -1)
            return act
        for m in range(D):
            when(me == m, go(m))

    def lane_of(p):
        l = p[0] * cr // qw
        return l // T, l % T, p[0] * cr - l * qw

    def mul(acc_ref, at, a, b, xs, lo, hi):
        for half in range(G):
            acc_ref[at : at + b - a, half * rows : (half + 1) * rows] = lax.dot_general(
                wq[a:b, lo:hi], xs[half] if xs is not x2 else xs[half, :, lo:hi],
                (((1,), (1,)), ((), ())), preferred_element_type=f32,
            )

    def t_copy(p, out):
        a, b = p[0] * cr, p[1] * cr
        i = PIECES.index(p)
        if out:
            at = a - K * cr
            return remote(
                po.at[at : at + b - a], bo.at[at : at + b - a], ot_s.at[i], ot_r.at[i],
                {"tp": 1 - t},
            )
        return remote(pt.at[a:b], bq.at[a:b], t_s.at[i], t_r.at[i], {"tp": 1 - t})

    def h_copy(p, out):
        la = lane_of(p)[2]
        n, i = (p[1] - p[0]) * cr, PIECES.index(p)
        src, dst, send, recv = (co, eo, oh_s, oh_r) if out else (cq, eq, h_s, h_r)
        return remote(
            src.at[la : la + n], dst.at[la : la + n], send.at[i], recv.at[i], {"stg": 1 - s}
        )

    def v_copy(p, out):
        la = lane_of(p)[2]
        n, i = (p[1] - p[0]) * cr, PIECES.index(p)
        src, dst, send, recv = (yo, yi, ov_s, ov_r) if out else (yq, yr, v_s, v_r)
        return remote(
            src.at[la : la + n], dst.at[la : la + n], send.at[i], recv.at[i], {"grp": 1 - g}
        )

    def z_back(p, m):
        la = lane_of(p)[2]
        n, i = (p[1] - p[0]) * cr, PIECES.index(p)
        return remote(
            ro.at[la : la + n], ri.at[la : la + n], oz_s.at[i], oz_r.at[i],
            {"dec": 0 if m == 1 else D - 1},
        )

    def is_in(planes):
        result = me == planes[0]
        for m in planes[1:]:
            result = result | (me == m)
        return result

    def step_compute(p, planes, out):
        a, b = p[0] * cr, p[1] * cr
        sl, tl, _ = lane_of(p)
        for m in planes:
            def arrive(m=m):
                for i in range(*p):
                    if i // K != m and not out and not waited_at_tick(i, m):
                        z_wait(i, m)
            if not out and any(i // K != m and not waited_at_tick(i, m) for i in range(*p)):
                when(me == m, arrive)

        def full():
            if out:
                mul(po, a - K * cr, a, b, xo, N, fh)
            else:
                mul(pt, a, a, b, x2, 0, fh)

        def narrow():
            mul(pt, a, a, b, x2, 0, N)

        ended = tuple(m for m in planes if m in (0, D - 1))
        inner = tuple(m for m in planes if m not in (0, D - 1))
        if not out and F and p[0] >= K:
            if inner:
                when(is_in(inner), full)
            if ended:
                when(is_in(ended), narrow)
        else:
            when(is_in(planes), full)
        when(is_in(planes) & (t != tl), t_copy(p, out).start)

    def step_tp(p, planes, out):
        a, b = p[0] * cr, p[1] * cr
        sl, tl, la = lane_of(p)
        acc, add, to = (po, bo, co) if out else (pt, bq, cq)
        at = a - K * cr if out else a
        n = b - a

        def act():
            t_copy(p, out).wait_recv()

            @pl.when(s != sl)
            def _():
                to[la : la + n, :] = (acc[at : at + n, :] + add[at : at + n, :]).astype(bf)
                h_copy(p, out).start()

            @pl.when(s == sl)
            def _():
                acc[at : at + n, :] = acc[at : at + n, :] + add[at : at + n, :]
        when(is_in(planes) & (t == tl), act)

    def g_cols(which):
        return pl.ds(pl.multiple_of(which * rows, 128), rows)

    def step_x(p, planes, out):
        a, b = p[0] * cr, p[1] * cr
        sl, tl, la = lane_of(p)
        acc, came, keep, to = (po, eo, qo, yo) if out else (pt, eq, qa, yq)
        at = a - K * cr if out else a
        n = b - a

        def act():
            h_copy(p, out).wait_recv()
            to[la : la + n, :] = (
                acc[at : at + n, g_cols(1 - g)] + came[la : la + n, g_cols(1 - g)].astype(f32)
            ).astype(bf)
            v_copy(p, out).start()
            keep[la : la + n, :] = (
                acc[at : at + n, g_cols(g)] + came[la : la + n, g_cols(g)].astype(f32)
            )
        when(is_in(planes) & (t == tl) & (s == sl), act)

    def step_y(p, planes, out):
        sl, tl, la = lane_of(p)
        n = (p[1] - p[0]) * cr

        def act():
            v_copy(p, out).wait_recv()
            if out:
                ro[la : la + n, :] = (
                    qo[la : la + n, :] + yi[la : la + n, :].astype(f32)
                ).astype(bf)
                for m in planes:
                    when(me == m, z_back(p, m).start)
            else:
                qa[la : la + n, :] = qa[la : la + n, :] + yr[la : la + n, :].astype(f32)
        when(is_in(planes) & (t == tl) & (s == sl), act)

    def step_back(p):
        sl, tl, la = lane_of(p)
        n = (p[1] - p[0]) * cr

        def act():
            z_back(p, 1).wait_recv()
            qa[la : la + n, :] = qa[la : la + n, :] + ri[la : la + n, :].astype(f32)
        when(is_in((0, D - 1)) & (t == tl) & (s == sl), act)

    def k_lane(at):
        return pl.ds(pl.multiple_of(at * lane_rows, 8), lane_rows)

    tk, sk, pg, ag, cc, ff, small = [], [], [], [], [], [], []

    def kv_project():
        for i in range(NQ, D * K):
            when(me != i // K, k_copy(i).wait_recv)
        for half in range(2):
            at = pl.ds(half * (rows // 2), rows // 2)
            total = lax.dot_general(
                x2[g, at, :], wq[QL:, :], (((1,), (1,)), ((), ())), preferred_element_type=f32
            ) + lax.dot_general(
                xk[at, :], wk[...], (((1,), (1,)), ((), ())), preferred_element_type=f32
            )
            kvp[pl.ds(half * (pages // 2), pages // 2)] = total.reshape(pages // 2, PAGE, kvw)
        for i in range(S):
            a = lax.rem(s + 1 + i, S)
            copy = remote(
                kvp.at[:, k_lane(a * T + 1 - t)], bk.at[a], tk_s.at[i], tk_r.at[i], {"tp": 1 - t}
            )
            copy.start()
            tk.append(copy)

    def kv_across():
        tk[0].wait_recv()
        ck[...] = kvp[:, k_lane((1 - s) * T + t), :] + bk[1 - s]
        copy = remote(ck, ek, sk_s.at[0], sk_r.at[0], {"stg": 1 - s})
        copy.start()
        sk.append(copy)

    def kv_norm():
        tk[1].wait_recv()
        k = kvp[:, k_lane(lane), :] + bk[s]
        sk[0].wait_recv()
        k = (k + ek[...]).reshape(pages * lane_rows, kvw)
        lat, tail = k[:, :KVL], k[:, KVL:]
        square = jnp.sum(lat * lat, axis=1, keepdims=True)
        lat = lat * (lax.rsqrt(square / KVL + norm_eps) * kg_ref[...])
        to = lax.broadcasted_iota(jnp.int32, (ROPE, ROPE), 1)
        at = lax.broadcasted_iota(jnp.int32, (ROPE, ROPE), 0)
        even = lax.rem(to, 2) == 0
        swap = jnp.where(even & (at == to + 1), -1.0, 0.0)
        swap = jnp.where(jnp.logical_not(even) & (at == to - 1), 1.0, swap)
        partner = jnp.dot(
            tail, swap, preferred_element_type=f32, precision=lax.Precision.HIGHEST
        )
        turn = rope[...].reshape(pages * lane_rows, 2 * ROPE)
        tail = tail * turn[:, :ROPE] + partner * turn[:, ROPE:]
        kvl[:, :, :KVL] = lat.reshape(pages, lane_rows, KVL)
        kvl[:, :, KVL:] = tail.reshape(pages, lane_rows, ROPE)
        for o in range(D):
            taken = [kvl[source_of(o, r)] for r in range(cap)]
            taken += [jnp.zeros((lane_rows, kvw), f32)] * (cap_rows // lane_rows - cap)
            sendp[o] = jnp.concatenate(taken, axis=0).astype(bf)
        for d in range(1, D):
            to = lax.rem(me + d, D)
            copy = remote(
                sendp.at[to], got.at[lane, me], pg_s.at[d - 1], pg_r.at[d - 1], {"dec": to}
            )
            copy.start()
            pg.append(copy)
        got[lane, me] = sendp[me]

    picked = {}

    def choose():
        owners = [plan_s_ref[0, p] for p in range(pages)]
        ranks = []
        for p in range(pages):
            rank = jnp.int32(0)
            for e in range(p):
                rank = rank + (owners[e] == owners[p]).astype(jnp.int32)
            ranks.append(rank)
        for o in range(D):
            for r in range(cap):
                found = jnp.int32(0)
                for p in range(pages):
                    found = jnp.where((owners[p] == o) & (ranks[p] == r), p, found)
                picked[o, r] = found

    def source_of(o, r):
        return picked[o, r]

    def tables():
        for copy in plan_copies:
            copy.wait_recv()
        copy = pltpu.make_async_copy(plans, plans_s, local_sem.at[6])
        copy.start()
        copy.wait()
        count = requests * per
        slots_row = jnp.full((8, 128), -1, jnp.int32)
        slots_col = jnp.full((16, 128), -1, jnp.int32)
        across = lax.broadcasted_iota(jnp.int32, (8, 128), 1)
        down = lax.broadcasted_iota(jnp.int32, (16, 128), 0)
        for d in range(D):
            rank = jnp.int32(d * cap)
            for p in range(pages):
                ours = plans_s[d, 0, p] == me
                slot = plans_s[d, 1, p]
                at = jnp.where(ours, rank, -1)
                slots_row = jnp.where(across == at, slot, slots_row)
                slots_col = jnp.where(down == at, slot, slots_col)
                rank = rank + ours.astype(jnp.int32)
        table_row = jnp.full((16, 128), -2, jnp.int32)
        table_col = jnp.full((count, 128), -2, jnp.int32)
        across16 = lax.broadcasted_iota(jnp.int32, (16, 128), 1)
        down_count = lax.broadcasted_iota(jnp.int32, (count, 128), 0)
        for k in range(count):
            slot = bt_ref[0, k // per, k % per]
            table_row = jnp.where(across16 == k, slot, table_row)
            table_col = jnp.where(down_count == k, slot, table_col)
        hit = jnp.where(table_col == slots_row[0:1], 1.0, 0.0)
        over = jnp.max(hit, axis=1, keepdims=True)
        key = lax.broadcasted_iota(jnp.int32, (count, count * PAGE), 1)
        entry = lax.broadcasted_iota(jnp.int32, (count, count * PAGE), 0)
        over = jnp.sum(jnp.where(key // PAGE == entry, over, 0.0), axis=0, keepdims=True)
        over_keys[...] = jnp.broadcast_to(over, over_keys.shape)
        place = jnp.where(slots_col == table_row, across16.astype(f32) + 1.0, 0.0)
        place = jnp.max(place, axis=1, keepdims=True)
        width = new_keys.shape[1]
        key = lax.broadcasted_iota(jnp.int32, (16, width), 1)
        entry = lax.broadcasted_iota(jnp.int32, (16, width), 0)
        inside = lax.rem(key, cap_rows)
        source = lax.rem(key // cap_rows, D)
        arrival = source * cap + inside // lane_rows
        valid = (inside // lane_rows < cap) & (arrival == entry)
        place = jnp.sum(jnp.where(valid, place, 0.0), axis=0, keepdims=True)
        new_keys[...] = jnp.broadcast_to(place, new_keys.shape)

    def old_attend(r):
        def act():
            keys = jnp.concatenate(
                [oldv[bt_ref[0, r, j]] for j in range(per)], axis=0
            )
            scores = lax.dot_general(
                dq_ref[r], keys, (((1,), (1,)), ((), ())), preferred_element_type=f32
            ) * softmax_scale
            at = lax.broadcasted_iota(jnp.int32, scores.shape, 1)
            live = (at < lens_ref[0, r]) & (
                over_keys[0:1, r * spans : (r + 1) * spans] < 0.5
            )
            scores = jnp.where(live, scores, -1e30)
            peak = jnp.max(scores, axis=1, keepdims=True)
            weight = jnp.where(live, jnp.exp(scores - peak), 0.0)
            total = jnp.sum(weight, axis=1, keepdims=True)
            mine = slice(r * heads, (r + 1) * heads)
            first_out[mine, :] = jnp.dot(
                weight.astype(bf), keys[:, :KVL], preferred_element_type=f32
            )
            column = lax.broadcasted_iota(jnp.int32, (heads, 128), 1)
            stat[mine, :] = jnp.where(column < 64, peak, total)
            query = dq_ref[r].astype(f32)
            row = nk_ref[r : r + 1, :].astype(f32)
            score = jnp.sum(query * row, axis=1, keepdims=True) * softmax_scale
            selfs[mine, :] = jnp.broadcast_to(score, (heads, 128))
            newk[mine, :] = jnp.broadcast_to(row[:, :KVL], (heads, KVL))
        return act

    def got_copy(at, which, target):
        return remote(got.at[at], got.at[at], ag_s.at[which], ag_r.at[which], target)

    def gather():
        for copy in pg:
            copy.wait_recv()
        for which, target in ((0, {"stg": 1 - s}), (1, {"tp": 1 - t})):
            copy = got_copy(lane, which, target)
            copy.start()
            ag.append(copy)

    def gather_on():
        ag[0].wait_recv()
        copy = got_copy((1 - s) * T + t, 2, {"tp": 1 - t})
        copy.start()
        ag.append(copy)

    def attend():
        ag[1].wait_recv()
        ag[2].wait_recv()
        keys = got[...].reshape(S * T * D * cap_rows, kvw)
        queries = dq_ref[...].reshape(requests * heads, kvw)
        scores = lax.dot_general(
            queries, keys, (((1,), (1,)), ((), ())), preferred_element_type=f32
        ) * softmax_scale
        place = new_keys[0:1, :].astype(jnp.int32) - 1
        at = lax.broadcasted_iota(jnp.int32, (1, scores.shape[1]), 1)
        inside = lax.rem(at, cap_rows)
        from_lane = at // (D * cap_rows)
        token = lax.rem(place, per) * PAGE + from_lane * lane_rows + lax.rem(inside, lane_rows)
        asked = jnp.where(place >= 0, place // per, -1)
        request = lax.broadcasted_iota(jnp.int32, (requests * heads, 1), 0) // heads
        length = jnp.zeros((requests * heads, 1), jnp.int32)
        for r in range(requests):
            length = jnp.where(request == r, lens_ref[0, r], length)
        live = (asked == request) & (token < length)
        scores = jnp.where(live, scores, -1e30)
        peak = stat[:, 0:1]
        peak2 = jnp.maximum(peak, jnp.max(scores, axis=1, keepdims=True))
        weight = jnp.where(live, jnp.exp(scores - peak2), 0.0)
        scale = jnp.exp(peak - peak2)
        total = jnp.sum(weight, axis=1, keepdims=True) + stat[:, 64:65] * scale
        part[...] = (
            jnp.dot(weight.astype(bf), keys[:, :KVL], preferred_element_type=f32)
            + first_out[...] * scale
        ).astype(bf)
        column = lax.broadcasted_iota(jnp.int32, pstat.shape, 1)
        pstat[...] = jnp.where(column < 64, peak2, total)
        for d in range(1, D):
            to = lax.rem(me + d, D)
            at = pl.ds(pl.multiple_of(to * fold, 16), fold)
            for which, src, dst in ((0, pstat, pstats), (1, part, parts)):
                copy = remote(
                    src.at[at], dst.at[d - 1], c_s.at[which, d - 1], c_r.at[which, d - 1],
                    {"dec": to},
                )
                copy.start()
                cc.append(copy)

    def combine():
        for copy in cc:
            copy.wait_recv()
        mine = pl.ds(pl.multiple_of(me * fold, 16), fold)
        shares = [(pstat[mine, :], part[mine, :])]
        shares += [(pstats[d], parts[d]) for d in range(D - 1)]
        own_score = selfs[mine, 0:1]
        top = own_score
        for stats, _ in shares:
            top = jnp.maximum(top, stats[:, 0:1])
        own_weight = jnp.exp(own_score - top)
        numer, denom = own_weight * newk[mine, :], own_weight
        for stats, share in shares:
            factor = jnp.exp(stats[:, 0:1] - top)
            numer = numer + factor * share.astype(f32)
            denom = denom + factor * stats[:, 64:65]
        fin[me] = (numer / denom).astype(bf)
        for d in range(1, D):
            copy = remote(
                fin.at[me], fin.at[me], f_s.at[d - 1], f_r.at[d - 1], {"dec": lax.rem(me + d, D)}
            )
            copy.start()
            ff.append(copy)

    def settle():
        for copy in ff:
            copy.wait_recv()
        for e in range(D):
            a_out[e * fold : (e + 1) * fold, :] = fin[e]

    PIECES = pieces_of(K, NQ, qw // cr)
    due = {}

    def add(tick, action, *args):
        due.setdefault(tick, []).append((action, args))

    def route(tick, p, planes, out=False):
        add(tick, step_compute, p, planes, out)
        add(tick + 1, step_tp, p, planes, out)
        add(tick + 1 + HOPX, step_x, p, planes, out)
        add(tick + 1 + HOPX + HOPY, step_y, p, planes, out)
        if out:
            add(tick + 2 + HOPX + 2 * HOPY, step_back, p)

    blocks = [[p for p in PIECES if p[0] // K == j] for j in range(3)]
    last = 2 * K - 1

    def x_need():
        x_arrived().wait_recv()
        if F:
            for m in (0, D - 1):
                when(me == m, x_out_other(m).start)

    add(1, choose)
    add(3, tables)
    for r in range(requests):
        add(4 + r // 2, old_attend(r))
    add(OWN - 1, x_need)
    for j in range(3):
        for n, p in enumerate(blocks[j]):
            add_tick = OWN + n
            route(add_tick, p, (j,))
    for p in blocks[1]:
        done = p[1] - K - 1
        route(max(done + 1, OWN + 3), p, (2, 3))
        route(last - (1 if p is blocks[1][0] else 0), p, (0,))
    for p in blocks[0]:
        route(K + p[1] - 1, p, (1, 2, 3))
    for n, p in enumerate(blocks[2]):
        route(OWN + 5 + n, p, (3,))
        route(K + (3 * K - NQ) + p[1] - 2 * K - 1, p, (0, 1))
    if F:
        def xo_need():
            when(is_in((1, 2)), lambda: x_wait_in())
        add(OUT - 1, xo_need)
        for n, p in enumerate(blocks[1] + blocks[2]):
            route(max(OUT + n, last + 1 if p[0] >= 2 * K and p is blocks[2][-1] else 0), p, (1, 2), True)

    def x_wait_in():
        for half in range(2):
            remote(
                xo.at[half], xo.at[half], xz_s.at[0], xz_r.at[half], {"grp": 1 - g}
            ).wait_recv()

    kv_at = KV
    for gap, stage in zip(KV_GAPS, (kv_project, kv_across, kv_norm, gather, gather_on, attend, combine, settle)):
        add(kv_at + gap, stage)

    for j in range(D):
        if j in wk_copies:
            when(me == j, wk_copies[j].wait)
    x_mine.wait()
    x_other.wait()
    rope_copy.wait()
    old_copy.wait()
    for j in range(D):
        when(me == j, own_w[j].wait)

    for n in range(max(list(due) + [2 * K]) + 1):
        if n < 2 * K:
            relay(n)
        for action, args in due.get(n, ()):
            action(*args)

    q = qa[...]
    ss[...] = jnp.broadcast_to(jnp.sum(q * q, axis=0, keepdims=True), ss.shape)
    for i, target in enumerate(({"tp": 1 - t}, {"stg": 1 - s}, {"stg": 1 - s, "tp": 1 - t})):
        copy = remote(ss, ssin.at[i], n_s.at[i], n_r.at[i], target)
        copy.start()
        small.append(copy)
    gain = qg_ref[:, pl.ds(pl.multiple_of(lane * qw, 128), qw)]
    turned = jnp.transpose(q) * gain
    square = ss[...]
    for i, copy in enumerate(small):
        copy.wait_recv()
        square = square + ssin[i]
    inverse = jnp.transpose(lax.rsqrt(square / QL + norm_eps))
    q_out[...] = (turned * inverse[:, 0:1]).astype(bf)

    for copy in [x_swap] + plan_copies + tk + sk + pg + ag + cc + ff + small:
        copy.wait_send()
    for m in range(D):
        def left(m=m):
            for way in (-1, 1):
                for i in sends_of(m, way):
                    z_copy(i, m, way).wait_send()
            for i in range(NQ, D * K):
                if i // K != m:
                    k_copy(i).wait_send()
            if F and m in (0, D - 1):
                x_out_own(m).wait_send()
                x_out_other(m).wait_send()
        when(me == m, left)
    for p in PIECES:
        sl, tl, _ = lane_of(p)
        for out in ((False, True) if F and p[0] >= K else (False,)):
            inside = is_in((1, 2)) if out else is_in(tuple(range(D)))
            when(inside & (t != tl), t_copy(p, out).wait_send)
            when(inside & (t == tl) & (s != sl), h_copy(p, out).wait_send)
            when(inside & (t == tl) & (s == sl), v_copy(p, out).wait_send)
            if out:
                when(inside & (t == tl) & (s == sl), z_back(p, 1).wait_send)


def capacity(pages, owners):
    return max(2, -(-pages // owners))


def chunk_count(rows):
    return next((k for k in (11, 3, 2) if rows % (16 * k) == 0), 1)


def pieces_of(K, NQ, lane_chunks):
    cuts = sorted(set(range(0, NQ + 1, lane_chunks)) | set(range(0, NQ, K)) | {NQ})
    pieces = []
    for a, b in zip(cuts, cuts[1:]):
        parts = -(-(b - a) // LONGEST)
        ends = [a + (b - a) * i // parts for i in range(parts + 1)]
        pieces += list(zip(ends, ends[1:]))
    return pieces


OWN, OUT, HOPX, HOPY = 8, 19, 5, 3
KV, KV_GAPS = 14, (0, 1, 4, 7, 9, 10, 14, 17)
LONGEST = 4
SHARE = 4


def fused_ok(hidden_x, proj_weight, old_cache, dec_query, page_plan, block_table):
    D, G, S, T = [lax.axis_size(n) for n in ("dec", "grp", "stg", "tp")]
    if (D, G, S, T) != (4, 2, 2, 2):
        return False
    rows, features = hidden_x.shape
    C = proj_weight.shape[1]
    K = chunk_count(C)
    cr, qw, lane_rows = C // K, QL // (S * T), PAGE // (S * T)
    pages = page_plan.shape[0]
    return (
        cr % 16 == 0
        and D * C == QL + KVL + ROPE
        and qw % cr == 0
        and qw % 128 == 0
        and 2 * C < QL < 3 * C
        and features % (128 * 7 * G) == 0
        and rows == pages * PAGE
        and rows % 128 == 0
        and pages % 2 == 0
        and lane_rows % 8 == 0
        and D * capacity(pages, D) <= 16
        and block_table.shape[1] * block_table.shape[2] <= 128
        and block_table.shape[1] == D
        and dec_query.shape[0] == D
        and dec_query.shape[1] % 16 == 0
    )


def fused(
    hidden_x, proj_weight, q_gain, kv_gain, old_cache, page_plan, block_table, split_lens,
    dec_query, new_key,
):
    D, G, S, T = [lax.axis_size(n) for n in ("dec", "grp", "stg", "tp")]
    L = S * T
    rows, features = hidden_x.shape
    C = proj_weight.shape[1]
    K = chunk_count(C)
    fh, qw, kvw = features // G, QL // L, KVL + ROPE
    F = fh * SHARE // 7
    cr, NQ = C // K, QL // (C // K)
    lane_rows = PAGE // L
    pages = page_plan.shape[0]
    cap = capacity(pages, D)
    cap_rows = -(-cap * lane_rows // 16) * 16
    requests, heads = dec_query.shape[0], dec_query.shape[1]
    width = block_table.shape[2]
    fold = requests * heads // D

    positions = np.arange(D * rows, dtype=np.float32)
    pair_index = np.arange(ROPE, dtype=np.int32) // 2
    frequency = np.power(np.float32(10000.0), -(2 * pair_index).astype(np.float32) / np.float32(ROPE))
    angles = positions[:, None] * frequency.astype(np.float32)[None, :]
    rope = np.concatenate([np.cos(angles), np.sin(angles)], axis=1).astype(np.float32)
    rope = jnp.asarray(rope.reshape(D * pages, PAGE, 2 * ROPE))

    dma = pltpu.SemaphoreType.DMA
    bf, f32, i32 = jnp.bfloat16, jnp.float32, jnp.int32
    vmem = pl.BlockSpec(memory_space=pltpu.VMEM)
    smem = pl.BlockSpec(memory_space=pltpu.SMEM)
    hbm = pl.BlockSpec(memory_space=pl.ANY)
    n = len(pieces_of(K, NQ, qw // cr))
    both = G * rows
    outs = (NQ - K) * cr if F else 16
    qo_rows = qw if F else 16
    V = pltpu.VMEM
    q_out, a_out = pl.pallas_call(
        functools.partial(fused_kernel, (D, G, S, T, K, F)),
        out_shape=(
            jax.ShapeDtypeStruct((rows, qw), bf),
            jax.ShapeDtypeStruct((requests * heads, KVL), bf),
        ),
        in_specs=[hbm, hbm, vmem, vmem, hbm, smem, smem, smem, vmem, hbm, vmem, vmem],
        out_specs=(vmem, vmem),
        scratch_shapes=[
            V((D * C, fh), bf), V((kvw, fh), bf), V((G, rows, fh), bf), V((rows, fh), bf),
            V((G, rows, max(F, 128)), bf),
            V((QL, both), f32), V((QL, both), f32), V((qw, both), bf), V((qw, both), bf),
            V((qw, rows), bf), V((qw, rows), bf), V((qw, rows), f32),
            V((outs, both), f32), V((outs, both), f32), V((qo_rows, both), bf), V((qo_rows, both), bf),
            V((qo_rows, rows), bf), V((qo_rows, rows), bf), V((qo_rows, rows), f32),
            V((qo_rows, rows), bf), V((qo_rows, rows), bf),
            V((8, rows), f32), V((L - 1, 8, rows), f32),
            V((pages, PAGE, kvw), f32), V((S, pages, lane_rows, kvw), f32),
            V((pages, lane_rows, kvw), f32), V((pages, lane_rows, kvw), f32),
            V((pages, lane_rows, kvw), f32),
            V((D, cap_rows, kvw), bf), V((L, D, cap_rows, kvw), bf),
            V((8, 128), i32), V((D, 8, 128), i32), pltpu.SMEM((D, 8, 128), i32),
            V((pages, lane_rows, 2 * ROPE), f32), V(old_cache.shape, bf),
            V((8, requests * width * PAGE), f32), V((8, L * D * cap_rows), f32),
            V((requests * heads, 128), f32), V((requests * heads, KVL), f32),
            V((requests * heads, KVL), bf), V((requests * heads, 128), f32),
            V((D - 1, fold, KVL), bf), V((D - 1, fold, 128), f32),
            V((requests * heads, 128), f32), V((requests * heads, KVL), f32),
            V((D, fold, KVL), bf),
            dma((7,)), dma((2, D * K)), dma((D * K,)), dma((D * K - NQ,)), dma((D * K - NQ,)),
            dma((2,)), dma((2,)), dma((2,)),
            dma((n,)), dma((n,)), dma((n,)), dma((n,)), dma((n,)), dma((n,)),
            dma((n,)), dma((n,)), dma((n,)), dma((n,)), dma((n,)), dma((n,)), dma((n,)), dma((n,)),
            dma((S,)), dma((S,)), dma((1,)), dma((1,)), dma((D - 1,)), dma((D - 1,)),
            dma((D - 1,)), dma((D - 1,)), dma((3,)), dma((3,)),
            dma((2, D - 1)), dma((2, D - 1)), dma((D - 1,)), dma((D - 1,)), dma((3,)), dma((3,)),
        ],
        compiler_params=pltpu.CompilerParams(
            collective_id=0, has_side_effects=True, vmem_limit_bytes=60 * 1024 * 1024
        ),
    )(
        proj_weight.T, hidden_x, q_gain[None, :], kv_gain[None, :], rope, block_table, split_lens.T,
        page_plan.T, page_plan.T, old_cache, dec_query, new_key,
    )
    return q_out, a_out.reshape(requests, heads, KVL)


def body(
    hidden_x,
    proj_weight,
    q_gain,
    kv_gain,
    old_cache,
    page_plan,
    block_table,
    split_lens,
    dec_query,
    new_key,
):
    if fused_ok(hidden_x, proj_weight, old_cache, dec_query, page_plan, block_table):
        return fused(
            hidden_x, proj_weight, q_gain, kv_gain, old_cache, page_plan, block_table,
            split_lens, dec_query, new_key,
        )
    projected = jnp.dot(
        hidden_x,
        lax.all_gather(proj_weight, "dec", axis=1, tiled=True),
        preferred_element_type=jnp.float32,
    )
    query_part = projected[:, :QL]
    kv_part = projected[:, QL:]
    tokens_here = hidden_x.shape[0]
    positions = (
        lax.axis_index("dec") * tokens_here + jnp.arange(tokens_here, dtype=jnp.int32)
    ).astype(jnp.float32)
    lane_count = lax.axis_size(("stg", "tp"))
    lane_index = lax.axis_index(("stg", "tp"))
    owner_count = lax.axis_size("dec")
    page_count = page_plan.shape[0]
    capacity = max(2, -(-page_count // owner_count))
    query_width = QL // lane_count
    query_cols, kv_cols = (
        lax.psum_scatter(query_part, ("stg", "tp"), scatter_dimension=1, tiled=True),
        lax.psum_scatter(kv_part, ("stg", "tp"), scatter_dimension=1, tiled=True),
    )
    kv_width = kv_cols.shape[1]
    col_start = lane_index * kv_width
    columns = col_start + jnp.arange(kv_width, dtype=jnp.int32)
    latent_part_sq = jnp.sum(jnp.where(columns[None, :] < KVL, kv_cols * kv_cols, 0.0), axis=1)
    query_sq, latent_sq = lax.psum(
        (jnp.sum(query_cols * query_cols, axis=1), latent_part_sq), ("stg", "tp")
    )
    kv_rows = kv_finish(kv_cols, col_start, latent_sq, kv_gain, positions)
    kv_pages = kv_rows.reshape(page_count, PAGE, kv_width)
    send_pages, send_labels = pack_pages(kv_pages, page_plan, owner_count, capacity)
    got_slices, got_labels = (
        lax.all_to_all(send_pages, "dec", split_axis=0, concat_axis=0, tiled=True),
        lax.all_to_all(send_labels, "dec", split_axis=0, concat_axis=0, tiled=True),
    )
    got_pages = lax.all_gather(got_slices, ("stg", "tp"), axis=3, tiled=True)
    query_gain = lax.dynamic_slice_in_dim(q_gain, lane_index * query_width, query_width)
    q_latent = (
        query_cols * lax.rsqrt(query_sq / QL + norm_eps)[:, None] * query_gain[None, :]
    ).astype(jnp.bfloat16)
    cache = place_pages(old_cache, got_pages, got_labels)
    slot_table = block_table[0]
    request_count = slot_table.shape[0]
    key_rows = take_each(cache, slot_table.reshape(-1)).reshape(
        request_count, -1, cache.shape[2]
    )
    scores = (
        jnp.einsum("rhc,rlc->rhl", dec_query, key_rows, preferred_element_type=jnp.float32)
        * softmax_scale
    )
    live_mask = jnp.arange(key_rows.shape[1], dtype=jnp.int32)[None, :] < split_lens[:, 0][:, None]
    scores = jnp.where(live_mask[:, None, :], scores, -1e30)
    row_peak = jnp.max(scores, axis=2)
    weights = jnp.where(live_mask[:, None, :], jnp.exp(scores - row_peak[:, :, None]), 0.0)
    row_total = jnp.sum(weights, axis=2)
    rounded = weights.astype(jnp.bfloat16)
    partial_out = jnp.einsum(
        "rhl,rlc->rhc", rounded, key_rows[:, :, :KVL], preferred_element_type=jnp.float32
    )
    peak_all, total_all, output_all = combined_all(
        (row_peak, row_total, partial_out), "dec", combine_parts
    )
    self_score = (
        jnp.einsum("rhc,rc->rh", dec_query, new_key, preferred_element_type=jnp.float32)
        * softmax_scale
    )
    overall = jnp.maximum(peak_all, self_score)
    carried = jnp.exp(peak_all - overall)
    self_weight = jnp.exp(self_score - overall)
    denom = total_all * carried + self_weight
    numer = output_all * carried[:, :, None] + self_weight[:, :, None] * new_key[
        :, None, :KVL
    ].astype(jnp.float32)
    attn_latent = (numer / denom[:, :, None]).astype(jnp.bfloat16)
    return (q_latent, attn_latent)


def solution(mesh):
    return jax.shard_map(
        body,
        mesh=mesh,
        in_specs=(
            P(("grp", "dec"), ("stg", "tp")),
            P(("stg", "tp"), "dec"),
            P(),
            P(),
            P(("grp", "dec"), None, None),
            P(("grp", "dec"), None),
            P(("grp", "dec"), None, None),
            P("grp", "dec"),
            P("grp", ("stg", "tp"), None),
            P("grp", None),
        ),
        out_specs=(P(("grp", "dec"), ("stg", "tp")), P("grp", ("stg", "tp"), None)),
        check_vma=False,
    )
```

```python
import functools

import jax
import jax.numpy as jnp
import numpy as np
from jax import lax
from jax.experimental import pallas as pl
from jax.experimental.pallas import tpu as pltpu
from jax.sharding import PartitionSpec as P

QL = 1536
KVL = 512
ROPE = 64
PAGE = 32


softmax_scale = 192.0 ** (-0.5)
norm_eps = 1e-06


def combined_all(part, axis, combine):
    gathered = jax.tree.map(lambda a: lax.all_gather(a, axis), part)

    def take(source):
        return jax.tree.map(lambda a: lax.dynamic_index_in_dim(a, source, 0, False), gathered)

    return lax.fori_loop(
        1, lax.axis_size(axis), lambda source, state: combine(state, take(source)), take(0)
    )


def rope_rotate(matrix, col_start, positions):
    col_count = matrix.shape[1]
    columns = col_start + jnp.arange(col_count, dtype=jnp.int32)
    is_rope = columns >= KVL
    pair_index = jnp.maximum(columns - KVL, 0) // 2
    frequency = jnp.power(jnp.float32(10000.0), -(2 * pair_index).astype(jnp.float32) / ROPE)
    angles = positions[:, None] * frequency[None, :]
    cosine = jnp.where(is_rope[None, :], jnp.cos(angles), 1.0)
    sine_part = jnp.where(is_rope[None, :], jnp.sin(angles), 0.0)
    paired = matrix.reshape(matrix.shape[0], col_count // 2, 2)
    partner = jnp.stack([-paired[:, :, 1], paired[:, :, 0]], axis=2).reshape(matrix.shape)
    return matrix * cosine + partner * sine_part


def kv_finish(matrix, col_start, latent_sq, kv_gain, positions):
    col_count = matrix.shape[1]
    columns = col_start + jnp.arange(col_count, dtype=jnp.int32)
    gain_full = jnp.concatenate([kv_gain, jnp.ones((ROPE,), jnp.float32)])
    gain_cols = lax.dynamic_slice_in_dim(gain_full, col_start, col_count)
    inverse = lax.rsqrt(latent_sq / KVL + norm_eps)
    row_scale = jnp.where(columns[None, :] < KVL, inverse[:, None] * gain_cols[None, :], 1.0)
    return rope_rotate(matrix * row_scale, col_start, positions).astype(jnp.bfloat16)


def take_each(array, ids):
    return lax.map(lambda i: lax.dynamic_index_in_dim(array, i, 0, False), ids)


def pack_pages(kv_pages, page_table, owner_count, capacity):
    owners = page_table[:, 0]
    slot_ids = page_table[:, 1]
    page_ids = jnp.arange(kv_pages.shape[0], dtype=jnp.int32)
    earlier = (owners[:, None] == owners[None, :]) & (page_ids[None, :] < page_ids[:, None])
    ranking = jnp.sum(earlier.astype(jnp.int32), axis=1)
    targets = owners * capacity + ranking
    places = jnp.arange(owner_count * capacity, dtype=jnp.int32)
    matches = targets[None, :] == places[:, None]
    source_ids = jnp.sum(jnp.where(matches, page_ids[None, :], 0), axis=1)
    filled = jnp.any(matches, axis=1)
    chosen = jnp.where(
        filled[:, None, None], take_each(kv_pages, source_ids), jnp.zeros((), kv_pages.dtype)
    )
    labels = jnp.where(filled, jnp.take(slot_ids, source_ids), -1).astype(jnp.bfloat16)
    return (
        chosen.reshape(owner_count, capacity, kv_pages.shape[1], kv_pages.shape[2]),
        labels.reshape(owner_count, capacity),
    )


def place_pages(old_cache, got_pages, got_labels):
    flat_pages = got_pages.reshape(-1, old_cache.shape[1], old_cache.shape[2])
    label_ids = got_labels.reshape(-1).astype(jnp.int32)
    slot_ids = jnp.arange(old_cache.shape[0], dtype=jnp.int32)
    arrival_ids = jnp.arange(label_ids.shape[0], dtype=jnp.int32)
    matches = label_ids[None, :] == slot_ids[:, None]
    source_ids = jnp.sum(jnp.where(matches, arrival_ids[None, :], 0), axis=1)
    arrived = jnp.any(matches, axis=1)
    return jnp.where(arrived[:, None, None], take_each(flat_pages, source_ids), old_cache)


def combine_parts(former, latter):
    overall = jnp.maximum(former[0], latter[0])
    front_scale = jnp.exp(former[0] - overall)
    back_scale = jnp.exp(latter[0] - overall)
    return (
        overall,
        former[1] * front_scale + latter[1] * back_scale,
        former[2] * front_scale[:, :, None] + latter[2] * back_scale[:, :, None],
    )


MESH = pl.DeviceIdType.MESH


def fused_kernel(
    dims, w_ref, x_ref, qg_ref, kg_ref, rope_ref, bt_ref, lens_ref, plan_s_ref, plan_ref,
    old_ref, dq_ref, nk_ref, q_out, a_out,
    wq, wk, x2, xk, xo, pt, bq, cq, eq, yq, yr, qa, po, bo, co, eo, yo, yi, qo, ro, ri,
    ss, ssin, kvp, bk, ck, ek, kvl, sendp, got, plan_pad, plans, plans_s, rope, oldv,
    over_keys, new_keys, stat, first_out, part, pstat, parts, pstats, selfs, newk, fin,
    local_sem, zs, zr, ks, kr, xy, xz_s, xz_r,
    t_s, t_r, h_s, h_r, v_s, v_r, ot_s, ot_r, oh_s, oh_r, ov_s, ov_r, oz_s, oz_r,
    tk_s, tk_r, sk_s, sk_r, pl_s, pl_r, pg_s, pg_r, ag_s, ag_r, c_s, c_r, f_s, f_r, n_s, n_r,
):
    D, G, S, T, K, F = dims
    C, fh = w_ref.shape[0], w_ref.shape[1] // G
    rows = x_ref.shape[0]
    qw = q_out.shape[1]
    kvw = kvl.shape[2]
    cr = C // K
    N = fh - F
    NQ = QL // cr
    OUT_END = NQ - LATE
    pages = rows // PAGE
    lane_rows = kvl.shape[1]
    cap_rows = sendp.shape[1]
    cap = capacity(pages, D)
    requests, heads = dq_ref.shape[0], dq_ref.shape[1]
    per = bt_ref.shape[2]
    spans = per * PAGE
    fold = requests * heads // D
    bf, f32 = jnp.bfloat16, jnp.float32
    me, g = lax.axis_index("dec"), lax.axis_index("grp")
    s, t = lax.axis_index("stg"), lax.axis_index("tp")
    lane = s * T + t
    mine_half = pl.ds(pl.multiple_of(g * fh, 128), fh)
    other_half = pl.ds(pl.multiple_of((1 - g) * fh, 128), fh)
    ends = []

    def remote(src, dst, send, recv, target):
        return pltpu.make_async_remote_copy(
            src_ref=src, dst_ref=dst, send_sem=send, recv_sem=recv,
            device_id=target, device_id_type=MESH,
        )

    def local(src, dst, i):
        copy = pltpu.make_async_copy(src, dst, local_sem.at[i])
        copy.start()
        return copy

    def when(condition, action):
        @pl.when(condition)
        def _():
            action()

    own_w = []
    for j in range(D):
        own_w.append(pltpu.make_async_copy(
            w_ref.at[:, mine_half], wq.at[j * C : (j + 1) * C], local_sem.at[0]
        ))
        when(me == j, own_w[j].start)
    x_mine = local(x_ref.at[:, mine_half], x2.at[g], 1)
    x_other = local(x_ref.at[:, other_half], xk, 2)
    kv_cut = 3 * C - QL
    wk_copies = {
        2: pltpu.make_async_copy(
            w_ref.at[C - kv_cut : C, other_half], wk.at[:kv_cut], local_sem.at[3]),
        3: pltpu.make_async_copy(w_ref.at[:, other_half], wk.at[kv_cut:], local_sem.at[3]),
    }
    for j, copy in wk_copies.items():
        when(me == j, copy.start)
    rope_copy = local(
        rope_ref.at[pl.ds(me * pages, pages),
                    pl.ds(pl.multiple_of(lane * lane_rows, 8), lane_rows)], rope, 4
    )
    old_copy = local(old_ref, oldv, 5)

    barrier = pltpu.get_barrier_semaphore()
    greeted = [{"dec": lax.rem(me + d, D)} for d in range(1, D)]
    greeted += [{"grp": 1 - g}, {"tp": 1 - t}, {"stg": 1 - s}, {"stg": 1 - s, "tp": 1 - t}]
    for target in greeted:
        pl.semaphore_signal(barrier, inc=1, device_id=target, device_id_type=MESH)
    pl.semaphore_wait(barrier, len(greeted))

    def w_rows(i, width):
        return wq.at[i * cr : (i + 1) * cr, :width]

    def z_width(i, m, way):
        return N if (m + way in (0, D - 1) and K <= i < OUT_END) else fh

    def z_copy(i, m, way):
        width = z_width(i, m, way)
        if i // K == m:
            at = (i - m * K) * cr
            src = w_ref.at[at : at + cr, pl.ds(pl.multiple_of(g * fh, 128), width)]
        else:
            src = w_rows(i, width)
        return remote(
            src, w_rows(i, width), zs.at[(way + 1) // 2, i], zr.at[i], {"dec": m + way}
        )

    def z_start(i, m, way):
        z_copy(i, m, way).start()

    def z_wait(i, m):
        way = -1 if i // K > m else 1
        z_copy_in(i, m, way).wait_recv()

    def z_copy_in(i, m, way):
        width = z_width(i, m - way, way)
        return remote(
            w_rows(i, width), w_rows(i, width), zs.at[(way + 1) // 2, i], zr.at[i],
            {"dec": m - way},
        )

    def k_rows(i):
        return (i - NQ) * cr

    def k_copy(i):
        at = k_rows(i)
        return remote(
            w_rows(i, fh), wk.at[at : at + cr], ks.at[i - NQ], kr.at[i - NQ], {"grp": 1 - g}
        )

    def sends_of(m, way):
        if not 0 <= m + way < D:
            return []
        return [
            i for i in range(D * K)
            if (i // K == m or (i // K > m if way < 0 else i // K < m))
            and not (way > 0 and i // K == D - 1) and not (way < 0 and i // K == 0)
        ]

    LM = list(range(NQ, 4 * K)) + list(range(2 * K, NQ))
    RM = list(range(K, 2 * K)) + list(range(K))
    kvn = 3 * K - NQ

    x_swap = remote(
        x_ref.at[:, other_half], x2.at[g], xy.at[0], xy.at[1], {"grp": 1 - g}
    )

    def x_arrived():
        return remote(
            x2.at[1 - g], x2.at[1 - g], xy.at[0], xy.at[1], {"grp": 1 - g}
        )

    def x_out_own(m):
        way = 1 if m == 0 else -1
        return remote(
            x_ref.at[:, pl.ds(pl.multiple_of(g * fh + N, 128), F)], xo.at[g],
            xz_s.at[0], xz_r.at[0], {"dec": m + way},
        )

    def x_out_other(m):
        way = 1 if m == 0 else -1
        return remote(
            x2.at[1 - g, :, N:], xo.at[1 - g], xz_s.at[1], xz_r.at[1], {"dec": m + way}
        )

    plan_pad[...] = jnp.full(plan_pad.shape, -1, jnp.int32)
    plan_pad[0:2, 0:pages] = plan_ref[...]
    plan_copies = []

    def start_first(m):
        def go():
            if m == 3:
                for i in range(3 * K, 4 * K):
                    z_start(i, 3, -1)
                if F:
                    x_out_own(3).start()
            if m == 2:
                for i in range(NQ, 3 * K):
                    z_start(i, 2, -1)
                    z_start(i, 2, 1)
                for i in range(2 * K, NQ):
                    z_start(i, 2, 1)
            if m == 1:
                for i in range(K, 2 * K):
                    z_start(i, 1, 1)
                    z_start(i, 1, -1)
            if m == 0:
                for i in range(K):
                    z_start(i, 0, 1)
                if F:
                    x_out_own(0).start()
        return go

    for d in range(1, D):
        copy = remote(
            plan_pad, plans.at[me], pl_s.at[d - 1], pl_r.at[d - 1], {"dec": lax.rem(me + d, D)}
        )
        copy.start()
        plan_copies.append(copy)
    plans[me] = plan_pad[...]
    for m in (3, 2, 1, 0):
        when(me == m, start_first(m))
    x_swap.start()

    def waited_at_tick(i, m):
        if i // K > m:
            return i in LM and (m > 0 or i >= NQ)
        return (i in RM and m < D - 1) or i >= NQ

    def relay(n):
        def go(m):
            def act():
                if n < len(LM):
                    i = LM[n]
                    if i // K > m and waited_at_tick(i, m):
                        z_wait(i, m)
                        if m > 0:
                            z_start(i, m, -1)
                        if i >= NQ:
                            k_copy(i).start()
                at = n + AHEAD if m == 1 else n - kvn
                if 0 <= at < len(RM):
                    i = RM[at]
                    if i // K < m and waited_at_tick(i, m):
                        z_wait(i, m)
                        z_start(i, m, 1)
                if m == D - 1 and n < 3 * K - NQ:
                    i = NQ + n
                    z_wait(i, m)
                    k_copy(i).start()
                if m == 2 and n == K:
                    for i in range(2 * K, 2 * K + LEAD):
                        z_start(i, 2, -1)
                if m == 2 and K < n < NQ - K - LEAD + 1:
                    z_start(n + K + LEAD - 1, 2, -1)
            return act
        for m in range(D):
            when(me == m, go(m))

    def lane_of(p):
        l = p[0] * cr // qw
        return l // T, l % T, p[0] * cr - l * qw

    def mul(acc_ref, at, a, b, xs, lo, hi):
        for half in range(G):
            acc_ref[at : at + b - a, half * rows : (half + 1) * rows] = lax.dot_general(
                wq[a:b, lo:hi], xs[half] if xs is not x2 else xs[half, :, lo:hi],
                (((1,), (1,)), ((), ())), preferred_element_type=f32,
            )

    def t_copy(p, out):
        a, b = p[0] * cr, p[1] * cr
        i = PIECES.index(p)
        if out:
            at = a - K * cr
            return remote(
                po.at[at : at + b - a], bo.at[at : at + b - a], ot_s.at[i], ot_r.at[i],
                {"tp": 1 - t},
            )
        return remote(pt.at[a:b], bq.at[a:b], t_s.at[i], t_r.at[i], {"tp": 1 - t})

    def h_copy(p, out):
        la = lane_of(p)[2]
        n, i = (p[1] - p[0]) * cr, PIECES.index(p)
        src, dst, send, recv = (co, eo, oh_s, oh_r) if out else (cq, eq, h_s, h_r)
        return remote(
            src.at[la : la + n], dst.at[la : la + n], send.at[i], recv.at[i], {"stg": 1 - s}
        )

    def v_copy(p, out):
        la = lane_of(p)[2]
        n, i = (p[1] - p[0]) * cr, PIECES.index(p)
        src, dst, send, recv = (yo, yi, ov_s, ov_r) if out else (yq, yr, v_s, v_r)
        return remote(
            src.at[la : la + n], dst.at[la : la + n], send.at[i], recv.at[i], {"grp": 1 - g}
        )

    def z_back(p, m):
        la = lane_of(p)[2]
        n, i = (p[1] - p[0]) * cr, PIECES.index(p)
        return remote(
            ro.at[la : la + n], ri.at[la : la + n], oz_s.at[i], oz_r.at[i],
            {"dec": 0 if m == 1 else D - 1},
        )

    def is_in(planes):
        result = me == planes[0]
        for m in planes[1:]:
            result = result | (me == m)
        return result

    def step_compute(p, planes, out):
        a, b = p[0] * cr, p[1] * cr
        sl, tl, _ = lane_of(p)
        for m in planes:
            def arrive(m=m):
                for i in range(*p):
                    if i // K != m and not out and not waited_at_tick(i, m):
                        z_wait(i, m)
            if not out and any(i // K != m and not waited_at_tick(i, m) for i in range(*p)):
                when(me == m, arrive)

        def full():
            if out:
                mul(po, a - K * cr, a, b, xo, N, fh)
            else:
                mul(pt, a, a, b, x2, 0, fh)

        def narrow():
            mul(pt, a, a, b, x2, 0, N)

        ended = tuple(m for m in planes if m in (0, D - 1))
        inner = tuple(m for m in planes if m not in (0, D - 1))
        if not out and F and K <= p[0] < OUT_END:
            if inner:
                when(is_in(inner), full)
            if ended:
                when(is_in(ended), narrow)
        else:
            when(is_in(planes), full)
        when(is_in(planes) & (t != tl), t_copy(p, out).start)

    def step_tp(p, planes, out):
        a, b = p[0] * cr, p[1] * cr
        sl, tl, la = lane_of(p)
        acc, add, to = (po, bo, co) if out else (pt, bq, cq)
        at = a - K * cr if out else a
        n = b - a

        def act():
            t_copy(p, out).wait_recv()

            @pl.when(s != sl)
            def _():
                to[la : la + n, :] = (acc[at : at + n, :] + add[at : at + n, :]).astype(bf)
                h_copy(p, out).start()

            @pl.when(s == sl)
            def _():
                acc[at : at + n, :] = acc[at : at + n, :] + add[at : at + n, :]
        when(is_in(planes) & (t == tl), act)

    def g_cols(which):
        return pl.ds(pl.multiple_of(which * rows, 128), rows)

    def step_x(p, planes, out):
        a, b = p[0] * cr, p[1] * cr
        sl, tl, la = lane_of(p)
        acc, came, keep, to = (po, eo, qo, yo) if out else (pt, eq, qa, yq)
        at = a - K * cr if out else a
        n = b - a

        def act():
            h_copy(p, out).wait_recv()
            to[la : la + n, :] = (
                acc[at : at + n, g_cols(1 - g)] + came[la : la + n, g_cols(1 - g)].astype(f32)
            ).astype(bf)
            v_copy(p, out).start()
            keep[la : la + n, :] = (
                acc[at : at + n, g_cols(g)] + came[la : la + n, g_cols(g)].astype(f32)
            )
        when(is_in(planes) & (t == tl) & (s == sl), act)

    def step_y(p, planes, out):
        sl, tl, la = lane_of(p)
        n = (p[1] - p[0]) * cr

        def act():
            v_copy(p, out).wait_recv()
            if out:
                ro[la : la + n, :] = (
                    qo[la : la + n, :] + yi[la : la + n, :].astype(f32)
                ).astype(bf)
                for m in planes:
                    when(me == m, z_back(p, m).start)
            else:
                qa[la : la + n, :] = qa[la : la + n, :] + yr[la : la + n, :].astype(f32)
        when(is_in(planes) & (t == tl) & (s == sl), act)

    def step_back(p):
        sl, tl, la = lane_of(p)
        n = (p[1] - p[0]) * cr

        def act():
            z_back(p, 1).wait_recv()
            qa[la : la + n, :] = qa[la : la + n, :] + ri[la : la + n, :].astype(f32)
        when(is_in((0, D - 1)) & (t == tl) & (s == sl), act)

    def k_lane(at):
        return pl.ds(pl.multiple_of(at * lane_rows, 8), lane_rows)

    tk, sk, pg, ag, cc, ff, small = [], [], [], [], [], [], []

    cuts = [0] + [c for c in KV_CUTS if c < kvw] + [kvw]
    kv_parts = list(zip(cuts, cuts[1:]))

    def kv_project(part):
        lo, hi = kv_parts[part]
        for i in range(NQ, D * K):
            if lo < k_rows(i) + cr <= hi or (hi < kvw and lo <= k_rows(i) < hi < k_rows(i) + cr):
                when(me != i // K, k_copy(i).wait_recv)
        for half in range(2):
            at = pl.ds(half * (rows // 2), rows // 2)
            total = lax.dot_general(
                x2[g, at, :], wq[QL + lo : QL + hi, :], (((1,), (1,)), ((), ())),
                preferred_element_type=f32,
            ) + lax.dot_general(
                xk[at, :], wk[lo:hi, :], (((1,), (1,)), ((), ())), preferred_element_type=f32
            )
            kvp[pl.ds(half * (pages // 2), pages // 2), :, lo:hi] = total.reshape(
                pages // 2, PAGE, hi - lo
            )
        for i in range(S):
            a = lax.rem(s + 1 + i, S)
            copy = remote(
                kvp.at[:, k_lane(a * T + 1 - t), lo:hi], bk.at[a, :, :, lo:hi],
                tk_s.at[part, i], tk_r.at[part, i], {"tp": 1 - t},
            )
            copy.start()
            tk.append(copy)

    def kv_across(part):
        lo, hi = kv_parts[part]
        tk[2 * part].wait_recv()
        ck[:, :, lo:hi] = (
            kvp[:, k_lane((1 - s) * T + t), lo:hi] + bk[1 - s, :, :, lo:hi]
        )
        copy = remote(
            ck.at[:, :, lo:hi], ek.at[:, :, lo:hi], sk_s.at[part], sk_r.at[part], {"stg": 1 - s}
        )
        copy.start()
        sk.append(copy)

    def kv_norm():
        for part in range(len(kv_parts)):
            tk[2 * part + 1].wait_recv()
        k = kvp[:, k_lane(lane), :] + bk[s]
        for copy in sk:
            copy.wait_recv()
        k = (k + ek[...]).reshape(pages * lane_rows, kvw)
        lat, tail = k[:, :KVL], k[:, KVL:]
        square = jnp.sum(lat * lat, axis=1, keepdims=True)
        lat = lat * (lax.rsqrt(square / KVL + norm_eps) * kg_ref[...])
        to = lax.broadcasted_iota(jnp.int32, (ROPE, ROPE), 1)
        at = lax.broadcasted_iota(jnp.int32, (ROPE, ROPE), 0)
        even = lax.rem(to, 2) == 0
        swap = jnp.where(even & (at == to + 1), -1.0, 0.0)
        swap = jnp.where(jnp.logical_not(even) & (at == to - 1), 1.0, swap)
        partner = jnp.dot(
            tail, swap, preferred_element_type=f32, precision=lax.Precision.HIGHEST
        )
        turn = rope[...].reshape(pages * lane_rows, 2 * ROPE)
        tail = tail * turn[:, :ROPE] + partner * turn[:, ROPE:]
        kvl[:, :, :KVL] = lat.reshape(pages, lane_rows, KVL)
        kvl[:, :, KVL:] = tail.reshape(pages, lane_rows, ROPE)
        for o in range(D):
            taken = [kvl[source_of(o, r)] for r in range(cap)]
            taken += [jnp.zeros((lane_rows, kvw), f32)] * (cap_rows // lane_rows - cap)
            sendp[o] = jnp.concatenate(taken, axis=0).astype(bf)
        for d in range(1, D):
            to = lax.rem(me + d, D)
            copy = remote(
                sendp.at[to], got.at[lane, me], pg_s.at[d - 1], pg_r.at[d - 1], {"dec": to}
            )
            copy.start()
            pg.append(copy)
        got[lane, me] = sendp[me]

    picked = {}

    def choose():
        owners = [plan_s_ref[0, p] for p in range(pages)]
        ranks = []
        for p in range(pages):
            rank = jnp.int32(0)
            for e in range(p):
                rank = rank + (owners[e] == owners[p]).astype(jnp.int32)
            ranks.append(rank)
        for o in range(D):
            for r in range(cap):
                found = jnp.int32(0)
                for p in range(pages):
                    found = jnp.where((owners[p] == o) & (ranks[p] == r), p, found)
                picked[o, r] = found

    def source_of(o, r):
        return picked[o, r]

    def tables():
        for copy in plan_copies:
            copy.wait_recv()
        copy = pltpu.make_async_copy(plans, plans_s, local_sem.at[6])
        copy.start()
        copy.wait()
        count = requests * per
        slots_row = jnp.full((8, 128), -1, jnp.int32)
        slots_col = jnp.full((16, 128), -1, jnp.int32)
        across = lax.broadcasted_iota(jnp.int32, (8, 128), 1)
        down = lax.broadcasted_iota(jnp.int32, (16, 128), 0)
        for d in range(D):
            rank = jnp.int32(d * cap)
            for p in range(pages):
                ours = plans_s[d, 0, p] == me
                slot = plans_s[d, 1, p]
                at = jnp.where(ours, rank, -1)
                slots_row = jnp.where(across == at, slot, slots_row)
                slots_col = jnp.where(down == at, slot, slots_col)
                rank = rank + ours.astype(jnp.int32)
        table_row = jnp.full((16, 128), -2, jnp.int32)
        table_col = jnp.full((count, 128), -2, jnp.int32)
        across16 = lax.broadcasted_iota(jnp.int32, (16, 128), 1)
        down_count = lax.broadcasted_iota(jnp.int32, (count, 128), 0)
        for k in range(count):
            slot = bt_ref[0, k // per, k % per]
            table_row = jnp.where(across16 == k, slot, table_row)
            table_col = jnp.where(down_count == k, slot, table_col)
        hit = jnp.where(table_col == slots_row[0:1], 1.0, 0.0)
        over = jnp.max(hit, axis=1, keepdims=True)
        key = lax.broadcasted_iota(jnp.int32, (count, count * PAGE), 1)
        entry = lax.broadcasted_iota(jnp.int32, (count, count * PAGE), 0)
        over = jnp.sum(jnp.where(key // PAGE == entry, over, 0.0), axis=0, keepdims=True)
        over_keys[...] = jnp.broadcast_to(over, over_keys.shape)
        place = jnp.where(slots_col == table_row, across16.astype(f32) + 1.0, 0.0)
        place = jnp.max(place, axis=1, keepdims=True)
        width = new_keys.shape[1]
        key = lax.broadcasted_iota(jnp.int32, (16, width), 1)
        entry = lax.broadcasted_iota(jnp.int32, (16, width), 0)
        inside = lax.rem(key, cap_rows)
        source = lax.rem(key // cap_rows, D)
        arrival = source * cap + inside // lane_rows
        valid = (inside // lane_rows < cap) & (arrival == entry)
        place = jnp.sum(jnp.where(valid, place, 0.0), axis=0, keepdims=True)
        new_keys[...] = jnp.broadcast_to(place, new_keys.shape)

    def old_attend(r):
        def act():
            keys = jnp.concatenate(
                [oldv[bt_ref[0, r, j]] for j in range(per)], axis=0
            )
            scores = lax.dot_general(
                dq_ref[r], keys, (((1,), (1,)), ((), ())), preferred_element_type=f32
            ) * softmax_scale
            at = lax.broadcasted_iota(jnp.int32, scores.shape, 1)
            live = (at < lens_ref[0, r]) & (
                over_keys[0:1, r * spans : (r + 1) * spans] < 0.5
            )
            scores = jnp.where(live, scores, -1e30)
            peak = jnp.max(scores, axis=1, keepdims=True)
            weight = jnp.where(live, jnp.exp(scores - peak), 0.0)
            total = jnp.sum(weight, axis=1, keepdims=True)
            mine = slice(r * heads, (r + 1) * heads)
            first_out[mine, :] = jnp.dot(
                weight.astype(bf), keys[:, :KVL], preferred_element_type=f32
            )
            column = lax.broadcasted_iota(jnp.int32, (heads, 128), 1)
            stat[mine, :] = jnp.where(column < 64, peak, total)
            query = dq_ref[r].astype(f32)
            row = nk_ref[r : r + 1, :].astype(f32)
            score = jnp.sum(query * row, axis=1, keepdims=True) * softmax_scale
            selfs[mine, :] = jnp.broadcast_to(score, (heads, 128))
            newk[mine, :] = jnp.broadcast_to(row[:, :KVL], (heads, KVL))
        return act

    def got_copy(at, which, target):
        return remote(got.at[at], got.at[at], ag_s.at[which], ag_r.at[which], target)

    def gather():
        for copy in pg:
            copy.wait_recv()
        for which, target in ((0, {"stg": 1 - s}), (1, {"tp": 1 - t})):
            copy = got_copy(lane, which, target)
            copy.start()
            ag.append(copy)

    def gather_on():
        ag[0].wait_recv()
        copy = got_copy((1 - s) * T + t, 2, {"tp": 1 - t})
        copy.start()
        ag.append(copy)

    def attend():
        ag[1].wait_recv()
        ag[2].wait_recv()
        keys = got[...].reshape(S * T * D * cap_rows, kvw)
        queries = dq_ref[...].reshape(requests * heads, kvw)
        scores = lax.dot_general(
            queries, keys, (((1,), (1,)), ((), ())), preferred_element_type=f32
        ) * softmax_scale
        place = new_keys[0:1, :].astype(jnp.int32) - 1
        at = lax.broadcasted_iota(jnp.int32, (1, scores.shape[1]), 1)
        inside = lax.rem(at, cap_rows)
        from_lane = at // (D * cap_rows)
        token = lax.rem(place, per) * PAGE + from_lane * lane_rows + lax.rem(inside, lane_rows)
        asked = jnp.where(place >= 0, place // per, -1)
        request = lax.broadcasted_iota(jnp.int32, (requests * heads, 1), 0) // heads
        length = jnp.zeros((requests * heads, 1), jnp.int32)
        for r in range(requests):
            length = jnp.where(request == r, lens_ref[0, r], length)
        live = (asked == request) & (token < length)
        scores = jnp.where(live, scores, -1e30)
        peak = stat[:, 0:1]
        peak2 = jnp.maximum(peak, jnp.max(scores, axis=1, keepdims=True))
        weight = jnp.where(live, jnp.exp(scores - peak2), 0.0)
        scale = jnp.exp(peak - peak2)
        total = jnp.sum(weight, axis=1, keepdims=True) + stat[:, 64:65] * scale
        part[...] = (
            jnp.dot(weight.astype(bf), keys[:, :KVL], preferred_element_type=f32)
            + first_out[...] * scale
        ).astype(bf)
        column = lax.broadcasted_iota(jnp.int32, pstat.shape, 1)
        pstat[...] = jnp.where(column < 64, peak2, total)
        for d in range(1, D):
            to = lax.rem(me + d, D)
            at = pl.ds(pl.multiple_of(to * fold, 16), fold)
            for which, src, dst in ((0, pstat, pstats), (1, part, parts)):
                copy = remote(
                    src.at[at], dst.at[d - 1], c_s.at[which, d - 1], c_r.at[which, d - 1],
                    {"dec": to},
                )
                copy.start()
                cc.append(copy)

    def combine():
        for copy in cc:
            copy.wait_recv()
        mine = pl.ds(pl.multiple_of(me * fold, 16), fold)
        shares = [(pstat[mine, :], part[mine, :])]
        shares += [(pstats[d], parts[d]) for d in range(D - 1)]
        own_score = selfs[mine, 0:1]
        top = own_score
        for stats, _ in shares:
            top = jnp.maximum(top, stats[:, 0:1])
        own_weight = jnp.exp(own_score - top)
        numer, denom = own_weight * newk[mine, :], own_weight
        for stats, share in shares:
            factor = jnp.exp(stats[:, 0:1] - top)
            numer = numer + factor * share.astype(f32)
            denom = denom + factor * stats[:, 64:65]
        fin[me] = (numer / denom).astype(bf)
        for d in range(1, D):
            copy = remote(
                fin.at[me], fin.at[me], f_s.at[d - 1], f_r.at[d - 1], {"dec": lax.rem(me + d, D)}
            )
            copy.start()
            ff.append(copy)

    def settle():
        for copy in ff:
            copy.wait_recv()
        for e in range(D):
            a_out[e * fold : (e + 1) * fold, :] = fin[e]

    PIECES = pieces_of(K, NQ, qw // cr)
    due = {}

    def add(tick, action, *args):
        due.setdefault(tick, []).append((action, args))

    def route(tick, p, planes, out=False):
        add(tick, step_compute, p, planes, out)
        add(tick + 1, step_tp, p, planes, out)
        add(tick + 1 + HOPX, step_x, p, planes, out)
        add(tick + 1 + HOPX + HOPY, step_y, p, planes, out)
        if out:
            add(tick + 2 + HOPX + 2 * HOPY, step_back, p)

    blocks = [[p for p in PIECES if p[0] // K == j] for j in range(3)]
    last = 2 * K

    def x_need():
        x_arrived().wait_recv()
        if F:
            for m in (0, D - 1):
                when(me == m, x_out_other(m).start)

    kv_at = KV
    for nth, (early, later) in enumerate(KV_STEPS):
        add(early, kv_project, nth)
        add(later, kv_across, nth)
    for gap, stage in zip(KV_GAPS, (kv_norm, gather, gather_on, attend, combine, settle)):
        add(kv_at + gap, stage)
    add(1, choose)
    add(3, tables)
    for r in range(requests):
        add(4 + r // 2, old_attend(r))
    add(OWN - 1, x_need)
    for j in range(3):
        for n, p in enumerate(blocks[j]):
            add_tick = OWN + n
            route(add_tick, p, (j,))
    for p in blocks[1]:
        done = p[1] - K - 1
        route(max(done + 2, OWN + 3), p, (2, 3))
        route(OWN + 4 + blocks[1].index(p), p, (0,))
    for p in blocks[0]:
        route(K + p[1] - 1 - AHEAD, p, (1,))
        route(K + p[1] - 1 + kvn, p, (2,))
        route(K + p[1] - 1 + kvn + 2, p, (3,))
    for n, p in enumerate(blocks[2]):
        route(OWN + 5 + n, p, (3,))
        route(K + (3 * K - NQ) + p[1] - 2 * K - 1, p, (0, 1))
    if F:
        def xo_need():
            when(is_in((1, 2)), lambda: x_wait_in())
        add(OUT - 1, xo_need)
        for n, p in enumerate(p for p in PIECES if K <= p[0] < OUT_END):
            there = K + (3 * K - NQ) + p[1] - 2 * K - 1
            route(max(OUT + n // 2, there), p, (1, 2), True)

    def x_wait_in():
        for half in range(2):
            remote(
                xo.at[half], xo.at[half], xz_s.at[0], xz_r.at[half], {"grp": 1 - g}
            ).wait_recv()

    for j in range(D):
        if j in wk_copies:
            when(me == j, wk_copies[j].wait)
    x_mine.wait()
    x_other.wait()
    rope_copy.wait()
    old_copy.wait()
    for j in range(D):
        when(me == j, own_w[j].wait)

    for n in range(max(list(due) + [2 * K]) + 1):
        if n <= 2 * K:
            relay(n)
        for action, args in due.get(n, ()):
            action(*args)

    q = qa[...]
    ss[...] = jnp.broadcast_to(jnp.sum(q * q, axis=0, keepdims=True), ss.shape)
    for i, target in enumerate(({"tp": 1 - t}, {"stg": 1 - s}, {"stg": 1 - s, "tp": 1 - t})):
        copy = remote(ss, ssin.at[i], n_s.at[i], n_r.at[i], target)
        copy.start()
        small.append(copy)
    gain = qg_ref[pl.ds(pl.multiple_of(lane * qw, 128), qw)].reshape(1, qw)
    turned = jnp.transpose(q) * gain
    square = ss[...]
    for i, copy in enumerate(small):
        copy.wait_recv()
        square = square + ssin[i]
    inverse = jnp.transpose(lax.rsqrt(square / QL + norm_eps))
    q_out[...] = (turned * inverse[:, 0:1]).astype(bf)

    for copy in [x_swap] + plan_copies + tk + sk + pg + ag + cc + ff + small:
        copy.wait_send()
    for m in range(D):
        def left(m=m):
            for way in (-1, 1):
                for i in sends_of(m, way):
                    z_copy(i, m, way).wait_send()
            for i in range(NQ, D * K):
                if i // K != m:
                    k_copy(i).wait_send()
            if F and m in (0, D - 1):
                x_out_own(m).wait_send()
                x_out_other(m).wait_send()
        when(me == m, left)
    for p in PIECES:
        sl, tl, _ = lane_of(p)
        for out in ((False, True) if F and K <= p[0] < OUT_END else (False,)):
            inside = is_in((1, 2)) if out else is_in(tuple(range(D)))
            when(inside & (t != tl), t_copy(p, out).wait_send)
            when(inside & (t == tl) & (s != sl), h_copy(p, out).wait_send)
            when(inside & (t == tl) & (s == sl), v_copy(p, out).wait_send)
            if out:
                when(inside & (t == tl) & (s == sl), z_back(p, 1).wait_send)


def hand_over_kernel(q_ref, a_ref, q_out, a_out):
    q_out[...] = q_ref[...]
    a_out[...] = a_ref[...]


def capacity(pages, owners):
    return max(2, -(-pages // owners))


def chunk_count(rows):
    return next((k for k in (11, 3, 2) if rows % (16 * k) == 0), 1)


def pieces_of(K, NQ, lane_chunks):
    cuts = set(range(0, NQ + 1, lane_chunks)) | set(range(0, NQ, K)) | {NQ}
    cuts = sorted(cuts | {NQ - c for c in MORE})
    pieces = []
    for a, b in zip(cuts, cuts[1:]):
        parts = -(-(b - a) // LONGEST)
        ends = [a + (b - a) * i // parts for i in range(parts + 1)]
        pieces += list(zip(ends, ends[1:]))
    return pieces


OWN, OUT, HOPX, HOPY = 8, 19, 6, 4
KV, KV_GAPS = 21, (0, 3, 5, 6, 10, 13)
KV_CUTS, KV_STEPS = (384,), ((15, 16), (18, 19))
LONGEST, MORE = 6, ()
LATE = 10
LEAD = 10
AHEAD = 3
SHARE = 5


def fused_ok(hidden_x, proj_weight, old_cache, dec_query, page_plan, block_table):
    D, G, S, T = [lax.axis_size(n) for n in ("dec", "grp", "stg", "tp")]
    if (D, G, S, T) != (4, 2, 2, 2):
        return False
    rows, features = hidden_x.shape
    C = proj_weight.shape[1]
    K = chunk_count(C)
    cr, qw, lane_rows = C // K, QL // (S * T), PAGE // (S * T)
    pages = page_plan.shape[0]
    return (
        cr % 16 == 0
        and D * C == QL + KVL + ROPE
        and qw % cr == 0
        and qw % 128 == 0
        and 2 * C < QL < 3 * C
        and features % (128 * 7 * G) == 0
        and rows == pages * PAGE
        and rows % 128 == 0
        and pages % 2 == 0
        and lane_rows % 8 == 0
        and D * capacity(pages, D) <= 16
        and block_table.shape[1] * block_table.shape[2] <= 128
        and block_table.shape[1] == D
        and dec_query.shape[0] == D
        and dec_query.shape[1] % 16 == 0
    )


def fused(
    hidden_x, proj_weight, q_gain, kv_gain, old_cache, page_plan, block_table, split_lens,
    dec_query, new_key,
):
    D, G, S, T = [lax.axis_size(n) for n in ("dec", "grp", "stg", "tp")]
    L = S * T
    rows, features = hidden_x.shape
    C = proj_weight.shape[1]
    K = chunk_count(C)
    fh, qw, kvw = features // G, QL // L, KVL + ROPE
    F = fh * SHARE // 7
    cr, NQ = C // K, QL // (C // K)
    lane_rows = PAGE // L
    pages = page_plan.shape[0]
    cap = capacity(pages, D)
    cap_rows = -(-cap * lane_rows // 16) * 16
    requests, heads = dec_query.shape[0], dec_query.shape[1]
    width = block_table.shape[2]
    fold = requests * heads // D

    positions = np.arange(D * rows, dtype=np.float32)
    pair_index = np.arange(ROPE, dtype=np.int32) // 2
    frequency = np.power(np.float32(10000.0), -(2 * pair_index).astype(np.float32) / np.float32(ROPE))
    angles = positions[:, None] * frequency.astype(np.float32)[None, :]
    rope = np.concatenate([np.cos(angles), np.sin(angles)], axis=1).astype(np.float32)
    rope = jnp.asarray(rope.reshape(D * pages, PAGE, 2 * ROPE))

    dma = pltpu.SemaphoreType.DMA
    bf, f32, i32 = jnp.bfloat16, jnp.float32, jnp.int32
    vmem = pl.BlockSpec(memory_space=pltpu.VMEM)
    smem = pl.BlockSpec(memory_space=pltpu.SMEM)
    hbm = pl.BlockSpec(memory_space=pl.ANY)
    kn = len(KV_STEPS)
    n = len(pieces_of(K, NQ, qw // cr))
    both = G * rows
    outs = (NQ - K) * cr if F else 16
    qo_rows = qw if F else 16
    V = pltpu.VMEM
    q_out, a_out = pl.pallas_call(
        functools.partial(fused_kernel, (D, G, S, T, K, F)),
        out_shape=(
            jax.ShapeDtypeStruct((rows, qw), bf),
            jax.ShapeDtypeStruct((requests * heads, KVL), bf),
        ),
        in_specs=[hbm, hbm, vmem, vmem, hbm, smem, smem, smem, vmem, hbm, vmem, vmem],
        out_specs=(vmem, vmem),
        scratch_shapes=[
            V((D * C, fh), bf), V((kvw, fh), bf), V((G, rows, fh), bf), V((rows, fh), bf),
            V((G, rows, max(F, 128)), bf),
            V((QL, both), f32), V((QL, both), f32), V((qw, both), bf), V((qw, both), bf),
            V((qw, rows), bf), V((qw, rows), bf), V((qw, rows), f32),
            V((outs, both), f32), V((outs, both), f32), V((qo_rows, both), bf), V((qo_rows, both), bf),
            V((qo_rows, rows), bf), V((qo_rows, rows), bf), V((qo_rows, rows), f32),
            V((qo_rows, rows), bf), V((qo_rows, rows), bf),
            V((8, rows), f32), V((L - 1, 8, rows), f32),
            V((pages, PAGE, kvw), f32), V((S, pages, lane_rows, kvw), f32),
            V((pages, lane_rows, kvw), f32), V((pages, lane_rows, kvw), f32),
            V((pages, lane_rows, kvw), f32),
            V((D, cap_rows, kvw), bf), V((L, D, cap_rows, kvw), bf),
            V((8, 128), i32), V((D, 8, 128), i32), pltpu.SMEM((D, 8, 128), i32),
            V((pages, lane_rows, 2 * ROPE), f32), V(old_cache.shape, bf),
            V((8, requests * width * PAGE), f32), V((8, L * D * cap_rows), f32),
            V((requests * heads, 128), f32), V((requests * heads, KVL), f32),
            V((requests * heads, KVL), bf), V((requests * heads, 128), f32),
            V((D - 1, fold, KVL), bf), V((D - 1, fold, 128), f32),
            V((requests * heads, 128), f32), V((requests * heads, KVL), f32),
            V((D, fold, KVL), bf),
            dma((7,)), dma((2, D * K)), dma((D * K,)), dma((D * K - NQ,)), dma((D * K - NQ,)),
            dma((2,)), dma((2,)), dma((2,)),
            dma((n,)), dma((n,)), dma((n,)), dma((n,)), dma((n,)), dma((n,)),
            dma((n,)), dma((n,)), dma((n,)), dma((n,)), dma((n,)), dma((n,)), dma((n,)), dma((n,)),
            dma((kn, S)), dma((kn, S)), dma((kn,)), dma((kn,)), dma((D - 1,)), dma((D - 1,)),
            dma((D - 1,)), dma((D - 1,)), dma((3,)), dma((3,)),
            dma((2, D - 1)), dma((2, D - 1)), dma((D - 1,)), dma((D - 1,)), dma((3,)), dma((3,)),
        ],
        compiler_params=pltpu.CompilerParams(
            collective_id=0, has_side_effects=True, vmem_limit_bytes=60 * 1024 * 1024
        ),
    )(
        proj_weight.T, hidden_x, q_gain, kv_gain[None, :], rope, block_table, split_lens.T,
        page_plan.T, page_plan.T, old_cache, dec_query, new_key,
    )
    return pl.pallas_call(
        hand_over_kernel,
        out_shape=(
            jax.ShapeDtypeStruct((rows, qw), bf),
            jax.ShapeDtypeStruct((requests, heads, KVL), bf),
        ),
        in_specs=[vmem, vmem],
        out_specs=(vmem, vmem),
    )(q_out, a_out.reshape(requests, heads, KVL))


def body(
    hidden_x,
    proj_weight,
    q_gain,
    kv_gain,
    old_cache,
    page_plan,
    block_table,
    split_lens,
    dec_query,
    new_key,
):
    if fused_ok(hidden_x, proj_weight, old_cache, dec_query, page_plan, block_table):
        return fused(
            hidden_x, proj_weight, q_gain, kv_gain, old_cache, page_plan, block_table,
            split_lens, dec_query, new_key,
        )
    projected = jnp.dot(
        hidden_x,
        lax.all_gather(proj_weight, "dec", axis=1, tiled=True),
        preferred_element_type=jnp.float32,
    )
    query_part = projected[:, :QL]
    kv_part = projected[:, QL:]
    tokens_here = hidden_x.shape[0]
    positions = (
        lax.axis_index("dec") * tokens_here + jnp.arange(tokens_here, dtype=jnp.int32)
    ).astype(jnp.float32)
    lane_count = lax.axis_size(("stg", "tp"))
    lane_index = lax.axis_index(("stg", "tp"))
    owner_count = lax.axis_size("dec")
    page_count = page_plan.shape[0]
    capacity = max(2, -(-page_count // owner_count))
    query_width = QL // lane_count
    query_cols, kv_cols = (
        lax.psum_scatter(query_part, ("stg", "tp"), scatter_dimension=1, tiled=True),
        lax.psum_scatter(kv_part, ("stg", "tp"), scatter_dimension=1, tiled=True),
    )
    kv_width = kv_cols.shape[1]
    col_start = lane_index * kv_width
    columns = col_start + jnp.arange(kv_width, dtype=jnp.int32)
    latent_part_sq = jnp.sum(jnp.where(columns[None, :] < KVL, kv_cols * kv_cols, 0.0), axis=1)
    query_sq, latent_sq = lax.psum(
        (jnp.sum(query_cols * query_cols, axis=1), latent_part_sq), ("stg", "tp")
    )
    kv_rows = kv_finish(kv_cols, col_start, latent_sq, kv_gain, positions)
    kv_pages = kv_rows.reshape(page_count, PAGE, kv_width)
    send_pages, send_labels = pack_pages(kv_pages, page_plan, owner_count, capacity)
    got_slices, got_labels = (
        lax.all_to_all(send_pages, "dec", split_axis=0, concat_axis=0, tiled=True),
        lax.all_to_all(send_labels, "dec", split_axis=0, concat_axis=0, tiled=True),
    )
    got_pages = lax.all_gather(got_slices, ("stg", "tp"), axis=3, tiled=True)
    query_gain = lax.dynamic_slice_in_dim(q_gain, lane_index * query_width, query_width)
    q_latent = (
        query_cols * lax.rsqrt(query_sq / QL + norm_eps)[:, None] * query_gain[None, :]
    ).astype(jnp.bfloat16)
    cache = place_pages(old_cache, got_pages, got_labels)
    slot_table = block_table[0]
    request_count = slot_table.shape[0]
    key_rows = take_each(cache, slot_table.reshape(-1)).reshape(
        request_count, -1, cache.shape[2]
    )
    scores = (
        jnp.einsum("rhc,rlc->rhl", dec_query, key_rows, preferred_element_type=jnp.float32)
        * softmax_scale
    )
    live_mask = jnp.arange(key_rows.shape[1], dtype=jnp.int32)[None, :] < split_lens[:, 0][:, None]
    scores = jnp.where(live_mask[:, None, :], scores, -1e30)
    row_peak = jnp.max(scores, axis=2)
    weights = jnp.where(live_mask[:, None, :], jnp.exp(scores - row_peak[:, :, None]), 0.0)
    row_total = jnp.sum(weights, axis=2)
    rounded = weights.astype(jnp.bfloat16)
    partial_out = jnp.einsum(
        "rhl,rlc->rhc", rounded, key_rows[:, :, :KVL], preferred_element_type=jnp.float32
    )
    peak_all, total_all, output_all = combined_all(
        (row_peak, row_total, partial_out), "dec", combine_parts
    )
    self_score = (
        jnp.einsum("rhc,rc->rh", dec_query, new_key, preferred_element_type=jnp.float32)
        * softmax_scale
    )
    overall = jnp.maximum(peak_all, self_score)
    carried = jnp.exp(peak_all - overall)
    self_weight = jnp.exp(self_score - overall)
    denom = total_all * carried + self_weight
    numer = output_all * carried[:, :, None] + self_weight[:, :, None] * new_key[
        :, None, :KVL
    ].astype(jnp.float32)
    attn_latent = (numer / denom[:, :, None]).astype(jnp.bfloat16)
    return (q_latent, attn_latent)


def solution(mesh):
    return jax.shard_map(
        body,
        mesh=mesh,
        in_specs=(
            P(("grp", "dec"), ("stg", "tp")),
            P(("stg", "tp"), "dec"),
            P(),
            P(),
            P(("grp", "dec"), None, None),
            P(("grp", "dec"), None),
            P(("grp", "dec"), None, None),
            P("grp", "dec"),
            P("grp", ("stg", "tp"), None),
            P("grp", None),
        ),
        out_specs=(P(("grp", "dec"), ("stg", "tp")), P("grp", ("stg", "tp"), None)),
        check_vma=False,
    )
```

```python
import functools

import jax
import jax.numpy as jnp
import numpy as np
from jax import lax
from jax.experimental import pallas as pl
from jax.experimental.pallas import tpu as pltpu
from jax.sharding import PartitionSpec as P

QL = 1536
KVL = 512
ROPE = 64
PAGE = 32


softmax_scale = 192.0 ** (-0.5)
norm_eps = 1e-06


def combined_all(part, axis, combine):
    gathered = jax.tree.map(lambda a: lax.all_gather(a, axis), part)

    def take(source):
        return jax.tree.map(lambda a: lax.dynamic_index_in_dim(a, source, 0, False), gathered)

    return lax.fori_loop(
        1, lax.axis_size(axis), lambda source, state: combine(state, take(source)), take(0)
    )


def rope_rotate(matrix, col_start, positions):
    col_count = matrix.shape[1]
    columns = col_start + jnp.arange(col_count, dtype=jnp.int32)
    is_rope = columns >= KVL
    pair_index = jnp.maximum(columns - KVL, 0) // 2
    frequency = jnp.power(jnp.float32(10000.0), -(2 * pair_index).astype(jnp.float32) / ROPE)
    angles = positions[:, None] * frequency[None, :]
    cosine = jnp.where(is_rope[None, :], jnp.cos(angles), 1.0)
    sine_part = jnp.where(is_rope[None, :], jnp.sin(angles), 0.0)
    paired = matrix.reshape(matrix.shape[0], col_count // 2, 2)
    partner = jnp.stack([-paired[:, :, 1], paired[:, :, 0]], axis=2).reshape(matrix.shape)
    return matrix * cosine + partner * sine_part


def kv_finish(matrix, col_start, latent_sq, kv_gain, positions):
    col_count = matrix.shape[1]
    columns = col_start + jnp.arange(col_count, dtype=jnp.int32)
    gain_full = jnp.concatenate([kv_gain, jnp.ones((ROPE,), jnp.float32)])
    gain_cols = lax.dynamic_slice_in_dim(gain_full, col_start, col_count)
    inverse = lax.rsqrt(latent_sq / KVL + norm_eps)
    row_scale = jnp.where(columns[None, :] < KVL, inverse[:, None] * gain_cols[None, :], 1.0)
    return rope_rotate(matrix * row_scale, col_start, positions).astype(jnp.bfloat16)


def take_each(array, ids):
    return lax.map(lambda i: lax.dynamic_index_in_dim(array, i, 0, False), ids)


def pack_pages(kv_pages, page_table, owner_count, capacity):
    owners = page_table[:, 0]
    slot_ids = page_table[:, 1]
    page_ids = jnp.arange(kv_pages.shape[0], dtype=jnp.int32)
    earlier = (owners[:, None] == owners[None, :]) & (page_ids[None, :] < page_ids[:, None])
    ranking = jnp.sum(earlier.astype(jnp.int32), axis=1)
    targets = owners * capacity + ranking
    places = jnp.arange(owner_count * capacity, dtype=jnp.int32)
    matches = targets[None, :] == places[:, None]
    source_ids = jnp.sum(jnp.where(matches, page_ids[None, :], 0), axis=1)
    filled = jnp.any(matches, axis=1)
    chosen = jnp.where(
        filled[:, None, None], take_each(kv_pages, source_ids), jnp.zeros((), kv_pages.dtype)
    )
    labels = jnp.where(filled, jnp.take(slot_ids, source_ids), -1).astype(jnp.bfloat16)
    return (
        chosen.reshape(owner_count, capacity, kv_pages.shape[1], kv_pages.shape[2]),
        labels.reshape(owner_count, capacity),
    )


def place_pages(old_cache, got_pages, got_labels):
    flat_pages = got_pages.reshape(-1, old_cache.shape[1], old_cache.shape[2])
    label_ids = got_labels.reshape(-1).astype(jnp.int32)
    slot_ids = jnp.arange(old_cache.shape[0], dtype=jnp.int32)
    arrival_ids = jnp.arange(label_ids.shape[0], dtype=jnp.int32)
    matches = label_ids[None, :] == slot_ids[:, None]
    source_ids = jnp.sum(jnp.where(matches, arrival_ids[None, :], 0), axis=1)
    arrived = jnp.any(matches, axis=1)
    return jnp.where(arrived[:, None, None], take_each(flat_pages, source_ids), old_cache)


def combine_parts(former, latter):
    overall = jnp.maximum(former[0], latter[0])
    front_scale = jnp.exp(former[0] - overall)
    back_scale = jnp.exp(latter[0] - overall)
    return (
        overall,
        former[1] * front_scale + latter[1] * back_scale,
        former[2] * front_scale[:, :, None] + latter[2] * back_scale[:, :, None],
    )


MESH = pl.DeviceIdType.MESH


def fused_kernel(
    dims, w_ref, x_ref, qg_ref, kg_ref, rope_ref, bt_ref, lens_ref, plan_s_ref, plan_ref,
    old_ref, dq_ref, nk_ref, q_out, a_out,
    wq, wk, x2, xk, xo, pt, bq, cq, eq, yq, yr, qa, po, bo, co, eo, yo, yi, qo, ro, ri,
    ss, ssin, kvp, bk, ck, ek, kvl, sendp, got, plan_pad, plans, plans_s, rope, oldv,
    over_keys, new_keys, stat, first_out, part, pstat, parts, pstats, selfs, newk, fin,
    local_sem, zs, zr, ks, kr, xy, xz_s, xz_r,
    t_s, t_r, h_s, h_r, v_s, v_r, ot_s, ot_r, oh_s, oh_r, ov_s, ov_r, oz_s, oz_r,
    tk_s, tk_r, sk_s, sk_r, pl_s, pl_r, pg_s, pg_r, ag_s, ag_r, c_s, c_r, f_s, f_r, n_s, n_r,
):
    D, G, S, T, K, F = dims
    C, fh = w_ref.shape[0], w_ref.shape[1] // G
    rows = x_ref.shape[0]
    qw = q_out.shape[1]
    kvw = kvl.shape[2]
    cr = C // K
    N = fh - F
    NQ = QL // cr
    OUT_END = NQ - LATE
    pages = rows // PAGE
    lane_rows = kvl.shape[1]
    cap_rows = sendp.shape[1]
    cap = capacity(pages, D)
    requests, heads = dq_ref.shape[0], dq_ref.shape[1]
    per = bt_ref.shape[2]
    spans = per * PAGE
    fold = requests * heads // D
    bf, f32 = jnp.bfloat16, jnp.float32
    me, g = lax.axis_index("dec"), lax.axis_index("grp")
    s, t = lax.axis_index("stg"), lax.axis_index("tp")
    lane = s * T + t
    mine_half = pl.ds(pl.multiple_of(g * fh, 128), fh)
    other_half = pl.ds(pl.multiple_of((1 - g) * fh, 128), fh)
    ends = []

    def remote(src, dst, send, recv, target):
        return pltpu.make_async_remote_copy(
            src_ref=src, dst_ref=dst, send_sem=send, recv_sem=recv,
            device_id=target, device_id_type=MESH,
        )

    def local(src, dst, i):
        copy = pltpu.make_async_copy(src, dst, local_sem.at[i])
        copy.start()
        return copy

    def when(condition, action):
        @pl.when(condition)
        def _():
            action()

    own_w = []
    for j in range(D):
        own_w.append(pltpu.make_async_copy(
            w_ref.at[:, mine_half], wq.at[j * C : (j + 1) * C], local_sem.at[0]
        ))
        when(me == j, own_w[j].start)
    x_mine = local(x_ref.at[:, mine_half], x2.at[g], 1)
    x_other = local(x_ref.at[:, other_half], xk, 2)
    kv_cut = 3 * C - QL
    wk_copies = {
        2: pltpu.make_async_copy(
            w_ref.at[C - kv_cut : C, other_half], wk.at[:kv_cut], local_sem.at[3]),
        3: pltpu.make_async_copy(w_ref.at[:, other_half], wk.at[kv_cut:], local_sem.at[3]),
    }
    for j, copy in wk_copies.items():
        when(me == j, copy.start)
    rope_copy = local(
        rope_ref.at[pl.ds(me * pages, pages),
                    pl.ds(pl.multiple_of(lane * lane_rows, 8), lane_rows)], rope, 4
    )
    old_copy = local(old_ref, oldv, 5)

    barrier = pltpu.get_barrier_semaphore()
    greeted = [{"dec": lax.rem(me + d, D)} for d in range(1, D)]
    greeted += [{"dec": lax.rem(me + d, D), "stg": 1 - s} for d in range(1, D)]
    greeted += [{"grp": 1 - g}, {"tp": 1 - t}, {"stg": 1 - s}, {"stg": 1 - s, "tp": 1 - t}]
    for target in greeted:
        pl.semaphore_signal(barrier, inc=1, device_id=target, device_id_type=MESH)
    pl.semaphore_wait(barrier, len(greeted))

    def w_rows(i, width):
        return wq.at[i * cr : (i + 1) * cr, :width]

    def z_width(i, m, way):
        return N if (m + way in (0, D - 1) and K <= i < OUT_END) else fh

    def z_copy(i, m, way):
        width = z_width(i, m, way)
        if i // K == m:
            at = (i - m * K) * cr
            src = w_ref.at[at : at + cr, pl.ds(pl.multiple_of(g * fh, 128), width)]
        else:
            src = w_rows(i, width)
        return remote(
            src, w_rows(i, width), zs.at[(way + 1) // 2, i], zr.at[i], {"dec": m + way}
        )

    def z_start(i, m, way):
        z_copy(i, m, way).start()

    def z_wait(i, m):
        way = -1 if i // K > m else 1
        z_copy_in(i, m, way).wait_recv()

    def z_copy_in(i, m, way):
        width = z_width(i, m - way, way)
        return remote(
            w_rows(i, width), w_rows(i, width), zs.at[(way + 1) // 2, i], zr.at[i],
            {"dec": m - way},
        )

    def k_rows(i):
        return (i - NQ) * cr

    def k_copy(i):
        at = k_rows(i)
        return remote(
            w_rows(i, fh), wk.at[at : at + cr], ks.at[i - NQ], kr.at[i - NQ], {"grp": 1 - g}
        )

    def sends_of(m, way):
        if not 0 <= m + way < D:
            return []
        return [
            i for i in range(D * K)
            if (i // K == m or (i // K > m if way < 0 else i // K < m))
            and not (way > 0 and i // K == D - 1) and not (way < 0 and i // K == 0)
        ]

    LM = list(range(NQ, 4 * K)) + list(range(2 * K, NQ))
    RM = list(range(K, 2 * K)) + list(range(K))
    kvn = 3 * K - NQ

    x_swap = remote(
        x_ref.at[:, other_half], x2.at[g], xy.at[0], xy.at[1], {"grp": 1 - g}
    )

    def x_arrived():
        return remote(
            x2.at[1 - g], x2.at[1 - g], xy.at[0], xy.at[1], {"grp": 1 - g}
        )

    def x_out_own(m):
        way = 1 if m == 0 else -1
        return remote(
            x_ref.at[:, pl.ds(pl.multiple_of(g * fh + N, 128), F)], xo.at[g],
            xz_s.at[0], xz_r.at[0], {"dec": m + way},
        )

    def x_out_other(m):
        way = 1 if m == 0 else -1
        return remote(
            x2.at[1 - g, :, N:], xo.at[1 - g], xz_s.at[1], xz_r.at[1], {"dec": m + way}
        )

    plan_pad[...] = jnp.full(plan_pad.shape, -1, jnp.int32)
    plan_pad[0:2, 0:pages] = plan_ref[...]
    plan_copies = []

    def start_first(m):
        def go():
            if m == 3:
                for i in range(3 * K, 4 * K):
                    z_start(i, 3, -1)
                if F:
                    x_out_own(3).start()
            if m == 2:
                for i in range(NQ, 3 * K):
                    z_start(i, 2, -1)
                    z_start(i, 2, 1)
                for i in range(2 * K, NQ):
                    z_start(i, 2, 1)
            if m == 1:
                for i in range(K, 2 * K):
                    z_start(i, 1, 1)
                    z_start(i, 1, -1)
            if m == 0:
                for i in range(K):
                    z_start(i, 0, 1)
                if F:
                    x_out_own(0).start()
        return go

    for d in range(1, D):
        copy = remote(
            plan_pad, plans.at[me], pl_s.at[d - 1], pl_r.at[d - 1], {"dec": lax.rem(me + d, D)}
        )
        copy.start()
        plan_copies.append(copy)
    plans[me] = plan_pad[...]
    for m in (3, 2, 1, 0):
        when(me == m, start_first(m))
    x_swap.start()

    def waited_at_tick(i, m):
        if i // K > m:
            return i in LM and (m > 0 or i >= NQ)
        return (i in RM and m < D - 1) or i >= NQ

    def relay(n):
        def go(m):
            def act():
                if n < len(LM):
                    i = LM[n]
                    if i // K > m and waited_at_tick(i, m):
                        z_wait(i, m)
                        if m > 0:
                            z_start(i, m, -1)
                        if i >= NQ:
                            k_copy(i).start()
                at = n + AHEAD if m == 1 else n - kvn
                if 0 <= at < len(RM):
                    i = RM[at]
                    if i // K < m and waited_at_tick(i, m):
                        z_wait(i, m)
                        z_start(i, m, 1)
                if m == D - 1 and n < 3 * K - NQ:
                    i = NQ + n
                    z_wait(i, m)
                    k_copy(i).start()
                if m == 2 and n == K:
                    for i in range(2 * K, 2 * K + LEAD):
                        z_start(i, 2, -1)
                if m == 2 and K < n < NQ - K - LEAD + 1:
                    z_start(n + K + LEAD - 1, 2, -1)
            return act
        for m in range(D):
            when(me == m, go(m))

    def lane_of(p):
        l = p[0] * cr // qw
        return l // T, l % T, p[0] * cr - l * qw

    def mul(acc_ref, at, a, b, xs, lo, hi):
        for half in range(G):
            acc_ref[at : at + b - a, half * rows : (half + 1) * rows] = lax.dot_general(
                wq[a:b, lo:hi], xs[half] if xs is not x2 else xs[half, :, lo:hi],
                (((1,), (1,)), ((), ())), preferred_element_type=f32,
            )

    def t_copy(p, out):
        a, b = p[0] * cr, p[1] * cr
        i = PIECES.index(p)
        if out:
            at = a - K * cr
            return remote(
                po.at[at : at + b - a], bo.at[at : at + b - a], ot_s.at[i], ot_r.at[i],
                {"tp": 1 - t},
            )
        return remote(pt.at[a:b], bq.at[a:b], t_s.at[i], t_r.at[i], {"tp": 1 - t})

    def h_copy(p, out):
        la = lane_of(p)[2]
        n, i = (p[1] - p[0]) * cr, PIECES.index(p)
        src, dst, send, recv = (co, eo, oh_s, oh_r) if out else (cq, eq, h_s, h_r)
        return remote(
            src.at[la : la + n], dst.at[la : la + n], send.at[i], recv.at[i], {"stg": 1 - s}
        )

    def v_copy(p, out):
        la = lane_of(p)[2]
        n, i = (p[1] - p[0]) * cr, PIECES.index(p)
        src, dst, send, recv = (yo, yi, ov_s, ov_r) if out else (yq, yr, v_s, v_r)
        return remote(
            src.at[la : la + n], dst.at[la : la + n], send.at[i], recv.at[i], {"grp": 1 - g}
        )

    def z_back(p, m):
        la = lane_of(p)[2]
        n, i = (p[1] - p[0]) * cr, PIECES.index(p)
        return remote(
            ro.at[la : la + n], ri.at[la : la + n], oz_s.at[i], oz_r.at[i],
            {"dec": 0 if m == 1 else D - 1},
        )

    def is_in(planes):
        result = me == planes[0]
        for m in planes[1:]:
            result = result | (me == m)
        return result

    def step_compute(p, planes, out):
        a, b = p[0] * cr, p[1] * cr
        sl, tl, _ = lane_of(p)
        for m in planes:
            def arrive(m=m):
                for i in range(*p):
                    if i // K != m and not out and not waited_at_tick(i, m):
                        z_wait(i, m)
            if not out and any(i // K != m and not waited_at_tick(i, m) for i in range(*p)):
                when(me == m, arrive)

        def full():
            if out:
                mul(po, a - K * cr, a, b, xo, N, fh)
            else:
                mul(pt, a, a, b, x2, 0, fh)

        def narrow():
            mul(pt, a, a, b, x2, 0, N)

        ended = tuple(m for m in planes if m in (0, D - 1))
        inner = tuple(m for m in planes if m not in (0, D - 1))
        if not out and F and K <= p[0] < OUT_END:
            if inner:
                when(is_in(inner), full)
            if ended:
                when(is_in(ended), narrow)
        else:
            when(is_in(planes), full)
        when(is_in(planes) & (t != tl), t_copy(p, out).start)

    def step_tp(p, planes, out):
        a, b = p[0] * cr, p[1] * cr
        sl, tl, la = lane_of(p)
        acc, add, to = (po, bo, co) if out else (pt, bq, cq)
        at = a - K * cr if out else a
        n = b - a

        def act():
            t_copy(p, out).wait_recv()

            @pl.when(s != sl)
            def _():
                to[la : la + n, :] = (acc[at : at + n, :] + add[at : at + n, :]).astype(bf)
                h_copy(p, out).start()

            @pl.when(s == sl)
            def _():
                acc[at : at + n, :] = acc[at : at + n, :] + add[at : at + n, :]
        when(is_in(planes) & (t == tl), act)

    def g_cols(which):
        return pl.ds(pl.multiple_of(which * rows, 128), rows)

    def step_x(p, planes, out):
        a, b = p[0] * cr, p[1] * cr
        sl, tl, la = lane_of(p)
        acc, came, keep, to = (po, eo, qo, yo) if out else (pt, eq, qa, yq)
        at = a - K * cr if out else a
        n = b - a

        def act():
            h_copy(p, out).wait_recv()
            to[la : la + n, :] = (
                acc[at : at + n, g_cols(1 - g)] + came[la : la + n, g_cols(1 - g)].astype(f32)
            ).astype(bf)
            v_copy(p, out).start()
            keep[la : la + n, :] = (
                acc[at : at + n, g_cols(g)] + came[la : la + n, g_cols(g)].astype(f32)
            )
        when(is_in(planes) & (t == tl) & (s == sl), act)

    def step_y(p, planes, out):
        sl, tl, la = lane_of(p)
        n = (p[1] - p[0]) * cr

        def act():
            v_copy(p, out).wait_recv()
            if out:
                ro[la : la + n, :] = (
                    qo[la : la + n, :] + yi[la : la + n, :].astype(f32)
                ).astype(bf)
                for m in planes:
                    when(me == m, z_back(p, m).start)
            else:
                qa[la : la + n, :] = qa[la : la + n, :] + yr[la : la + n, :].astype(f32)
        when(is_in(planes) & (t == tl) & (s == sl), act)

    def step_back(p):
        sl, tl, la = lane_of(p)
        n = (p[1] - p[0]) * cr

        def act():
            z_back(p, 1).wait_recv()
            qa[la : la + n, :] = qa[la : la + n, :] + ri[la : la + n, :].astype(f32)
        when(is_in((0, D - 1)) & (t == tl) & (s == sl), act)

    def k_lane(at):
        return pl.ds(pl.multiple_of(at * lane_rows, 8), lane_rows)

    tk, sk, pg, ag, cc, ff, small = [], [], [], [], [], [], []

    cuts = [0] + [c for c in KV_CUTS if c < kvw] + [kvw]
    kv_parts = list(zip(cuts, cuts[1:]))

    def kv_project(part):
        lo, hi = kv_parts[part]
        for i in range(NQ, D * K):
            if lo < k_rows(i) + cr <= hi or (hi < kvw and lo <= k_rows(i) < hi < k_rows(i) + cr):
                when(me != i // K, k_copy(i).wait_recv)
        for half in range(2):
            at = pl.ds(half * (rows // 2), rows // 2)
            total = lax.dot_general(
                x2[g, at, :], wq[QL + lo : QL + hi, :], (((1,), (1,)), ((), ())),
                preferred_element_type=f32,
            ) + lax.dot_general(
                xk[at, :], wk[lo:hi, :], (((1,), (1,)), ((), ())), preferred_element_type=f32
            )
            kvp[pl.ds(half * (pages // 2), pages // 2), :, lo:hi] = total.reshape(
                pages // 2, PAGE, hi - lo
            )
        for i in range(S):
            a = lax.rem(s + 1 + i, S)
            copy = remote(
                kvp.at[:, k_lane(a * T + 1 - t), lo:hi], bk.at[a, :, :, lo:hi],
                tk_s.at[part, i], tk_r.at[part, i], {"tp": 1 - t},
            )
            copy.start()
            tk.append(copy)

    def kv_across(part):
        lo, hi = kv_parts[part]
        tk[2 * part].wait_recv()
        ck[:, :, lo:hi] = (
            kvp[:, k_lane((1 - s) * T + t), lo:hi] + bk[1 - s, :, :, lo:hi]
        )
        copy = remote(
            ck.at[:, :, lo:hi], ek.at[:, :, lo:hi], sk_s.at[part], sk_r.at[part], {"stg": 1 - s}
        )
        copy.start()
        sk.append(copy)

    def kv_norm():
        for part in range(len(kv_parts)):
            tk[2 * part + 1].wait_recv()
        k = kvp[:, k_lane(lane), :] + bk[s]
        for copy in sk:
            copy.wait_recv()
        k = (k + ek[...]).reshape(pages * lane_rows, kvw)
        lat, tail = k[:, :KVL], k[:, KVL:]
        square = jnp.sum(lat * lat, axis=1, keepdims=True)
        lat = lat * (lax.rsqrt(square / KVL + norm_eps) * kg_ref[...])
        to = lax.broadcasted_iota(jnp.int32, (ROPE, ROPE), 1)
        at = lax.broadcasted_iota(jnp.int32, (ROPE, ROPE), 0)
        even = lax.rem(to, 2) == 0
        swap = jnp.where(even & (at == to + 1), -1.0, 0.0)
        swap = jnp.where(jnp.logical_not(even) & (at == to - 1), 1.0, swap)
        partner = jnp.dot(
            tail, swap, preferred_element_type=f32, precision=lax.Precision.HIGHEST
        )
        turn = rope[...].reshape(pages * lane_rows, 2 * ROPE)
        tail = tail * turn[:, :ROPE] + partner * turn[:, ROPE:]
        kvl[:, :, :KVL] = lat.reshape(pages, lane_rows, KVL)
        kvl[:, :, KVL:] = tail.reshape(pages, lane_rows, ROPE)
        for o in range(D):
            taken = [kvl[source_of(o, r)] for r in range(cap)]
            taken += [jnp.zeros((lane_rows, kvw), f32)] * (cap_rows // lane_rows - cap)
            sendp[o] = jnp.concatenate(taken, axis=0).astype(bf)
        for d in (2, 1, 3, 0):
            to = lax.rem(me + d, D)
            for across, target in enumerate(({"dec": to}, {"dec": to, "stg": 1 - s})):
                if d == 0:
                    target = {"stg": 1 - s}
                if d or across:
                    copy = remote(
                        sendp.at[to], got.at[lane, me], pg_s.at[across, d],
                        pg_r.at[across, d], target,
                    )
                    copy.start()
                    pg.append(copy)
        got[lane, me] = sendp[me]

    picked = {}

    def choose():
        owners = [plan_s_ref[0, p] for p in range(pages)]
        ranks = []
        for p in range(pages):
            rank = jnp.int32(0)
            for e in range(p):
                rank = rank + (owners[e] == owners[p]).astype(jnp.int32)
            ranks.append(rank)
        for o in range(D):
            for r in range(cap):
                found = jnp.int32(0)
                for p in range(pages):
                    found = jnp.where((owners[p] == o) & (ranks[p] == r), p, found)
                picked[o, r] = found

    def source_of(o, r):
        return picked[o, r]

    def tables():
        for copy in plan_copies:
            copy.wait_recv()
        copy = pltpu.make_async_copy(plans, plans_s, local_sem.at[6])
        copy.start()
        copy.wait()
        count = requests * per
        slots_row = jnp.full((8, 128), -1, jnp.int32)
        slots_col = jnp.full((16, 128), -1, jnp.int32)
        across = lax.broadcasted_iota(jnp.int32, (8, 128), 1)
        down = lax.broadcasted_iota(jnp.int32, (16, 128), 0)
        for d in range(D):
            rank = jnp.int32(d * cap)
            for p in range(pages):
                ours = plans_s[d, 0, p] == me
                slot = plans_s[d, 1, p]
                at = jnp.where(ours, rank, -1)
                slots_row = jnp.where(across == at, slot, slots_row)
                slots_col = jnp.where(down == at, slot, slots_col)
                rank = rank + ours.astype(jnp.int32)
        table_row = jnp.full((16, 128), -2, jnp.int32)
        table_col = jnp.full((count, 128), -2, jnp.int32)
        across16 = lax.broadcasted_iota(jnp.int32, (16, 128), 1)
        down_count = lax.broadcasted_iota(jnp.int32, (count, 128), 0)
        for k in range(count):
            slot = bt_ref[0, k // per, k % per]
            table_row = jnp.where(across16 == k, slot, table_row)
            table_col = jnp.where(down_count == k, slot, table_col)
        hit = jnp.where(table_col == slots_row[0:1], 1.0, 0.0)
        over = jnp.max(hit, axis=1, keepdims=True)
        key = lax.broadcasted_iota(jnp.int32, (count, count * PAGE), 1)
        entry = lax.broadcasted_iota(jnp.int32, (count, count * PAGE), 0)
        over = jnp.sum(jnp.where(key // PAGE == entry, over, 0.0), axis=0, keepdims=True)
        over_keys[...] = jnp.broadcast_to(over, over_keys.shape)
        place = jnp.where(slots_col == table_row, across16.astype(f32) + 1.0, 0.0)
        place = jnp.max(place, axis=1, keepdims=True)
        width = new_keys.shape[1]
        key = lax.broadcasted_iota(jnp.int32, (16, width), 1)
        entry = lax.broadcasted_iota(jnp.int32, (16, width), 0)
        inside = lax.rem(key, cap_rows)
        source = lax.rem(key // cap_rows, D)
        arrival = source * cap + inside // lane_rows
        valid = (inside // lane_rows < cap) & (arrival == entry)
        place = jnp.sum(jnp.where(valid, place, 0.0), axis=0, keepdims=True)
        new_keys[...] = jnp.broadcast_to(place, new_keys.shape)

    def old_attend(r):
        def act():
            keys = jnp.concatenate(
                [oldv[bt_ref[0, r, j]] for j in range(per)], axis=0
            )
            scores = lax.dot_general(
                dq_ref[r], keys, (((1,), (1,)), ((), ())), preferred_element_type=f32
            ) * softmax_scale
            at = lax.broadcasted_iota(jnp.int32, scores.shape, 1)
            live = (at < lens_ref[0, r]) & (
                over_keys[0:1, r * spans : (r + 1) * spans] < 0.5
            )
            scores = jnp.where(live, scores, -1e30)
            peak = jnp.max(scores, axis=1, keepdims=True)
            weight = jnp.where(live, jnp.exp(scores - peak), 0.0)
            total = jnp.sum(weight, axis=1, keepdims=True)
            mine = slice(r * heads, (r + 1) * heads)
            first_out[mine, :] = jnp.dot(
                weight.astype(bf), keys[:, :KVL], preferred_element_type=f32
            )
            column = lax.broadcasted_iota(jnp.int32, (heads, 128), 1)
            stat[mine, :] = jnp.where(column < 64, peak, total)
            query = dq_ref[r].astype(f32)
            row = nk_ref[r : r + 1, :].astype(f32)
            score = jnp.sum(query * row, axis=1, keepdims=True) * softmax_scale
            selfs[mine, :] = jnp.broadcast_to(score, (heads, 128))
            newk[mine, :] = jnp.broadcast_to(row[:, :KVL], (heads, KVL))
        return act

    def gather():
        for copy in pg:
            copy.wait_recv()
        for which, at in enumerate((lane, (1 - s) * T + t)):
            copy = remote(
                got.at[at], got.at[at], ag_s.at[which], ag_r.at[which], {"tp": 1 - t}
            )
            copy.start()
            ag.append(copy)

    def attend():
        for copy in ag:
            copy.wait_recv()
        keys = got[...].reshape(S * T * D * cap_rows, kvw)
        queries = dq_ref[...].reshape(requests * heads, kvw)
        scores = lax.dot_general(
            queries, keys, (((1,), (1,)), ((), ())), preferred_element_type=f32
        ) * softmax_scale
        place = new_keys[0:1, :].astype(jnp.int32) - 1
        at = lax.broadcasted_iota(jnp.int32, (1, scores.shape[1]), 1)
        inside = lax.rem(at, cap_rows)
        from_lane = at // (D * cap_rows)
        token = lax.rem(place, per) * PAGE + from_lane * lane_rows + lax.rem(inside, lane_rows)
        asked = jnp.where(place >= 0, place // per, -1)
        request = lax.broadcasted_iota(jnp.int32, (requests * heads, 1), 0) // heads
        length = jnp.zeros((requests * heads, 1), jnp.int32)
        for r in range(requests):
            length = jnp.where(request == r, lens_ref[0, r], length)
        live = (asked == request) & (token < length)
        scores = jnp.where(live, scores, -1e30)
        peak = stat[:, 0:1]
        peak2 = jnp.maximum(peak, jnp.max(scores, axis=1, keepdims=True))
        weight = jnp.where(live, jnp.exp(scores - peak2), 0.0)
        scale = jnp.exp(peak - peak2)
        total = jnp.sum(weight, axis=1, keepdims=True) + stat[:, 64:65] * scale
        part[...] = (
            jnp.dot(weight.astype(bf), keys[:, :KVL], preferred_element_type=f32)
            + first_out[...] * scale
        ).astype(bf)
        column = lax.broadcasted_iota(jnp.int32, pstat.shape, 1)
        pstat[...] = jnp.where(column < 64, peak2, total)
        for d in range(1, D):
            to = lax.rem(me + d, D)
            at = pl.ds(pl.multiple_of(to * fold, 16), fold)
            for which, src, dst in ((0, pstat, pstats), (1, part, parts)):
                copy = remote(
                    src.at[at], dst.at[d - 1], c_s.at[which, d - 1], c_r.at[which, d - 1],
                    {"dec": to},
                )
                copy.start()
                cc.append(copy)

    def combine():
        for copy in cc:
            copy.wait_recv()
        mine = pl.ds(pl.multiple_of(me * fold, 16), fold)
        shares = [(pstat[mine, :], part[mine, :])]
        shares += [(pstats[d], parts[d]) for d in range(D - 1)]
        own_score = selfs[mine, 0:1]
        top = own_score
        for stats, _ in shares:
            top = jnp.maximum(top, stats[:, 0:1])
        own_weight = jnp.exp(own_score - top)
        numer, denom = own_weight * newk[mine, :], own_weight
        for stats, share in shares:
            factor = jnp.exp(stats[:, 0:1] - top)
            numer = numer + factor * share.astype(f32)
            denom = denom + factor * stats[:, 64:65]
        fin[me] = (numer / denom).astype(bf)
        for d in range(1, D):
            copy = remote(
                fin.at[me], fin.at[me], f_s.at[d - 1], f_r.at[d - 1], {"dec": lax.rem(me + d, D)}
            )
            copy.start()
            ff.append(copy)

    def settle():
        for copy in ff:
            copy.wait_recv()
        for e in range(D):
            a_out[e * fold : (e + 1) * fold, :] = fin[e]

    PIECES = pieces_of(K, NQ, qw // cr)
    due = {}

    def add(tick, action, *args):
        due.setdefault(tick, []).append((action, args))

    def route(tick, p, planes, out=False):
        add(tick, step_compute, p, planes, out)
        add(tick + 1, step_tp, p, planes, out)
        add(tick + 1 + HOPX, step_x, p, planes, out)
        add(tick + 1 + HOPX + HOPY, step_y, p, planes, out)
        if out:
            add(tick + 2 + HOPX + 2 * HOPY, step_back, p)

    blocks = [[p for p in PIECES if p[0] // K == j] for j in range(3)]
    last = 2 * K

    def x_need():
        x_arrived().wait_recv()
        if F:
            for m in (0, D - 1):
                when(me == m, x_out_other(m).start)

    kv_at = KV
    for nth, (early, later) in enumerate(KV_STEPS):
        add(early, kv_project, nth)
        add(later, kv_across, nth)
    for gap, stage in zip(KV_GAPS, (kv_norm, gather, attend, combine)):
        add(kv_at + gap, stage)
    add(1, choose)
    add(3, tables)
    for r in range(requests):
        add(4 + r // 2, old_attend(r))
    add(OWN - 1, x_need)
    for j in range(3):
        for n, p in enumerate(blocks[j]):
            add_tick = OWN + n
            route(add_tick, p, (j,))
    for p in blocks[1]:
        done = p[1] - K - 1
        route(max(done + 2, OWN + 3), p, (2, 3))
        route(OWN + 4 + blocks[1].index(p), p, (0,))
    for p in blocks[0]:
        route(K + p[1] - 1 - AHEAD, p, (1,))
        route(K + p[1] - 1 + kvn, p, (2,))
        route(K + p[1] - 1 + kvn + 2, p, (3,))
    for n, p in enumerate(blocks[2]):
        route(OWN + 5 + n, p, (3,))
        route(K + (3 * K - NQ) + p[1] - 2 * K - 1, p, (0, 1))
    if F:
        def xo_need():
            when(is_in((1, 2)), lambda: x_wait_in())
        add(OUT - 1, xo_need)
        for n, p in enumerate(p for p in PIECES if K <= p[0] < OUT_END):
            there = K + (3 * K - NQ) + p[1] - 2 * K - 1
            route(max(OUT + n // 2, there), p, (1, 2), True)

    def x_wait_in():
        for half in range(2):
            remote(
                xo.at[half], xo.at[half], xz_s.at[0], xz_r.at[half], {"grp": 1 - g}
            ).wait_recv()

    for j in range(D):
        if j in wk_copies:
            when(me == j, wk_copies[j].wait)
    x_mine.wait()
    x_other.wait()
    rope_copy.wait()
    old_copy.wait()
    for j in range(D):
        when(me == j, own_w[j].wait)

    for n in range(max(list(due) + [2 * K]) + 1):
        if n <= 2 * K:
            relay(n)
        for action, args in due.get(n, ()):
            action(*args)

    q = qa[...]
    ss[...] = jnp.broadcast_to(jnp.sum(q * q, axis=0, keepdims=True), ss.shape)
    for i, target in enumerate(({"tp": 1 - t}, {"stg": 1 - s}, {"stg": 1 - s, "tp": 1 - t})):
        copy = remote(ss, ssin.at[i], n_s.at[i], n_r.at[i], target)
        copy.start()
        small.append(copy)
    gain = qg_ref[pl.ds(pl.multiple_of(lane * qw, 128), qw)].reshape(1, qw)
    turned = jnp.transpose(q) * gain
    square = ss[...]
    for i, copy in enumerate(small):
        copy.wait_recv()
        square = square + ssin[i]
    inverse = jnp.transpose(lax.rsqrt(square / QL + norm_eps))
    q_out[...] = (turned * inverse[:, 0:1]).astype(bf)
    settle()

    for copy in [x_swap] + plan_copies + tk + sk + pg + ag + cc + ff + small:
        copy.wait_send()
    for m in range(D):
        def left(m=m):
            for way in (-1, 1):
                for i in sends_of(m, way):
                    z_copy(i, m, way).wait_send()
            for i in range(NQ, D * K):
                if i // K != m:
                    k_copy(i).wait_send()
            if F and m in (0, D - 1):
                x_out_own(m).wait_send()
                x_out_other(m).wait_send()
        when(me == m, left)
    for p in PIECES:
        sl, tl, _ = lane_of(p)
        for out in ((False, True) if F and K <= p[0] < OUT_END else (False,)):
            inside = is_in((1, 2)) if out else is_in(tuple(range(D)))
            when(inside & (t != tl), t_copy(p, out).wait_send)
            when(inside & (t == tl) & (s != sl), h_copy(p, out).wait_send)
            when(inside & (t == tl) & (s == sl), v_copy(p, out).wait_send)
            if out:
                when(inside & (t == tl) & (s == sl), z_back(p, 1).wait_send)


def hand_over_kernel(q_ref, a_ref, q_out, a_out):
    q_out[...] = q_ref[...]
    a_out[...] = a_ref[...]


def capacity(pages, owners):
    return max(2, -(-pages // owners))


def chunk_count(rows):
    return next((k for k in (11, 3, 2) if rows % (16 * k) == 0), 1)


def pieces_of(K, NQ, lane_chunks):
    cuts = set(range(0, NQ + 1, lane_chunks)) | set(range(0, NQ, K)) | {NQ}
    cuts = sorted(cuts | {NQ - c for c in MORE})
    pieces = []
    for a, b in zip(cuts, cuts[1:]):
        parts = -(-(b - a) // LONGEST)
        ends = [a + (b - a) * i // parts for i in range(parts + 1)]
        pieces += list(zip(ends, ends[1:]))
    return pieces


OWN, OUT, HOPX, HOPY = 8, 19, 6, 4
KV, KV_GAPS = 21, (0, 6, 8, 12)
KV_CUTS, KV_STEPS = (384,), ((15, 16), (18, 19))
LONGEST, MORE = 6, ()
LATE = 10
LEAD = 10
AHEAD = 3
SHARE = 5


def fused_ok(hidden_x, proj_weight, old_cache, dec_query, page_plan, block_table):
    D, G, S, T = [lax.axis_size(n) for n in ("dec", "grp", "stg", "tp")]
    if (D, G, S, T) != (4, 2, 2, 2):
        return False
    rows, features = hidden_x.shape
    C = proj_weight.shape[1]
    K = chunk_count(C)
    cr, qw, lane_rows = C // K, QL // (S * T), PAGE // (S * T)
    pages = page_plan.shape[0]
    return (
        cr % 16 == 0
        and D * C == QL + KVL + ROPE
        and qw % cr == 0
        and qw % 128 == 0
        and 2 * C < QL < 3 * C
        and features % (128 * 7 * G) == 0
        and rows == pages * PAGE
        and rows % 128 == 0
        and pages % 2 == 0
        and lane_rows % 8 == 0
        and D * capacity(pages, D) <= 16
        and block_table.shape[1] * block_table.shape[2] <= 128
        and block_table.shape[1] == D
        and dec_query.shape[0] == D
        and dec_query.shape[1] % 16 == 0
    )


def fused(
    hidden_x, proj_weight, q_gain, kv_gain, old_cache, page_plan, block_table, split_lens,
    dec_query, new_key,
):
    D, G, S, T = [lax.axis_size(n) for n in ("dec", "grp", "stg", "tp")]
    L = S * T
    rows, features = hidden_x.shape
    C = proj_weight.shape[1]
    K = chunk_count(C)
    fh, qw, kvw = features // G, QL // L, KVL + ROPE
    F = fh * SHARE // 7
    cr, NQ = C // K, QL // (C // K)
    lane_rows = PAGE // L
    pages = page_plan.shape[0]
    cap = capacity(pages, D)
    cap_rows = -(-cap * lane_rows // 16) * 16
    requests, heads = dec_query.shape[0], dec_query.shape[1]
    width = block_table.shape[2]
    fold = requests * heads // D

    positions = np.arange(D * rows, dtype=np.float32)
    pair_index = np.arange(ROPE, dtype=np.int32) // 2
    frequency = np.power(np.float32(10000.0), -(2 * pair_index).astype(np.float32) / np.float32(ROPE))
    angles = positions[:, None] * frequency.astype(np.float32)[None, :]
    rope = np.concatenate([np.cos(angles), np.sin(angles)], axis=1).astype(np.float32)
    rope = jnp.asarray(rope.reshape(D * pages, PAGE, 2 * ROPE))

    dma = pltpu.SemaphoreType.DMA
    bf, f32, i32 = jnp.bfloat16, jnp.float32, jnp.int32
    vmem = pl.BlockSpec(memory_space=pltpu.VMEM)
    smem = pl.BlockSpec(memory_space=pltpu.SMEM)
    hbm = pl.BlockSpec(memory_space=pl.ANY)
    kn = len(KV_STEPS)
    n = len(pieces_of(K, NQ, qw // cr))
    both = G * rows
    outs = (NQ - K) * cr if F else 16
    qo_rows = qw if F else 16
    V = pltpu.VMEM
    q_out, a_out = pl.pallas_call(
        functools.partial(fused_kernel, (D, G, S, T, K, F)),
        out_shape=(
            jax.ShapeDtypeStruct((rows, qw), bf),
            jax.ShapeDtypeStruct((requests * heads, KVL), bf),
        ),
        in_specs=[hbm, hbm, vmem, vmem, hbm, smem, smem, smem, vmem, hbm, vmem, vmem],
        out_specs=(vmem, vmem),
        scratch_shapes=[
            V((D * C, fh), bf), V((kvw, fh), bf), V((G, rows, fh), bf), V((rows, fh), bf),
            V((G, rows, max(F, 128)), bf),
            V((QL, both), f32), V((QL, both), f32), V((qw, both), bf), V((qw, both), bf),
            V((qw, rows), bf), V((qw, rows), bf), V((qw, rows), f32),
            V((outs, both), f32), V((outs, both), f32), V((qo_rows, both), bf), V((qo_rows, both), bf),
            V((qo_rows, rows), bf), V((qo_rows, rows), bf), V((qo_rows, rows), f32),
            V((qo_rows, rows), bf), V((qo_rows, rows), bf),
            V((8, rows), f32), V((L - 1, 8, rows), f32),
            V((pages, PAGE, kvw), f32), V((S, pages, lane_rows, kvw), f32),
            V((pages, lane_rows, kvw), f32), V((pages, lane_rows, kvw), f32),
            V((pages, lane_rows, kvw), f32),
            V((D, cap_rows, kvw), bf), V((L, D, cap_rows, kvw), bf),
            V((8, 128), i32), V((D, 8, 128), i32), pltpu.SMEM((D, 8, 128), i32),
            V((pages, lane_rows, 2 * ROPE), f32), V(old_cache.shape, bf),
            V((8, requests * width * PAGE), f32), V((8, L * D * cap_rows), f32),
            V((requests * heads, 128), f32), V((requests * heads, KVL), f32),
            V((requests * heads, KVL), bf), V((requests * heads, 128), f32),
            V((D - 1, fold, KVL), bf), V((D - 1, fold, 128), f32),
            V((requests * heads, 128), f32), V((requests * heads, KVL), f32),
            V((D, fold, KVL), bf),
            dma((7,)), dma((2, D * K)), dma((D * K,)), dma((D * K - NQ,)), dma((D * K - NQ,)),
            dma((2,)), dma((2,)), dma((2,)),
            dma((n,)), dma((n,)), dma((n,)), dma((n,)), dma((n,)), dma((n,)),
            dma((n,)), dma((n,)), dma((n,)), dma((n,)), dma((n,)), dma((n,)), dma((n,)), dma((n,)),
            dma((kn, S)), dma((kn, S)), dma((kn,)), dma((kn,)), dma((D - 1,)), dma((D - 1,)),
            dma((2, D)), dma((2, D)), dma((2,)), dma((2,)),
            dma((2, D - 1)), dma((2, D - 1)), dma((D - 1,)), dma((D - 1,)), dma((3,)), dma((3,)),
        ],
        compiler_params=pltpu.CompilerParams(
            collective_id=0, has_side_effects=True, vmem_limit_bytes=60 * 1024 * 1024
        ),
    )(
        proj_weight.T, hidden_x, q_gain, kv_gain[None, :], rope, block_table, split_lens.T,
        page_plan.T, page_plan.T, old_cache, dec_query, new_key,
    )
    return pl.pallas_call(
        hand_over_kernel,
        out_shape=(
            jax.ShapeDtypeStruct((rows, qw), bf),
            jax.ShapeDtypeStruct((requests, heads, KVL), bf),
        ),
        in_specs=[vmem, vmem],
        out_specs=(vmem, vmem),
    )(q_out, a_out.reshape(requests, heads, KVL))


def body(
    hidden_x,
    proj_weight,
    q_gain,
    kv_gain,
    old_cache,
    page_plan,
    block_table,
    split_lens,
    dec_query,
    new_key,
):
    if fused_ok(hidden_x, proj_weight, old_cache, dec_query, page_plan, block_table):
        return fused(
            hidden_x, proj_weight, q_gain, kv_gain, old_cache, page_plan, block_table,
            split_lens, dec_query, new_key,
        )
    projected = jnp.dot(
        hidden_x,
        lax.all_gather(proj_weight, "dec", axis=1, tiled=True),
        preferred_element_type=jnp.float32,
    )
    query_part = projected[:, :QL]
    kv_part = projected[:, QL:]
    tokens_here = hidden_x.shape[0]
    positions = (
        lax.axis_index("dec") * tokens_here + jnp.arange(tokens_here, dtype=jnp.int32)
    ).astype(jnp.float32)
    lane_count = lax.axis_size(("stg", "tp"))
    lane_index = lax.axis_index(("stg", "tp"))
    owner_count = lax.axis_size("dec")
    page_count = page_plan.shape[0]
    capacity = max(2, -(-page_count // owner_count))
    query_width = QL // lane_count
    query_cols, kv_cols = (
        lax.psum_scatter(query_part, ("stg", "tp"), scatter_dimension=1, tiled=True),
        lax.psum_scatter(kv_part, ("stg", "tp"), scatter_dimension=1, tiled=True),
    )
    kv_width = kv_cols.shape[1]
    col_start = lane_index * kv_width
    columns = col_start + jnp.arange(kv_width, dtype=jnp.int32)
    latent_part_sq = jnp.sum(jnp.where(columns[None, :] < KVL, kv_cols * kv_cols, 0.0), axis=1)
    query_sq, latent_sq = lax.psum(
        (jnp.sum(query_cols * query_cols, axis=1), latent_part_sq), ("stg", "tp")
    )
    kv_rows = kv_finish(kv_cols, col_start, latent_sq, kv_gain, positions)
    kv_pages = kv_rows.reshape(page_count, PAGE, kv_width)
    send_pages, send_labels = pack_pages(kv_pages, page_plan, owner_count, capacity)
    got_slices, got_labels = (
        lax.all_to_all(send_pages, "dec", split_axis=0, concat_axis=0, tiled=True),
        lax.all_to_all(send_labels, "dec", split_axis=0, concat_axis=0, tiled=True),
    )
    got_pages = lax.all_gather(got_slices, ("stg", "tp"), axis=3, tiled=True)
    query_gain = lax.dynamic_slice_in_dim(q_gain, lane_index * query_width, query_width)
    q_latent = (
        query_cols * lax.rsqrt(query_sq / QL + norm_eps)[:, None] * query_gain[None, :]
    ).astype(jnp.bfloat16)
    cache = place_pages(old_cache, got_pages, got_labels)
    slot_table = block_table[0]
    request_count = slot_table.shape[0]
    key_rows = take_each(cache, slot_table.reshape(-1)).reshape(
        request_count, -1, cache.shape[2]
    )
    scores = (
        jnp.einsum("rhc,rlc->rhl", dec_query, key_rows, preferred_element_type=jnp.float32)
        * softmax_scale
    )
    live_mask = jnp.arange(key_rows.shape[1], dtype=jnp.int32)[None, :] < split_lens[:, 0][:, None]
    scores = jnp.where(live_mask[:, None, :], scores, -1e30)
    row_peak = jnp.max(scores, axis=2)
    weights = jnp.where(live_mask[:, None, :], jnp.exp(scores - row_peak[:, :, None]), 0.0)
    row_total = jnp.sum(weights, axis=2)
    rounded = weights.astype(jnp.bfloat16)
    partial_out = jnp.einsum(
        "rhl,rlc->rhc", rounded, key_rows[:, :, :KVL], preferred_element_type=jnp.float32
    )
    peak_all, total_all, output_all = combined_all(
        (row_peak, row_total, partial_out), "dec", combine_parts
    )
    self_score = (
        jnp.einsum("rhc,rc->rh", dec_query, new_key, preferred_element_type=jnp.float32)
        * softmax_scale
    )
    overall = jnp.maximum(peak_all, self_score)
    carried = jnp.exp(peak_all - overall)
    self_weight = jnp.exp(self_score - overall)
    denom = total_all * carried + self_weight
    numer = output_all * carried[:, :, None] + self_weight[:, :, None] * new_key[
        :, None, :KVL
    ].astype(jnp.float32)
    attn_latent = (numer / denom[:, :, None]).astype(jnp.bfloat16)
    return (q_latent, attn_latent)


def solution(mesh):
    return jax.shard_map(
        body,
        mesh=mesh,
        in_specs=(
            P(("grp", "dec"), ("stg", "tp")),
            P(("stg", "tp"), "dec"),
            P(),
            P(),
            P(("grp", "dec"), None, None),
            P(("grp", "dec"), None),
            P(("grp", "dec"), None, None),
            P("grp", "dec"),
            P("grp", ("stg", "tp"), None),
            P("grp", None),
        ),
        out_specs=(P(("grp", "dec"), ("stg", "tp")), P("grp", ("stg", "tp"), None)),
        check_vma=False,
    )
```

```python
import functools

import jax
import jax.numpy as jnp
import numpy as np
from jax import lax
from jax.experimental import pallas as pl
from jax.experimental.pallas import tpu as pltpu
from jax.sharding import PartitionSpec as P

QL = 1536
KVL = 512
ROPE = 64
PAGE = 32


softmax_scale = 192.0 ** (-0.5)
norm_eps = 1e-06


def combined_all(part, axis, combine):
    gathered = jax.tree.map(lambda a: lax.all_gather(a, axis), part)

    def take(source):
        return jax.tree.map(lambda a: lax.dynamic_index_in_dim(a, source, 0, False), gathered)

    return lax.fori_loop(
        1, lax.axis_size(axis), lambda source, state: combine(state, take(source)), take(0)
    )


def rope_rotate(matrix, col_start, positions):
    col_count = matrix.shape[1]
    columns = col_start + jnp.arange(col_count, dtype=jnp.int32)
    is_rope = columns >= KVL
    pair_index = jnp.maximum(columns - KVL, 0) // 2
    frequency = jnp.power(jnp.float32(10000.0), -(2 * pair_index).astype(jnp.float32) / ROPE)
    angles = positions[:, None] * frequency[None, :]
    cosine = jnp.where(is_rope[None, :], jnp.cos(angles), 1.0)
    sine_part = jnp.where(is_rope[None, :], jnp.sin(angles), 0.0)
    paired = matrix.reshape(matrix.shape[0], col_count // 2, 2)
    partner = jnp.stack([-paired[:, :, 1], paired[:, :, 0]], axis=2).reshape(matrix.shape)
    return matrix * cosine + partner * sine_part


def kv_finish(matrix, col_start, latent_sq, kv_gain, positions):
    col_count = matrix.shape[1]
    columns = col_start + jnp.arange(col_count, dtype=jnp.int32)
    gain_full = jnp.concatenate([kv_gain, jnp.ones((ROPE,), jnp.float32)])
    gain_cols = lax.dynamic_slice_in_dim(gain_full, col_start, col_count)
    inverse = lax.rsqrt(latent_sq / KVL + norm_eps)
    row_scale = jnp.where(columns[None, :] < KVL, inverse[:, None] * gain_cols[None, :], 1.0)
    return rope_rotate(matrix * row_scale, col_start, positions).astype(jnp.bfloat16)


def take_each(array, ids):
    return lax.map(lambda i: lax.dynamic_index_in_dim(array, i, 0, False), ids)


def pack_pages(kv_pages, page_table, owner_count, capacity):
    owners = page_table[:, 0]
    slot_ids = page_table[:, 1]
    page_ids = jnp.arange(kv_pages.shape[0], dtype=jnp.int32)
    earlier = (owners[:, None] == owners[None, :]) & (page_ids[None, :] < page_ids[:, None])
    ranking = jnp.sum(earlier.astype(jnp.int32), axis=1)
    targets = owners * capacity + ranking
    places = jnp.arange(owner_count * capacity, dtype=jnp.int32)
    matches = targets[None, :] == places[:, None]
    source_ids = jnp.sum(jnp.where(matches, page_ids[None, :], 0), axis=1)
    filled = jnp.any(matches, axis=1)
    chosen = jnp.where(
        filled[:, None, None], take_each(kv_pages, source_ids), jnp.zeros((), kv_pages.dtype)
    )
    labels = jnp.where(filled, jnp.take(slot_ids, source_ids), -1).astype(jnp.bfloat16)
    return (
        chosen.reshape(owner_count, capacity, kv_pages.shape[1], kv_pages.shape[2]),
        labels.reshape(owner_count, capacity),
    )


def place_pages(old_cache, got_pages, got_labels):
    flat_pages = got_pages.reshape(-1, old_cache.shape[1], old_cache.shape[2])
    label_ids = got_labels.reshape(-1).astype(jnp.int32)
    slot_ids = jnp.arange(old_cache.shape[0], dtype=jnp.int32)
    arrival_ids = jnp.arange(label_ids.shape[0], dtype=jnp.int32)
    matches = label_ids[None, :] == slot_ids[:, None]
    source_ids = jnp.sum(jnp.where(matches, arrival_ids[None, :], 0), axis=1)
    arrived = jnp.any(matches, axis=1)
    return jnp.where(arrived[:, None, None], take_each(flat_pages, source_ids), old_cache)


def combine_parts(former, latter):
    overall = jnp.maximum(former[0], latter[0])
    front_scale = jnp.exp(former[0] - overall)
    back_scale = jnp.exp(latter[0] - overall)
    return (
        overall,
        former[1] * front_scale + latter[1] * back_scale,
        former[2] * front_scale[:, :, None] + latter[2] * back_scale[:, :, None],
    )


MESH = pl.DeviceIdType.MESH


def fused_kernel(
    dims, w_ref, x_ref, qg_ref, kg_ref, rope_ref, bt_ref, lens_ref, plan_s_ref, plan_ref,
    old_ref, dq_ref, nk_ref, q_out, a_out,
    wq, wk, x2, xk, xo, pt, bq, cq, eq, yq, yr, qa, po, bo, co, eo, yo, yi, qo, ro, ri,
    ss, ssin, kvp, bk, ck, ek, kvl, sendp, got, plan_pad, plans, plans_s, rope, oldv,
    over_keys, new_keys, stat, first_out, part, pstat, parts, pstats, selfs, newk, fin,
    local_sem, zs, zr, ks, kr, xy, xz_s, xz_r,
    t_s, t_r, h_s, h_r, v_s, v_r, ot_s, ot_r, oh_s, oh_r, ov_s, ov_r, oz_s, oz_r,
    tk_s, tk_r, sk_s, sk_r, pl_s, pl_r, pg_s, pg_r, ag_s, ag_r, c_s, c_r, f_s, f_r, n_s, n_r,
):
    D, G, S, T, K, F = dims
    C, fh = w_ref.shape[0], w_ref.shape[1] // G
    rows = x_ref.shape[0]
    qw = q_out.shape[1]
    kvw = kvl.shape[2]
    cr = C // K
    N = fh - F
    NQ = QL // cr
    OUT_END = NQ - LATE
    pages = rows // PAGE
    lane_rows = kvl.shape[1]
    cap_rows = sendp.shape[1]
    cap = capacity(pages, D)
    requests, heads = dq_ref.shape[0], dq_ref.shape[1]
    per = bt_ref.shape[2]
    spans = per * PAGE
    fold = requests * heads // D
    bf, f32 = jnp.bfloat16, jnp.float32
    me, g = lax.axis_index("dec"), lax.axis_index("grp")
    s, t = lax.axis_index("stg"), lax.axis_index("tp")
    lane = s * T + t
    mine_half = pl.ds(pl.multiple_of(g * fh, 128), fh)
    other_half = pl.ds(pl.multiple_of((1 - g) * fh, 128), fh)
    ends = []

    def remote(src, dst, send, recv, target):
        return pltpu.make_async_remote_copy(
            src_ref=src, dst_ref=dst, send_sem=send, recv_sem=recv,
            device_id=target, device_id_type=MESH,
        )

    def local(src, dst, i):
        copy = pltpu.make_async_copy(src, dst, local_sem.at[i])
        copy.start()
        return copy

    def when(condition, action):
        @pl.when(condition)
        def _():
            action()

    own_w = []
    for j in range(D):
        own_w.append(pltpu.make_async_copy(
            w_ref.at[:, mine_half], wq.at[j * C : (j + 1) * C], local_sem.at[0]
        ))
        when(me == j, own_w[j].start)
    x_mine = local(x_ref.at[:, mine_half], x2.at[g], 1)
    x_other = local(x_ref.at[:, other_half], xk, 2)
    kv_cut = 3 * C - QL
    wk_copies = {
        2: pltpu.make_async_copy(
            w_ref.at[C - kv_cut : C, other_half], wk.at[:kv_cut], local_sem.at[3]),
        3: pltpu.make_async_copy(w_ref.at[:, other_half], wk.at[kv_cut:], local_sem.at[3]),
    }
    for j, copy in wk_copies.items():
        when(me == j, copy.start)
    rope_copy = local(
        rope_ref.at[pl.ds(me * pages, pages),
                    pl.ds(pl.multiple_of(lane * lane_rows, 8), lane_rows)], rope, 4
    )
    old_copy = local(old_ref, oldv, 5)

    barrier = pltpu.get_barrier_semaphore()
    greeted = [{"dec": lax.rem(me + d, D)} for d in range(1, D)]
    greeted += [{"dec": lax.rem(me + d, D), "stg": 1 - s} for d in range(1, D)]
    greeted += [{"grp": 1 - g}, {"tp": 1 - t}, {"stg": 1 - s}, {"stg": 1 - s, "tp": 1 - t}]
    for target in greeted:
        pl.semaphore_signal(barrier, inc=1, device_id=target, device_id_type=MESH)
    pl.semaphore_wait(barrier, len(greeted))

    def w_rows(i, width):
        return wq.at[i * cr : (i + 1) * cr, :width]

    def z_width(i, m, way):
        return N if (m + way in (0, D - 1) and K <= i < OUT_END) else fh

    def z_copy(i, m, way):
        width = z_width(i, m, way)
        if i // K == m:
            at = (i - m * K) * cr
            src = w_ref.at[at : at + cr, pl.ds(pl.multiple_of(g * fh, 128), width)]
        else:
            src = w_rows(i, width)
        return remote(
            src, w_rows(i, width), zs.at[(way + 1) // 2, i], zr.at[i], {"dec": m + way}
        )

    def z_start(i, m, way):
        z_copy(i, m, way).start()

    def z_wait(i, m):
        way = -1 if i // K > m else 1
        z_copy_in(i, m, way).wait_recv()

    def z_copy_in(i, m, way):
        width = z_width(i, m - way, way)
        return remote(
            w_rows(i, width), w_rows(i, width), zs.at[(way + 1) // 2, i], zr.at[i],
            {"dec": m - way},
        )

    def k_rows(i):
        return (i - NQ) * cr

    def k_copy(i):
        at = k_rows(i)
        return remote(
            w_rows(i, fh), wk.at[at : at + cr], ks.at[i - NQ], kr.at[i - NQ], {"grp": 1 - g}
        )

    def sends_of(m, way):
        if not 0 <= m + way < D:
            return []
        return [
            i for i in range(D * K)
            if (i // K == m or (i // K > m if way < 0 else i // K < m))
            and not (way > 0 and i // K == D - 1) and not (way < 0 and i // K == 0)
        ]

    LM = list(range(NQ, 4 * K)) + list(range(2 * K, NQ))
    RM = list(range(K, 2 * K)) + list(range(K))
    kvn = 3 * K - NQ

    x_swap = remote(
        x_ref.at[:, other_half], x2.at[g], xy.at[0], xy.at[1], {"grp": 1 - g}
    )

    def x_arrived():
        return remote(
            x2.at[1 - g], x2.at[1 - g], xy.at[0], xy.at[1], {"grp": 1 - g}
        )

    def x_out_own(m):
        way = 1 if m == 0 else -1
        return remote(
            x_ref.at[:, pl.ds(pl.multiple_of(g * fh + N, 128), F)], xo.at[g],
            xz_s.at[0], xz_r.at[0], {"dec": m + way},
        )

    def x_out_other(m):
        way = 1 if m == 0 else -1
        return remote(
            x2.at[1 - g, :, N:], xo.at[1 - g], xz_s.at[1], xz_r.at[1], {"dec": m + way}
        )

    plan_pad[...] = jnp.full(plan_pad.shape, -1, jnp.int32)
    plan_pad[0:2, 0:pages] = plan_ref[...]
    plan_copies = []

    def start_first(m):
        def go():
            if m == 3:
                for i in range(3 * K, 4 * K):
                    z_start(i, 3, -1)
                if F:
                    x_out_own(3).start()
            if m == 2:
                for i in range(NQ, 3 * K):
                    z_start(i, 2, -1)
                    z_start(i, 2, 1)
                for i in range(2 * K, NQ):
                    z_start(i, 2, 1)
            if m == 1:
                for i in range(K, 2 * K):
                    z_start(i, 1, 1)
                    z_start(i, 1, -1)
            if m == 0:
                for i in range(FIRST):
                    z_start(i, 0, 1)
                if F:
                    x_out_own(0).start()
                for i in range(FIRST, K):
                    z_start(i, 0, 1)
        return go

    for d in range(1, D):
        copy = remote(
            plan_pad, plans.at[me], pl_s.at[d - 1], pl_r.at[d - 1], {"dec": lax.rem(me + d, D)}
        )
        copy.start()
        plan_copies.append(copy)
    plans[me] = plan_pad[...]
    for m in (3, 2, 1, 0):
        when(me == m, start_first(m))
    x_swap.start()

    def waited_at_tick(i, m):
        if i // K > m:
            return i in LM and (m > 0 or i >= NQ)
        return (i in RM and m < D - 1) or i >= NQ

    def relay(n):
        def go(m):
            def act():
                if n < len(LM):
                    i = LM[n]
                    if i // K > m and waited_at_tick(i, m):
                        z_wait(i, m)
                        if m > 0:
                            z_start(i, m, -1)
                        if i >= NQ:
                            k_copy(i).start()
                at = n + AHEAD if m == 1 else n - kvn
                if 0 <= at < len(RM):
                    i = RM[at]
                    if i // K < m and waited_at_tick(i, m):
                        z_wait(i, m)
                        z_start(i, m, 1)
                if m == D - 1 and n < 3 * K - NQ:
                    i = NQ + n
                    z_wait(i, m)
                    k_copy(i).start()
                if m == 2 and n == K:
                    for i in range(2 * K, 2 * K + LEAD):
                        z_start(i, 2, -1)
                if m == 2 and K < n < NQ - K - LEAD + 1:
                    z_start(n + K + LEAD - 1, 2, -1)
            return act
        for m in range(D):
            when(me == m, go(m))

    def lane_of(p):
        l = p[0] * cr // qw
        return l // T, l % T, p[0] * cr - l * qw

    def mul(acc_ref, at, a, b, xs, lo, hi):
        for half in range(G):
            acc_ref[at : at + b - a, half * rows : (half + 1) * rows] = lax.dot_general(
                wq[a:b, lo:hi], xs[half] if xs is not x2 else xs[half, :, lo:hi],
                (((1,), (1,)), ((), ())), preferred_element_type=f32,
            )

    def t_copy(p, out):
        a, b = p[0] * cr, p[1] * cr
        i = PIECES.index(p)
        if out:
            at = a - K * cr
            return remote(
                po.at[at : at + b - a], bo.at[at : at + b - a], ot_s.at[i], ot_r.at[i],
                {"tp": 1 - t},
            )
        return remote(pt.at[a:b], bq.at[a:b], t_s.at[i], t_r.at[i], {"tp": 1 - t})

    def h_copy(p, out):
        la = lane_of(p)[2]
        n, i = (p[1] - p[0]) * cr, PIECES.index(p)
        src, dst, send, recv = (co, eo, oh_s, oh_r) if out else (cq, eq, h_s, h_r)
        return remote(
            src.at[la : la + n], dst.at[la : la + n], send.at[i], recv.at[i], {"stg": 1 - s}
        )

    def v_copy(p, out):
        la = lane_of(p)[2]
        n, i = (p[1] - p[0]) * cr, PIECES.index(p)
        src, dst, send, recv = (yo, yi, ov_s, ov_r) if out else (yq, yr, v_s, v_r)
        return remote(
            src.at[la : la + n], dst.at[la : la + n], send.at[i], recv.at[i], {"grp": 1 - g}
        )

    def z_back(p, m):
        la = lane_of(p)[2]
        n, i = (p[1] - p[0]) * cr, PIECES.index(p)
        return remote(
            ro.at[la : la + n], ri.at[la : la + n], oz_s.at[i], oz_r.at[i],
            {"dec": 0 if m == 1 else D - 1},
        )

    def is_in(planes):
        result = me == planes[0]
        for m in planes[1:]:
            result = result | (me == m)
        return result

    def step_compute(p, planes, out):
        a, b = p[0] * cr, p[1] * cr
        sl, tl, _ = lane_of(p)
        for m in planes:
            def arrive(m=m):
                for i in range(*p):
                    if i // K != m and not out and not waited_at_tick(i, m):
                        z_wait(i, m)
            if not out and any(i // K != m and not waited_at_tick(i, m) for i in range(*p)):
                when(me == m, arrive)

        def full():
            if out:
                mul(po, a - K * cr, a, b, xo, N, fh)
            else:
                mul(pt, a, a, b, x2, 0, fh)

        def narrow():
            mul(pt, a, a, b, x2, 0, N)

        ended = tuple(m for m in planes if m in (0, D - 1))
        inner = tuple(m for m in planes if m not in (0, D - 1))
        if not out and F and K <= p[0] < OUT_END:
            if inner:
                when(is_in(inner), full)
            if ended:
                when(is_in(ended), narrow)
        else:
            when(is_in(planes), full)
        when(is_in(planes) & (t != tl), t_copy(p, out).start)

    def step_tp(p, planes, out):
        a, b = p[0] * cr, p[1] * cr
        sl, tl, la = lane_of(p)
        acc, add, to = (po, bo, co) if out else (pt, bq, cq)
        at = a - K * cr if out else a
        n = b - a

        def act():
            t_copy(p, out).wait_recv()

            @pl.when(s != sl)
            def _():
                to[la : la + n, :] = (acc[at : at + n, :] + add[at : at + n, :]).astype(bf)
                h_copy(p, out).start()

            @pl.when(s == sl)
            def _():
                acc[at : at + n, :] = acc[at : at + n, :] + add[at : at + n, :]
        when(is_in(planes) & (t == tl), act)

    def g_cols(which):
        return pl.ds(pl.multiple_of(which * rows, 128), rows)

    def step_x(p, planes, out):
        a, b = p[0] * cr, p[1] * cr
        sl, tl, la = lane_of(p)
        acc, came, keep, to = (po, eo, qo, yo) if out else (pt, eq, qa, yq)
        at = a - K * cr if out else a
        n = b - a

        def act():
            h_copy(p, out).wait_recv()
            to[la : la + n, :] = (
                acc[at : at + n, g_cols(1 - g)] + came[la : la + n, g_cols(1 - g)].astype(f32)
            ).astype(bf)
            v_copy(p, out).start()
            keep[la : la + n, :] = (
                acc[at : at + n, g_cols(g)] + came[la : la + n, g_cols(g)].astype(f32)
            )
        when(is_in(planes) & (t == tl) & (s == sl), act)

    def step_y(p, planes, out):
        sl, tl, la = lane_of(p)
        n = (p[1] - p[0]) * cr

        def act():
            v_copy(p, out).wait_recv()
            if out:
                ro[la : la + n, :] = (
                    qo[la : la + n, :] + yi[la : la + n, :].astype(f32)
                ).astype(bf)
                for m in planes:
                    when(me == m, z_back(p, m).start)
            else:
                qa[la : la + n, :] = qa[la : la + n, :] + yr[la : la + n, :].astype(f32)
        when(is_in(planes) & (t == tl) & (s == sl), act)

    def step_back(p):
        sl, tl, la = lane_of(p)
        n = (p[1] - p[0]) * cr

        def act():
            z_back(p, 1).wait_recv()
            qa[la : la + n, :] = qa[la : la + n, :] + ri[la : la + n, :].astype(f32)
        when(is_in((0, D - 1)) & (t == tl) & (s == sl), act)

    def k_lane(at):
        return pl.ds(pl.multiple_of(at * lane_rows, 8), lane_rows)

    tk, sk, pg, ag, cc, ff, small = [], [], [], [], [], [], []

    cuts = [0] + [c for c in KV_CUTS if c < kvw] + [kvw]
    kv_parts = list(zip(cuts, cuts[1:]))

    def kv_project(part):
        lo, hi = kv_parts[part]
        for i in range(NQ, D * K):
            if lo < k_rows(i) + cr <= hi or (hi < kvw and lo <= k_rows(i) < hi < k_rows(i) + cr):
                when(me != i // K, k_copy(i).wait_recv)
        for half in range(2):
            at = pl.ds(half * (rows // 2), rows // 2)
            total = lax.dot_general(
                x2[g, at, :], wq[QL + lo : QL + hi, :], (((1,), (1,)), ((), ())),
                preferred_element_type=f32,
            ) + lax.dot_general(
                xk[at, :], wk[lo:hi, :], (((1,), (1,)), ((), ())), preferred_element_type=f32
            )
            kvp[pl.ds(half * (pages // 2), pages // 2), :, lo:hi] = total.reshape(
                pages // 2, PAGE, hi - lo
            )
        for i in range(S):
            a = lax.rem(s + 1 + i, S)
            copy = remote(
                kvp.at[:, k_lane(a * T + 1 - t), lo:hi], bk.at[a, :, :, lo:hi],
                tk_s.at[part, i], tk_r.at[part, i], {"tp": 1 - t},
            )
            copy.start()
            tk.append(copy)

    def kv_across(part):
        lo, hi = kv_parts[part]
        tk[2 * part].wait_recv()
        ck[:, :, lo:hi] = (
            kvp[:, k_lane((1 - s) * T + t), lo:hi] + bk[1 - s, :, :, lo:hi]
        )
        copy = remote(
            ck.at[:, :, lo:hi], ek.at[:, :, lo:hi], sk_s.at[part], sk_r.at[part], {"stg": 1 - s}
        )
        copy.start()
        sk.append(copy)

    def kv_norm():
        for part in range(len(kv_parts)):
            tk[2 * part + 1].wait_recv()
        k = kvp[:, k_lane(lane), :] + bk[s]
        for copy in sk:
            copy.wait_recv()
        k = (k + ek[...]).reshape(pages * lane_rows, kvw)
        lat, tail = k[:, :KVL], k[:, KVL:]
        square = jnp.sum(lat * lat, axis=1, keepdims=True)
        lat = lat * (lax.rsqrt(square / KVL + norm_eps) * kg_ref[...])
        to = lax.broadcasted_iota(jnp.int32, (ROPE, ROPE), 1)
        at = lax.broadcasted_iota(jnp.int32, (ROPE, ROPE), 0)
        even = lax.rem(to, 2) == 0
        swap = jnp.where(even & (at == to + 1), -1.0, 0.0)
        swap = jnp.where(jnp.logical_not(even) & (at == to - 1), 1.0, swap)
        partner = jnp.dot(
            tail, swap, preferred_element_type=f32, precision=lax.Precision.HIGHEST
        )
        turn = rope[...].reshape(pages * lane_rows, 2 * ROPE)
        tail = tail * turn[:, :ROPE] + partner * turn[:, ROPE:]
        kvl[:, :, :KVL] = lat.reshape(pages, lane_rows, KVL)
        kvl[:, :, KVL:] = tail.reshape(pages, lane_rows, ROPE)
        for o in range(D):
            taken = [kvl[source_of(o, r)] for r in range(cap)]
            taken += [jnp.zeros((lane_rows, kvw), f32)] * (cap_rows // lane_rows - cap)
            sendp[o] = jnp.concatenate(taken, axis=0).astype(bf)
        for d in (2, 1, 3, 0):
            to = lax.rem(me + d, D)
            for across, target in enumerate(({"dec": to}, {"dec": to, "stg": 1 - s})):
                if d == 0:
                    target = {"stg": 1 - s}
                if d or across:
                    copy = remote(
                        sendp.at[to], got.at[lane, me], pg_s.at[across, d],
                        pg_r.at[across, d], target,
                    )
                    copy.start()
                    pg.append(copy)
        got[lane, me] = sendp[me]

    picked = {}

    def choose():
        owners = [plan_s_ref[0, p] for p in range(pages)]
        ranks = []
        for p in range(pages):
            rank = jnp.int32(0)
            for e in range(p):
                rank = rank + (owners[e] == owners[p]).astype(jnp.int32)
            ranks.append(rank)
        for o in range(D):
            for r in range(cap):
                found = jnp.int32(0)
                for p in range(pages):
                    found = jnp.where((owners[p] == o) & (ranks[p] == r), p, found)
                picked[o, r] = found

    def source_of(o, r):
        return picked[o, r]

    def tables():
        for copy in plan_copies:
            copy.wait_recv()
        copy = pltpu.make_async_copy(plans, plans_s, local_sem.at[6])
        copy.start()
        copy.wait()
        count = requests * per
        slots_row = jnp.full((8, 128), -1, jnp.int32)
        slots_col = jnp.full((16, 128), -1, jnp.int32)
        across = lax.broadcasted_iota(jnp.int32, (8, 128), 1)
        down = lax.broadcasted_iota(jnp.int32, (16, 128), 0)
        for d in range(D):
            rank = jnp.int32(d * cap)
            for p in range(pages):
                ours = plans_s[d, 0, p] == me
                slot = plans_s[d, 1, p]
                at = jnp.where(ours, rank, -1)
                slots_row = jnp.where(across == at, slot, slots_row)
                slots_col = jnp.where(down == at, slot, slots_col)
                rank = rank + ours.astype(jnp.int32)
        table_row = jnp.full((16, 128), -2, jnp.int32)
        table_col = jnp.full((count, 128), -2, jnp.int32)
        across16 = lax.broadcasted_iota(jnp.int32, (16, 128), 1)
        down_count = lax.broadcasted_iota(jnp.int32, (count, 128), 0)
        for k in range(count):
            slot = bt_ref[0, k // per, k % per]
            table_row = jnp.where(across16 == k, slot, table_row)
            table_col = jnp.where(down_count == k, slot, table_col)
        hit = jnp.where(table_col == slots_row[0:1], 1.0, 0.0)
        over = jnp.max(hit, axis=1, keepdims=True)
        key = lax.broadcasted_iota(jnp.int32, (count, count * PAGE), 1)
        entry = lax.broadcasted_iota(jnp.int32, (count, count * PAGE), 0)
        over = jnp.sum(jnp.where(key // PAGE == entry, over, 0.0), axis=0, keepdims=True)
        over_keys[...] = jnp.broadcast_to(over, over_keys.shape)
        place = jnp.where(slots_col == table_row, across16.astype(f32) + 1.0, 0.0)
        place = jnp.max(place, axis=1, keepdims=True)
        width = new_keys.shape[1]
        key = lax.broadcasted_iota(jnp.int32, (16, width), 1)
        entry = lax.broadcasted_iota(jnp.int32, (16, width), 0)
        inside = lax.rem(key, cap_rows)
        source = lax.rem(key // cap_rows, D)
        arrival = source * cap + inside // lane_rows
        valid = (inside // lane_rows < cap) & (arrival == entry)
        place = jnp.sum(jnp.where(valid, place, 0.0), axis=0, keepdims=True)
        new_keys[...] = jnp.broadcast_to(place, new_keys.shape)

    def old_attend(r):
        def act():
            keys = jnp.concatenate(
                [oldv[bt_ref[0, r, j]] for j in range(per)], axis=0
            )
            scores = lax.dot_general(
                dq_ref[r], keys, (((1,), (1,)), ((), ())), preferred_element_type=f32
            ) * softmax_scale
            at = lax.broadcasted_iota(jnp.int32, scores.shape, 1)
            live = (at < lens_ref[0, r]) & (
                over_keys[0:1, r * spans : (r + 1) * spans] < 0.5
            )
            scores = jnp.where(live, scores, -1e30)
            peak = jnp.max(scores, axis=1, keepdims=True)
            weight = jnp.where(live, jnp.exp(scores - peak), 0.0)
            total = jnp.sum(weight, axis=1, keepdims=True)
            mine = slice(r * heads, (r + 1) * heads)
            first_out[mine, :] = jnp.dot(
                weight.astype(bf), keys[:, :KVL], preferred_element_type=f32
            )
            column = lax.broadcasted_iota(jnp.int32, (heads, 128), 1)
            stat[mine, :] = jnp.where(column < 64, peak, total)
            query = dq_ref[r].astype(f32)
            row = nk_ref[r : r + 1, :].astype(f32)
            score = jnp.sum(query * row, axis=1, keepdims=True) * softmax_scale
            selfs[mine, :] = jnp.broadcast_to(score, (heads, 128))
            newk[mine, :] = jnp.broadcast_to(row[:, :KVL], (heads, KVL))
        return act

    def gather():
        for copy in pg:
            copy.wait_recv()
        for which, at in enumerate((lane, (1 - s) * T + t)):
            copy = remote(
                got.at[at], got.at[at], ag_s.at[which], ag_r.at[which], {"tp": 1 - t}
            )
            copy.start()
            ag.append(copy)

    def attend():
        for copy in ag:
            copy.wait_recv()
        keys = got[...].reshape(S * T * D * cap_rows, kvw)
        queries = dq_ref[...].reshape(requests * heads, kvw)
        scores = lax.dot_general(
            queries, keys, (((1,), (1,)), ((), ())), preferred_element_type=f32
        ) * softmax_scale
        place = new_keys[0:1, :].astype(jnp.int32) - 1
        at = lax.broadcasted_iota(jnp.int32, (1, scores.shape[1]), 1)
        inside = lax.rem(at, cap_rows)
        from_lane = at // (D * cap_rows)
        token = lax.rem(place, per) * PAGE + from_lane * lane_rows + lax.rem(inside, lane_rows)
        asked = jnp.where(place >= 0, place // per, -1)
        request = lax.broadcasted_iota(jnp.int32, (requests * heads, 1), 0) // heads
        length = jnp.zeros((requests * heads, 1), jnp.int32)
        for r in range(requests):
            length = jnp.where(request == r, lens_ref[0, r], length)
        live = (asked == request) & (token < length)
        scores = jnp.where(live, scores, -1e30)
        peak = stat[:, 0:1]
        peak2 = jnp.maximum(peak, jnp.max(scores, axis=1, keepdims=True))
        weight = jnp.where(live, jnp.exp(scores - peak2), 0.0)
        scale = jnp.exp(peak - peak2)
        total = jnp.sum(weight, axis=1, keepdims=True) + stat[:, 64:65] * scale
        part[...] = (
            jnp.dot(weight.astype(bf), keys[:, :KVL], preferred_element_type=f32)
            + first_out[...] * scale
        ).astype(bf)
        column = lax.broadcasted_iota(jnp.int32, pstat.shape, 1)
        pstat[...] = jnp.where(column < 64, peak2, total)
        for d in (2, 3, 1):
            to = lax.rem(me + d, D)
            at = pl.ds(pl.multiple_of(to * fold, 16), fold)
            for which, src, dst in ((0, pstat, pstats), (1, part, parts)):
                copy = remote(
                    src.at[at], dst.at[d - 1], c_s.at[which, d - 1], c_r.at[which, d - 1],
                    {"dec": to},
                )
                copy.start()
                cc.append(copy)

    def combine():
        for copy in cc:
            copy.wait_recv()
        mine = pl.ds(pl.multiple_of(me * fold, 16), fold)
        shares = [(pstat[mine, :], part[mine, :])]
        shares += [(pstats[d], parts[d]) for d in range(D - 1)]
        own_score = selfs[mine, 0:1]
        top = own_score
        for stats, _ in shares:
            top = jnp.maximum(top, stats[:, 0:1])
        own_weight = jnp.exp(own_score - top)
        numer, denom = own_weight * newk[mine, :], own_weight
        for stats, share in shares:
            factor = jnp.exp(stats[:, 0:1] - top)
            numer = numer + factor * share.astype(f32)
            denom = denom + factor * stats[:, 64:65]
        fin[me] = (numer / denom).astype(bf)
        for d in (2, 3, 1):
            copy = remote(
                fin.at[me], fin.at[me], f_s.at[d - 1], f_r.at[d - 1], {"dec": lax.rem(me + d, D)}
            )
            copy.start()
            ff.append(copy)

    def settle():
        for copy in ff:
            copy.wait_recv()
        for e in range(D):
            a_out[e * fold : (e + 1) * fold, :] = fin[e]

    PIECES = pieces_of(K, NQ, qw // cr)
    due = {}

    def add(tick, action, *args):
        due.setdefault(tick, []).append((action, args))

    def route(tick, p, planes, out=False):
        add(tick, step_compute, p, planes, out)
        add(tick + 1, step_tp, p, planes, out)
        add(tick + 1 + HOPX, step_x, p, planes, out)
        add(tick + 1 + HOPX + HOPY, step_y, p, planes, out)
        if out:
            add(tick + 2 + HOPX + 2 * HOPY, step_back, p)

    blocks = [[p for p in PIECES if p[0] // K == j] for j in range(3)]
    last = 2 * K

    def x_need():
        x_arrived().wait_recv()
        if F:
            for m in (0, D - 1):
                when(me == m, x_out_other(m).start)

    kv_at = KV
    for nth, (early, later) in enumerate(KV_STEPS):
        add(early, kv_project, nth)
        add(later, kv_across, nth)
    for gap, stage in zip(KV_GAPS, (kv_norm, gather, attend, combine)):
        add(kv_at + gap, stage)
    add(1, choose)
    add(3, tables)
    for r in range(requests):
        add(4 + r // 2, old_attend(r))
    add(OWN - 1, x_need)
    for j in range(3):
        for n, p in enumerate(blocks[j]):
            add_tick = OWN + n
            route(add_tick, p, (j,))
    for p in blocks[1]:
        done = p[1] - K - 1
        route(max(done + 2, OWN + 3), p, (2, 3))
        route(OWN + 4 + blocks[1].index(p), p, (0,))
    for p in blocks[0]:
        route(K + p[1] - 1 - AHEAD, p, (1,))
        route(K + p[1] - 1 + kvn, p, (2,))
        route(K + p[1] - 1 + kvn + 2, p, (3,))
    for n, p in enumerate(blocks[2]):
        route(OWN + 5 + n, p, (3,))
        route(K + (3 * K - NQ) + p[1] - 2 * K - 1, p, (0, 1))
    if F:
        def xo_need():
            when(is_in((1, 2)), lambda: x_wait_in())
        add(OUT - 1, xo_need)
        for n, p in enumerate(p for p in PIECES if K <= p[0] < OUT_END):
            there = K + (3 * K - NQ) + p[1] - 2 * K - 1
            route(max(OUT + n // 2, there), p, (1, 2), True)

    def x_wait_in():
        for half in range(2):
            remote(
                xo.at[half], xo.at[half], xz_s.at[0], xz_r.at[half], {"grp": 1 - g}
            ).wait_recv()

    for j in range(D):
        if j in wk_copies:
            when(me == j, wk_copies[j].wait)
    x_mine.wait()
    x_other.wait()
    rope_copy.wait()
    old_copy.wait()
    for j in range(D):
        when(me == j, own_w[j].wait)

    for n in range(max(list(due) + [2 * K]) + 1):
        if n <= 2 * K:
            relay(n)
        for action, args in due.get(n, ()):
            action(*args)

    q = qa[...]
    ss[...] = jnp.broadcast_to(jnp.sum(q * q, axis=0, keepdims=True), ss.shape)
    for i, target in enumerate(({"tp": 1 - t}, {"stg": 1 - s}, {"stg": 1 - s, "tp": 1 - t})):
        copy = remote(ss, ssin.at[i], n_s.at[i], n_r.at[i], target)
        copy.start()
        small.append(copy)
    gain = qg_ref[pl.ds(pl.multiple_of(lane * qw, 128), qw)].reshape(1, qw)
    turned = jnp.transpose(q) * gain
    square = ss[...]
    for i, copy in enumerate(small):
        copy.wait_recv()
        square = square + ssin[i]
    inverse = jnp.transpose(lax.rsqrt(square / QL + norm_eps))
    q_out[...] = (turned * inverse[:, 0:1]).astype(bf)
    settle()

    for copy in [x_swap] + plan_copies + tk + sk + pg + ag + cc + ff + small:
        copy.wait_send()
    for m in range(D):
        def left(m=m):
            for way in (-1, 1):
                for i in sends_of(m, way):
                    z_copy(i, m, way).wait_send()
            for i in range(NQ, D * K):
                if i // K != m:
                    k_copy(i).wait_send()
            if F and m in (0, D - 1):
                x_out_own(m).wait_send()
                x_out_other(m).wait_send()
        when(me == m, left)
    for p in PIECES:
        sl, tl, _ = lane_of(p)
        for out in ((False, True) if F and K <= p[0] < OUT_END else (False,)):
            inside = is_in((1, 2)) if out else is_in(tuple(range(D)))
            when(inside & (t != tl), t_copy(p, out).wait_send)
            when(inside & (t == tl) & (s != sl), h_copy(p, out).wait_send)
            when(inside & (t == tl) & (s == sl), v_copy(p, out).wait_send)
            if out:
                when(inside & (t == tl) & (s == sl), z_back(p, 1).wait_send)


def hand_over_kernel(q_ref, a_ref, q_out, a_out):
    q_out[...] = q_ref[...]
    a_out[...] = a_ref[...]


def capacity(pages, owners):
    return max(2, -(-pages // owners))


def chunk_count(rows):
    return next((k for k in (11, 3, 2) if rows % (16 * k) == 0), 1)


def pieces_of(K, NQ, lane_chunks):
    cuts = set(range(0, NQ + 1, lane_chunks)) | set(range(0, NQ, K)) | {NQ}
    cuts = sorted(cuts | {NQ - c for c in MORE})
    pieces = []
    for a, b in zip(cuts, cuts[1:]):
        parts = -(-(b - a) // LONGEST)
        ends = [a + (b - a) * i // parts for i in range(parts + 1)]
        pieces += list(zip(ends, ends[1:]))
    return pieces


OWN, OUT, HOPX, HOPY = 8, 19, 6, 4
KV, KV_GAPS = 21, (0, 6, 8, 12)
KV_CUTS, KV_STEPS = (384,), ((15, 16), (18, 19))
LONGEST, MORE = 6, ()
LATE = 10
LEAD = 10
AHEAD = 3
FIRST = 4
SHARE = 5


def fused_ok(hidden_x, proj_weight, old_cache, dec_query, page_plan, block_table):
    D, G, S, T = [lax.axis_size(n) for n in ("dec", "grp", "stg", "tp")]
    if (D, G, S, T) != (4, 2, 2, 2):
        return False
    rows, features = hidden_x.shape
    C = proj_weight.shape[1]
    K = chunk_count(C)
    cr, qw, lane_rows = C // K, QL // (S * T), PAGE // (S * T)
    pages = page_plan.shape[0]
    return (
        cr % 16 == 0
        and D * C == QL + KVL + ROPE
        and qw % cr == 0
        and qw % 128 == 0
        and 2 * C < QL < 3 * C
        and features % (128 * 7 * G) == 0
        and rows == pages * PAGE
        and rows % 128 == 0
        and pages % 2 == 0
        and lane_rows % 8 == 0
        and D * capacity(pages, D) <= 16
        and block_table.shape[1] * block_table.shape[2] <= 128
        and block_table.shape[1] == D
        and dec_query.shape[0] == D
        and dec_query.shape[1] % 16 == 0
    )


def fused(
    hidden_x, proj_weight, q_gain, kv_gain, old_cache, page_plan, block_table, split_lens,
    dec_query, new_key,
):
    D, G, S, T = [lax.axis_size(n) for n in ("dec", "grp", "stg", "tp")]
    L = S * T
    rows, features = hidden_x.shape
    C = proj_weight.shape[1]
    K = chunk_count(C)
    fh, qw, kvw = features // G, QL // L, KVL + ROPE
    F = fh * SHARE // 7
    cr, NQ = C // K, QL // (C // K)
    lane_rows = PAGE // L
    pages = page_plan.shape[0]
    cap = capacity(pages, D)
    cap_rows = -(-cap * lane_rows // 16) * 16
    requests, heads = dec_query.shape[0], dec_query.shape[1]
    width = block_table.shape[2]
    fold = requests * heads // D

    positions = np.arange(D * rows, dtype=np.float32)
    pair_index = np.arange(ROPE, dtype=np.int32) // 2
    frequency = np.power(np.float32(10000.0), -(2 * pair_index).astype(np.float32) / np.float32(ROPE))
    angles = positions[:, None] * frequency.astype(np.float32)[None, :]
    rope = np.concatenate([np.cos(angles), np.sin(angles)], axis=1).astype(np.float32)
    rope = jnp.asarray(rope.reshape(D * pages, PAGE, 2 * ROPE))

    dma = pltpu.SemaphoreType.DMA
    bf, f32, i32 = jnp.bfloat16, jnp.float32, jnp.int32
    vmem = pl.BlockSpec(memory_space=pltpu.VMEM)
    smem = pl.BlockSpec(memory_space=pltpu.SMEM)
    hbm = pl.BlockSpec(memory_space=pl.ANY)
    kn = len(KV_STEPS)
    n = len(pieces_of(K, NQ, qw // cr))
    both = G * rows
    outs = (NQ - K) * cr if F else 16
    qo_rows = qw if F else 16
    V = pltpu.VMEM
    q_out, a_out = pl.pallas_call(
        functools.partial(fused_kernel, (D, G, S, T, K, F)),
        out_shape=(
            jax.ShapeDtypeStruct((rows, qw), bf),
            jax.ShapeDtypeStruct((requests * heads, KVL), bf),
        ),
        in_specs=[hbm, hbm, vmem, vmem, hbm, smem, smem, smem, vmem, hbm, vmem, vmem],
        out_specs=(vmem, vmem),
        scratch_shapes=[
            V((D * C, fh), bf), V((kvw, fh), bf), V((G, rows, fh), bf), V((rows, fh), bf),
            V((G, rows, max(F, 128)), bf),
            V((QL, both), f32), V((QL, both), f32), V((qw, both), bf), V((qw, both), bf),
            V((qw, rows), bf), V((qw, rows), bf), V((qw, rows), f32),
            V((outs, both), f32), V((outs, both), f32), V((qo_rows, both), bf), V((qo_rows, both), bf),
            V((qo_rows, rows), bf), V((qo_rows, rows), bf), V((qo_rows, rows), f32),
            V((qo_rows, rows), bf), V((qo_rows, rows), bf),
            V((8, rows), f32), V((L - 1, 8, rows), f32),
            V((pages, PAGE, kvw), f32), V((S, pages, lane_rows, kvw), f32),
            V((pages, lane_rows, kvw), f32), V((pages, lane_rows, kvw), f32),
            V((pages, lane_rows, kvw), f32),
            V((D, cap_rows, kvw), bf), V((L, D, cap_rows, kvw), bf),
            V((8, 128), i32), V((D, 8, 128), i32), pltpu.SMEM((D, 8, 128), i32),
            V((pages, lane_rows, 2 * ROPE), f32), V(old_cache.shape, bf),
            V((8, requests * width * PAGE), f32), V((8, L * D * cap_rows), f32),
            V((requests * heads, 128), f32), V((requests * heads, KVL), f32),
            V((requests * heads, KVL), bf), V((requests * heads, 128), f32),
            V((D - 1, fold, KVL), bf), V((D - 1, fold, 128), f32),
            V((requests * heads, 128), f32), V((requests * heads, KVL), f32),
            V((D, fold, KVL), bf),
            dma((7,)), dma((2, D * K)), dma((D * K,)), dma((D * K - NQ,)), dma((D * K - NQ,)),
            dma((2,)), dma((2,)), dma((2,)),
            dma((n,)), dma((n,)), dma((n,)), dma((n,)), dma((n,)), dma((n,)),
            dma((n,)), dma((n,)), dma((n,)), dma((n,)), dma((n,)), dma((n,)), dma((n,)), dma((n,)),
            dma((kn, S)), dma((kn, S)), dma((kn,)), dma((kn,)), dma((D - 1,)), dma((D - 1,)),
            dma((2, D)), dma((2, D)), dma((2,)), dma((2,)),
            dma((2, D - 1)), dma((2, D - 1)), dma((D - 1,)), dma((D - 1,)), dma((3,)), dma((3,)),
        ],
        compiler_params=pltpu.CompilerParams(
            collective_id=0, has_side_effects=True, vmem_limit_bytes=60 * 1024 * 1024
        ),
    )(
        proj_weight.T, hidden_x, q_gain, kv_gain[None, :], rope, block_table, split_lens.T,
        page_plan.T, page_plan.T, old_cache, dec_query, new_key,
    )
    return pl.pallas_call(
        hand_over_kernel,
        out_shape=(
            jax.ShapeDtypeStruct((rows, qw), bf),
            jax.ShapeDtypeStruct((requests, heads, KVL), bf),
        ),
        in_specs=[vmem, vmem],
        out_specs=(vmem, vmem),
    )(q_out, a_out.reshape(requests, heads, KVL))


def body(
    hidden_x,
    proj_weight,
    q_gain,
    kv_gain,
    old_cache,
    page_plan,
    block_table,
    split_lens,
    dec_query,
    new_key,
):
    if fused_ok(hidden_x, proj_weight, old_cache, dec_query, page_plan, block_table):
        return fused(
            hidden_x, proj_weight, q_gain, kv_gain, old_cache, page_plan, block_table,
            split_lens, dec_query, new_key,
        )
    projected = jnp.dot(
        hidden_x,
        lax.all_gather(proj_weight, "dec", axis=1, tiled=True),
        preferred_element_type=jnp.float32,
    )
    query_part = projected[:, :QL]
    kv_part = projected[:, QL:]
    tokens_here = hidden_x.shape[0]
    positions = (
        lax.axis_index("dec") * tokens_here + jnp.arange(tokens_here, dtype=jnp.int32)
    ).astype(jnp.float32)
    lane_count = lax.axis_size(("stg", "tp"))
    lane_index = lax.axis_index(("stg", "tp"))
    owner_count = lax.axis_size("dec")
    page_count = page_plan.shape[0]
    capacity = max(2, -(-page_count // owner_count))
    query_width = QL // lane_count
    query_cols, kv_cols = (
        lax.psum_scatter(query_part, ("stg", "tp"), scatter_dimension=1, tiled=True),
        lax.psum_scatter(kv_part, ("stg", "tp"), scatter_dimension=1, tiled=True),
    )
    kv_width = kv_cols.shape[1]
    col_start = lane_index * kv_width
    columns = col_start + jnp.arange(kv_width, dtype=jnp.int32)
    latent_part_sq = jnp.sum(jnp.where(columns[None, :] < KVL, kv_cols * kv_cols, 0.0), axis=1)
    query_sq, latent_sq = lax.psum(
        (jnp.sum(query_cols * query_cols, axis=1), latent_part_sq), ("stg", "tp")
    )
    kv_rows = kv_finish(kv_cols, col_start, latent_sq, kv_gain, positions)
    kv_pages = kv_rows.reshape(page_count, PAGE, kv_width)
    send_pages, send_labels = pack_pages(kv_pages, page_plan, owner_count, capacity)
    got_slices, got_labels = (
        lax.all_to_all(send_pages, "dec", split_axis=0, concat_axis=0, tiled=True),
        lax.all_to_all(send_labels, "dec", split_axis=0, concat_axis=0, tiled=True),
    )
    got_pages = lax.all_gather(got_slices, ("stg", "tp"), axis=3, tiled=True)
    query_gain = lax.dynamic_slice_in_dim(q_gain, lane_index * query_width, query_width)
    q_latent = (
        query_cols * lax.rsqrt(query_sq / QL + norm_eps)[:, None] * query_gain[None, :]
    ).astype(jnp.bfloat16)
    cache = place_pages(old_cache, got_pages, got_labels)
    slot_table = block_table[0]
    request_count = slot_table.shape[0]
    key_rows = take_each(cache, slot_table.reshape(-1)).reshape(
        request_count, -1, cache.shape[2]
    )
    scores = (
        jnp.einsum("rhc,rlc->rhl", dec_query, key_rows, preferred_element_type=jnp.float32)
        * softmax_scale
    )
    live_mask = jnp.arange(key_rows.shape[1], dtype=jnp.int32)[None, :] < split_lens[:, 0][:, None]
    scores = jnp.where(live_mask[:, None, :], scores, -1e30)
    row_peak = jnp.max(scores, axis=2)
    weights = jnp.where(live_mask[:, None, :], jnp.exp(scores - row_peak[:, :, None]), 0.0)
    row_total = jnp.sum(weights, axis=2)
    rounded = weights.astype(jnp.bfloat16)
    partial_out = jnp.einsum(
        "rhl,rlc->rhc", rounded, key_rows[:, :, :KVL], preferred_element_type=jnp.float32
    )
    peak_all, total_all, output_all = combined_all(
        (row_peak, row_total, partial_out), "dec", combine_parts
    )
    self_score = (
        jnp.einsum("rhc,rc->rh", dec_query, new_key, preferred_element_type=jnp.float32)
        * softmax_scale
    )
    overall = jnp.maximum(peak_all, self_score)
    carried = jnp.exp(peak_all - overall)
    self_weight = jnp.exp(self_score - overall)
    denom = total_all * carried + self_weight
    numer = output_all * carried[:, :, None] + self_weight[:, :, None] * new_key[
        :, None, :KVL
    ].astype(jnp.float32)
    attn_latent = (numer / denom[:, :, None]).astype(jnp.bfloat16)
    return (q_latent, attn_latent)


def solution(mesh):
    return jax.shard_map(
        body,
        mesh=mesh,
        in_specs=(
            P(("grp", "dec"), ("stg", "tp")),
            P(("stg", "tp"), "dec"),
            P(),
            P(),
            P(("grp", "dec"), None, None),
            P(("grp", "dec"), None),
            P(("grp", "dec"), None, None),
            P("grp", "dec"),
            P("grp", ("stg", "tp"), None),
            P("grp", None),
        ),
        out_specs=(P(("grp", "dec"), ("stg", "tp")), P("grp", ("stg", "tp"), None)),
        check_vma=False,
    )
```
